32 devices in a mesh: row: 8 (over y, x, core), col: 4 (over z).
Axes of the slice: x: 2, y: 2, z: 4, core: 2. Of those that a mesh axis runs over, the one named last changes fastest.
Arguments:
- tokens: bfloat16 [2, 8192, 512], P(None, ('row', 'col')), may hold values from -6 to 6
- encoded: bfloat16 [2, 8192, 512], P(None, ('row', 'col')), may hold values from -6 to 6
- source_len: int32 [2, 8], P(None, 'row'), may hold values from 256 to 1024, as said below
- out_grad: float32 [2, 8192, 512], P(None, ('row', 'col')), may hold values from -6 to 6
- self_query: bfloat16 [512, 512], P('row', 'col'), may hold values from -0.25 to 0.25
- self_key: bfloat16 [512, 512], P('row', 'col'), may hold values from -0.25 to 0.25
- self_value: bfloat16 [512, 512], P('row', 'col'), may hold values from -0.25 to 0.25
- self_output: bfloat16 [512, 512], P('col', 'row'), may hold values from -2 to 2
- self_query_bias: float32 [512], replicated, may hold values from -3 to 3
- self_value_bias: float32 [512], replicated, may hold values from -3 to 3
- self_output_bias: float32 [512], replicated, may hold values from -3 to 3
- cross_query: bfloat16 [512, 512], P('row', 'col'), may hold values from -0.25 to 0.25
- cross_key: bfloat16 [512, 512], P('row', 'col'), may hold values from -0.25 to 0.25
- cross_value: bfloat16 [512, 512], P('row', 'col'), may hold values from -0.25 to 0.25
- cross_output: bfloat16 [512, 512], P('col', 'row'), may hold values from -2 to 2
- cross_query_bias: float32 [512], replicated, may hold values from -3 to 3
- cross_value_bias: float32 [512], replicated, may hold values from -3 to 3
- cross_output_bias: float32 [512], replicated, may hold values from -3 to 3
- expand: bfloat16 [512, 2048], P('row', 'col'), may hold values from -0.25 to 0.25
- expand_bias: float32 [2048], replicated, may hold values from -3 to 3
- contract: bfloat16 [2048, 512], P('col', 'row'), may hold values from -0.125 to 0.125
- contract_bias: float32 [512], replicated, may hold values from -3 to 3
- attn_gain: float32 [512], replicated, may hold values from 0.1 to 1.9
- attn_shift: float32 [512], replicated, may hold values from -3 to 3
- cross_gain: float32 [512], replicated, may hold values from 0.1 to 1.9
- cross_shift: float32 [512], replicated, may hold values from -3 to 3
- final_gain: float32 [512], replicated, may hold values from 0.1 to 1.9
- final_shift: float32 [512], replicated, may hold values from -3 to 3
Outputs:
- result: float32 [2, 8192, 512], P(None, ('row', 'col'))
- tokens_grad: float32 [2, 8192, 512], P(None, ('row', 'col'))
- encoded_grad: float32 [2, 8192, 512], P(None, ('row', 'col'))
- self_query_grad: float32 [512, 512], P('row', 'col')
- self_key_grad: float32 [512, 512], P('row', 'col')
- self_value_grad: float32 [512, 512], P('row', 'col')
- self_output_grad: float32 [512, 512], P('col', 'row')
- self_query_bias_grad: float32 [512], replicated
- self_value_bias_grad: float32 [512], replicated
- self_output_bias_grad: float32 [512], replicated
- cross_query_grad: float32 [512, 512], P('row', 'col')
- cross_key_grad: float32 [512, 512], P('row', 'col')
- cross_value_grad: float32 [512, 512], P('row', 'col')
- cross_output_grad: float32 [512, 512], P('col', 'row')
- cross_query_bias_grad: float32 [512], replicated
- cross_value_bias_grad: float32 [512], replicated
- cross_output_bias_grad: float32 [512], replicated
- expand_grad: float32 [512, 2048], P('row', 'col')
- expand_bias_grad: float32 [2048], replicated
- contract_grad: float32 [2048, 512], P('col', 'row')
- contract_bias_grad: float32 [512], replicated
- attn_gain_grad: float32 [512], replicated
- attn_shift_grad: float32 [512], replicated
- cross_gain_grad: float32 [512], replicated
- cross_shift_grad: float32 [512], replicated
- final_gain_grad: float32 [512], replicated
- final_shift_grad: float32 [512], replicated
The draws below stay inside these ranges and needn't reach their ends.
Inputs may be any that keep to these rules, and one draw needn't show every extreme that they name: `source_len`: every micro-batch has a sequence with all 1024 encoder states and one with 256.
All inputs are finite; a program needn't handle non-finite values.
Results may differ from the reference program's by a relative error of at most 0.022.
The reference program's roundings to bfloat16 on the way count: a program that leaves them out, or rounds other values in their place, can miss the bound.
Values may be sent and summed in bfloat16 or wider, within the bound.
A program may use at most 128 MiB of HBM per device.

```python
import jax
import jax.numpy as jnp
from jax import lax

D = 512
HEAD_DIM = 64
FF = 2048
ENC_LEN = 1024
MICRO = 2
SEQ_DEV = 1
MBT = 8192
MBE = 8192
N_ROW = 8


def draw_source_len(key, part):
    drawn = jax.random.randint(key, (MICRO, SEQ_DEV * N_ROW), ENC_LEN // 4, ENC_LEN + 1)
    drawn = drawn.at[:, 0].set(ENC_LEN)
    drawn = drawn.at[:, 1].set(ENC_LEN // 4)
    return drawn.astype(jnp.int32)


def block_scale(own_key, dims, split, smallest, largest):
    level = 1.0
    for axis_at, blocks in split:
        heights = jax.random.uniform(jax.random.fold_in(jax.random.fold_in(own_key, 6), axis_at), (blocks,), jnp.float32, smallest / len(split), largest / len(split))
        level = level * jnp.repeat(jnp.exp(heights), dims[axis_at] // blocks).reshape((-1,) + (1,) * (len(dims) - 1 - axis_at))
    return level


def normal_values(stream_key, dims, scale, reach, cuts=(), dtype=jnp.bfloat16):
    factor_of = block_scale(stream_key, dims, cuts, -0.22, 0.18) if cuts else 1.0
    values = jax.random.normal(stream_key, dims, jnp.float32) * scale * factor_of
    return jnp.minimum(jnp.maximum(values, -reach), reach).astype(dtype)


def setup_inputs(seed: int = 0) -> dict:
    key_list = jax.random.split(jax.random.key(seed), 29)
    return {
        "tokens": normal_values(key_list[0], (MICRO, MBT, D), 1.0, 6.0, ((1, 32),)),
        "encoded": normal_values(key_list[1], (MICRO, MBE, D), 1.0, 6.0, ((1, 32),)),
        "source_len": draw_source_len(jax.random.fold_in(key_list[28], 71), 0),
        "out_grad": normal_values(key_list[3], (MICRO, MBT, D), 1.0, 6.0, ((1, 32),), jnp.float32),
        "self_query": normal_values(key_list[4], (D, D), D ** -0.5, 0.25, ((0, 8), (1, 4))),
        "self_key": normal_values(key_list[5], (D, D), D ** -0.5, 0.25, ((0, 8), (1, 4))),
        "self_value": normal_values(key_list[6], (D, D), D ** -0.5, 0.25, ((0, 8), (1, 4))),
        "self_output": normal_values(key_list[7], (D, D), 8 ** -0.5, 2.0, ((0, 4), (1, 8))),
        "self_query_bias": normal_values(key_list[8], (D,), 0.5, 3.0, (), jnp.float32),
        "self_value_bias": normal_values(key_list[9], (D,), 0.5, 3.0, (), jnp.float32),
        "self_output_bias": normal_values(key_list[10], (D,), 0.5, 3.0, (), jnp.float32),
        "cross_query": normal_values(key_list[11], (D, D), D ** -0.5, 0.25, ((0, 8), (1, 4))),
        "cross_key": normal_values(key_list[12], (D, D), D ** -0.5, 0.25, ((0, 8), (1, 4))),
        "cross_value": normal_values(key_list[13], (D, D), D ** -0.5, 0.25, ((0, 8), (1, 4))),
        "cross_output": normal_values(key_list[14], (D, D), 8 ** -0.5, 2.0, ((0, 4), (1, 8))),
        "cross_query_bias": normal_values(key_list[15], (D,), 0.5, 3.0, (), jnp.float32),
        "cross_value_bias": normal_values(key_list[16], (D,), 0.5, 3.0, (), jnp.float32),
        "cross_output_bias": normal_values(key_list[17], (D,), 0.5, 3.0, (), jnp.float32),
        "expand": normal_values(key_list[18], (D, FF), D ** -0.5, 0.25, ((0, 8), (1, 4))),
        "expand_bias": normal_values(key_list[19], (FF,), 0.5, 3.0, (), jnp.float32),
        "contract": normal_values(key_list[20], (FF, D), FF ** -0.5, 0.125, ((0, 4), (1, 8))),
        "contract_bias": normal_values(key_list[21], (D,), 0.5, 3.0, (), jnp.float32),
        "attn_gain": jnp.clip(1.0 + 0.18 * jax.random.normal(key_list[22], (D,), jnp.float32), 0.1, 1.9),
        "attn_shift": normal_values(key_list[23], (D,), 0.5, 3.0, (), jnp.float32),
        "cross_gain": jnp.clip(1.0 + 0.18 * jax.random.normal(key_list[24], (D,), jnp.float32), 0.1, 1.9),
        "cross_shift": normal_values(key_list[25], (D,), 0.5, 3.0, (), jnp.float32),
        "final_gain": jnp.clip(1.0 + 0.18 * jax.random.normal(key_list[26], (D,), jnp.float32), 0.1, 1.9),
        "final_shift": normal_values(key_list[27], (D,), 0.5, 3.0, (), jnp.float32),
    }


@jax.custom_vjp
def low(v):
    return lax.optimization_barrier(v.astype(jnp.bfloat16)).astype(jnp.float32)

@jax.custom_vjp
def low_back(v):
    return v

def low_keep(v):
    return (low(v), None)

def low_pass(kept, grad):
    return (grad,)

def back_keep(v):
    return (v, None)

def back_low(kept, grad):
    return (low(grad),)
low.defvjp(low_keep, low_pass)
low_back.defvjp(back_keep, back_low)
NEGATIVE = -1e+30
EPSILON = 1e-05

def matmul(left_side, right_side):
    return jnp.dot(left_side, right_side, precision=lax.Precision.HIGHEST)

def layer_norm(values, norm_gain, norm_shift):
    average = lax.optimization_barrier(jnp.mean(values, axis=-1, keepdims=True))
    centered = values - average
    spread_sq = lax.optimization_barrier(jnp.mean(centered * centered, axis=-1, keepdims=True))
    return centered * lax.rsqrt(spread_sq + EPSILON) * norm_gain + norm_shift

def attention(query_rows, key_rows, value_rows, allowed):
    head_count = query_rows.shape[-1] // HEAD_DIM
    query_heads = query_rows.reshape(query_rows.shape[0], head_count, HEAD_DIM)
    key_heads = key_rows.reshape(key_rows.shape[0], head_count, HEAD_DIM)
    value_heads = value_rows.reshape(value_rows.shape[0], head_count, HEAD_DIM)
    scores = low_back(jnp.einsum('qhd,khd->hqk', query_heads, key_heads, precision=lax.Precision.HIGHEST))
    scores = jnp.where(allowed[None], scores, NEGATIVE)
    attn_probs = jax.nn.softmax(scores, axis=-1)
    mixed_heads = jnp.einsum('hqk,khd->qhd', low(attn_probs), value_heads, precision=lax.Precision.HIGHEST)
    return mixed_heads.reshape(query_rows.shape[0], -1)

def group_forward(params, token_rows, encoder_rows, source_len):
    self_query, self_key, self_value, self_output, self_query_bias, self_value_bias, self_output_bias, cross_query, cross_key, cross_value, cross_output, cross_query_bias, cross_value_bias, cross_output_bias, expand, expand_bias, contract, contract_bias, attn_gain, attn_shift, cross_gain, cross_shift, final_gain, final_shift = params
    query_scale = HEAD_DIM ** (-0.5)
    seq_count = source_len.shape[0]
    length = token_rows.shape[0] // seq_count
    enc_length = encoder_rows.shape[0] // seq_count
    query_rows = low_back(low((matmul(token_rows, self_query) + self_query_bias) * query_scale))
    key_rows = low_back(low(matmul(token_rows, self_key)))
    value_rows = low_back(low(matmul(token_rows, self_value) + self_value_bias))
    positions = jnp.arange(length)
    causal = positions[:, None] >= positions[None, :]

    def self_block(block_item):
        return attention(block_item[0], block_item[1], block_item[2], causal)
    mixed_heads = lax.map(jax.checkpoint(self_block), (query_rows.reshape(seq_count, length, -1), key_rows.reshape(seq_count, length, -1), value_rows.reshape(seq_count, length, -1)))
    mixed_heads = low_back(low(mixed_heads.reshape(token_rows.shape[0], -1)))
    first_out = layer_norm(token_rows + low_back(matmul(mixed_heads, self_output)) + self_output_bias, attn_gain, attn_shift)
    cross_rows = low_back(low((matmul(low(first_out), cross_query) + cross_query_bias) * query_scale))
    cross_keys = low_back(low(matmul(encoder_rows, cross_key)))
    cross_values = low_back(low(matmul(encoder_rows, cross_value) + cross_value_bias))
    enc_positions = jnp.arange(enc_length)

    def cross_block(block_item):
        allowed = jnp.broadcast_to(enc_positions[None, :] < block_item[3], (length, enc_length))
        return attention(block_item[0], block_item[1], block_item[2], allowed)
    cross_mixed = lax.map(jax.checkpoint(cross_block), (cross_rows.reshape(seq_count, length, -1), cross_keys.reshape(seq_count, enc_length, -1), cross_values.reshape(seq_count, enc_length, -1), source_len))
    cross_mixed = low_back(low(cross_mixed.reshape(token_rows.shape[0], -1)))
    second_out = layer_norm(first_out + low_back(matmul(cross_mixed, cross_output)) + cross_output_bias, cross_gain, cross_shift)
    inner_act = low_back(matmul(low(second_out), expand) + expand_bias)
    hidden = low(jax.nn.silu(inner_act))
    return layer_norm(second_out + low_back(matmul(hidden, contract)) + contract_bias, final_gain, final_shift)

def reference(tokens, encoded, source_len, out_grad, self_query, self_key, self_value, self_output, self_query_bias, self_value_bias, self_output_bias, cross_query, cross_key, cross_value, cross_output, cross_query_bias, cross_value_bias, cross_output_bias, expand, expand_bias, contract, contract_bias, attn_gain, attn_shift, cross_gain, cross_shift, final_gain, final_shift):
    params = tuple((weight.astype(jnp.float32) for weight in (self_query, self_key, self_value, self_output, self_query_bias, self_value_bias, self_output_bias, cross_query, cross_key, cross_value, cross_output, cross_query_bias, cross_value_bias, cross_output_bias, expand, expand_bias, contract, contract_bias, attn_gain, attn_shift, cross_gain, cross_shift, final_gain, final_shift)))
    group_count = MICRO * N_ROW
    token_groups = tokens.astype(jnp.float32).reshape(group_count, -1, D)
    encoder_groups = encoded.astype(jnp.float32).reshape(group_count, -1, D)
    length_groups = source_len.reshape(group_count, -1)
    cotangent_groups = out_grad.astype(jnp.float32).reshape(group_count, -1, D)

    def one_group(running, group_item):
        token_rows, encoder_rows, group_len, cotangent = group_item

        def forward(param_set, token_in, encoder_in):
            return group_forward(param_set, token_in, encoder_in, group_len)
        result_rows, pullback = jax.vjp(forward, params, token_rows, encoder_rows)
        param_grads, token_grads, encoder_grads = pullback(cotangent)
        updated = tuple((left_side + right_side for left_side, right_side in zip(running, param_grads)))
        return (updated, (result_rows, token_grads, encoder_grads))
    zeros_init = tuple((jnp.zeros_like(weight) for weight in params))
    summed, (result_rows, token_grads, encoder_grads) = lax.scan(one_group, zeros_init, (token_groups, encoder_groups, length_groups, cotangent_groups))
    return (result_rows.reshape(MICRO, -1, D), token_grads.reshape(MICRO, -1, D), encoder_grads.reshape(MICRO, -1, D), summed[0], summed[1], summed[2], summed[3], summed[4], summed[5], summed[6], summed[7], summed[8], summed[9], summed[10], summed[11], summed[12], summed[13], summed[14], summed[15], summed[16], summed[17], summed[18], summed[19], summed[20], summed[21], summed[22], summed[23])
```

```python
import functools

import jax
import jax.numpy as jnp
from jax import lax
from jax.experimental import pallas as pl
from jax.experimental.pallas import tpu as pltpu
from jax.sharding import PartitionSpec as P

HEAD_DIM = 64
PAIR = 2 * HEAD_DIM
NEGATIVE = -1e30
EPSILON = 1e-05
AXES = ("row", "col")
MESH = pl.DeviceIdType.MESH
F32 = jnp.float32
BF16 = jnp.bfloat16
VMEM_SPEC = pl.BlockSpec(memory_space=pltpu.VMEM)
SMEM_SPEC = pl.BlockSpec(memory_space=pltpu.SMEM)
ANY_SPEC = pl.BlockSpec(memory_space=pl.ANY)
VMEM_LIMIT = 60 * 1024 * 1024


def dot_nn(a, b):
    return lax.dot_general(a, b, (((1,), (0,)), ((), ())), preferred_element_type=F32)


def dot_nt(a, b):
    return lax.dot_general(a, b, (((1,), (1,)), ((), ())), preferred_element_type=F32)


def dot_tn(a, b):
    return lax.dot_general(a, b, (((0,), (0,)), ((), ())), preferred_element_type=F32)


def norm_forward(values):
    average = jnp.mean(values, axis=1, keepdims=True)
    centered = values - average
    inverse = lax.rsqrt(jnp.mean(centered * centered, axis=1, keepdims=True) + EPSILON)
    return centered * inverse, inverse


def norm_backward(gradient, normed, inverse, gain):
    scaled = gradient * gain
    mean_scaled = jnp.mean(scaled, axis=1, keepdims=True)
    mean_product = jnp.mean(scaled * normed, axis=1, keepdims=True)
    return (scaled - mean_scaled - normed * mean_product) * inverse


def column_sum(values):
    return jnp.sum(values, axis=0, keepdims=True)


def spread_lanes(column, width):
    return jnp.broadcast_to(column, (column.shape[0], width))


def call(kernel, outs, in_specs, args, scratch=(), flops=0, out_specs=None, name=None):
    return pl.pallas_call(
        kernel,
        out_shape=outs,
        in_specs=in_specs,
        out_specs=out_specs if out_specs is not None else [VMEM_SPEC] * len(outs),
        scratch_shapes=list(scratch),
        compiler_params=pltpu.CompilerParams(vmem_limit_bytes=VMEM_LIMIT),
        cost_estimate=pl.CostEstimate(flops=flops, bytes_accessed=8 << 20, transcendentals=0),
        name=name,
    )(*args)


def lane_masks():
    lane = lax.broadcasted_iota(jnp.int32, (1, PAIR), 1)
    first = (lane < HEAD_DIM).astype(F32)
    return first, (1.0 - first)


def attend_block(q_ref, kv_ref, out_ref, lse_ref, row0, rows, span, mask):
    first, second = lane_masks()
    halves = (first.astype(BF16), second.astype(BF16))

    def one_pair(z, carry):
        q_pair = q_ref[z, pl.ds(row0, rows), :]
        k_pair = kv_ref[0, z, pl.ds(0, span), :]
        v_pair = kv_ref[1, z, pl.ds(0, span), :]
        outs, stats = [], []
        for half in halves:
            scores = mask(dot_nt(q_pair * half, k_pair))
            row_max = jnp.max(scores, axis=1, keepdims=True)
            raised = jnp.exp(scores - row_max)
            summed = jnp.sum(raised, axis=1, keepdims=True)
            probs = (raised * (1.0 / summed)).astype(BF16)
            outs.append(dot_nn(probs, v_pair))
            stats.append(row_max + jnp.log(summed))
        out_ref[z, pl.ds(row0, rows), :] = (outs[0] * first + outs[1] * second).astype(BF16)
        lse_ref[z, pl.ds(row0, rows), :] = (
            spread_lanes(stats[0], PAIR) * first + spread_lanes(stats[1], PAIR) * second
        )
        return carry

    lax.fori_loop(0, q_ref.shape[0], one_pair, 0)


def attend_block_back(
    q_ref, kv_ref, mixed_ref, lse_ref, grad_ref, dq_ref, dkv_ref, row0, rows, span, chunk, mask
):
    first, second = lane_masks()
    halves = (first.astype(BF16), second.astype(BF16))

    def one_pair(z, carry):
        q_pair = q_ref[z, pl.ds(row0, rows), :]
        g_pair = grad_ref[z, pl.ds(row0, rows), :]
        stats = jnp.transpose(lse_ref[z, pl.ds(row0, rows), :])
        products = jnp.transpose(
            g_pair.astype(F32) * mixed_ref[z, pl.ds(row0, rows), :].astype(F32)
        )
        lse_rows = (stats[0:1, :], stats[HEAD_DIM : HEAD_DIM + 1, :])
        deltas = (column_sum(products[:HEAD_DIM, :]), column_sum(products[HEAD_DIM:, :]))
        q_half = [q_pair * half for half in halves]
        g_half = [g_pair * half for half in halves]
        dq = [jnp.zeros((rows, PAIR), F32), jnp.zeros((rows, PAIR), F32)]
        for at in range(0, span, chunk):
            k_part = kv_ref[0, z, pl.ds(at, chunk), :]
            v_part = kv_ref[1, z, pl.ds(at, chunk), :]
            dk = jnp.zeros((chunk, PAIR), F32)
            dv = jnp.zeros((chunk, PAIR), F32)
            for h in range(2):
                scores = mask(dot_nt(k_part, q_half[h]), at)
                probs = jnp.exp(scores - lse_rows[h])
                prob_grads = dot_nt(v_part, g_half[h])
                score_low = (probs * (prob_grads - deltas[h])).astype(BF16)
                dv = dv + dot_nn(probs.astype(BF16), g_half[h])
                dk = dk + dot_nn(score_low, q_half[h])
                dq[h] = dq[h] + dot_tn(score_low, k_part)
            dkv_ref[0, z, pl.ds(at, chunk), :] += dk
            dkv_ref[1, z, pl.ds(at, chunk), :] += dv
        dq_ref[z, pl.ds(row0, rows), :] = (dq[0] * first + dq[1] * second).astype(
            BF16
        ) * jnp.asarray(HEAD_DIM**-0.5, BF16)
        return carry

    lax.fori_loop(0, q_ref.shape[0], one_pair, 0)


def join_keys(core, own_ref, other_ref, full_ref, part):
    for ref, low, high in ((own_ref, core, 3 - core), (other_ref, 1 - core, 2 + core)):
        low_at = pl.multiple_of(low * part, part)
        high_at = pl.multiple_of(high * part, part)
        for i in range(2):
            full_ref[i, :, pl.ds(low_at, part), :] = ref[i, :, 0:part, :]
            full_ref[i, :, pl.ds(high_at, part), :] = ref[i, :, part : 2 * part, :]


def part_keys(core, full_ref, own_ref, other_ref, part):
    for ref, low, high in ((own_ref, core, 3 - core), (other_ref, 1 - core, 2 + core)):
        low_at = pl.multiple_of(low * part, part)
        high_at = pl.multiple_of(high * part, part)
        for i in range(2):
            ref[i, :, 0:part, :] = full_ref[i, :, pl.ds(low_at, part), :].astype(ref.dtype)
            ref[i, :, part : 2 * part, :] = full_ref[i, :, pl.ds(high_at, part), :].astype(
                ref.dtype
            )


def causal_last(rows, span):
    def mask(scores):
        query = lax.broadcasted_iota(jnp.int32, scores.shape, 0) + (span - rows)
        key = lax.broadcasted_iota(jnp.int32, scores.shape, 1)
        return jnp.where(key <= query, scores, NEGATIVE)

    return mask


def causal_last_back(rows, span):
    def mask(scores, at):
        if at + scores.shape[0] <= span - rows:
            return scores
        key = lax.broadcasted_iota(jnp.int32, scores.shape, 0) + at
        query = lax.broadcasted_iota(jnp.int32, scores.shape, 1) + (span - rows)
        return jnp.where(key <= query, scores, NEGATIVE)

    return mask


def project_kernel(
    x_ref, e_ref, ws_ref, wk_ref, wv_ref, bq_ref, bv_ref, bcv_ref, q_ref, kv_ref, ckv_ref
):
    x = x_ref[...]
    e = e_ref[...]
    scale = HEAD_DIM**-0.5
    for z in range(ws_ref.shape[0]):
        rows = dot_nn(x, ws_ref[z])
        q_ref[z] = ((rows[:, 0:PAIR] + bq_ref[z : z + 1, :]) * scale).astype(BF16)
        kv_ref[0, z] = rows[:, PAIR : 2 * PAIR].astype(BF16)
        kv_ref[1, z] = (rows[:, 2 * PAIR :] + bv_ref[z : z + 1, :]).astype(BF16)
    for z in range(ws_ref.shape[0]):
        ckv_ref[0, z] = dot_nn(e, wk_ref[z]).astype(BF16)
        ckv_ref[1, z] = (dot_nn(e, wv_ref[z]) + bcv_ref[z : z + 1, :]).astype(BF16)


def forward_kernel(
    info_ref,
    q_ref,
    kv_ref,
    okv_ref,
    ckv_ref,
    ockv_ref,
    x_ref,
    wo_ref,
    wcq_ref,
    wco_ref,
    bcq_ref,
    vec_ref,
    mixed_ref,
    lse_ref,
    n1_ref,
    i1_ref,
    cq_ref,
    cmixed_ref,
    clse_ref,
    n2_ref,
    i2_ref,
    full_ref,
):
    core = info_ref[0]
    limit = info_ref[1]
    heads = q_ref.shape[0]
    rows = q_ref.shape[1] // 2
    span = 4 * rows
    out_bias, gain1, shift1, cout_bias = (vec_ref[i : i + 1, :] for i in range(4))
    join_keys(core, kv_ref, okv_ref, full_ref, rows)
    for parity in range(2):

        @pl.when(core == parity)
        def _():
            low = (parity + 1) * rows
            high = (4 - parity) * rows
            attend_block(
                q_ref, full_ref, mixed_ref, lse_ref, 0, rows, low, causal_last(rows, low)
            )
            attend_block(
                q_ref, full_ref, mixed_ref, lse_ref, rows, rows, high, causal_last(rows, high)
            )

    branch = out_bias + x_ref[...].astype(F32)
    for z in range(heads):
        branch = branch + dot_nt(mixed_ref[z], wo_ref[z])
    normed, inverse = norm_forward(branch)
    n1_ref[...] = normed
    i1_ref[...] = spread_lanes(inverse, PAIR)
    first_low = (normed * gain1 + shift1).astype(BF16)
    for z in range(heads):
        cq_ref[z] = (
            (dot_nn(first_low, wcq_ref[z]) + bcq_ref[z : z + 1, :]) * HEAD_DIM**-0.5
        ).astype(BF16)
    join_keys(core, ckv_ref, ockv_ref, full_ref, rows)

    def mask(scores):
        key = lax.broadcasted_iota(jnp.int32, scores.shape, 1)
        return jnp.where(key < limit, scores, NEGATIVE)

    for row0 in (0, rows):
        attend_block(cq_ref, full_ref, cmixed_ref, clse_ref, row0, rows, span, mask)
    branch = n1_ref[...] * gain1 + shift1 + cout_bias
    for z in range(heads):
        branch = branch + dot_nt(cmixed_ref[z], wco_ref[z])
    normed, inverse = norm_forward(branch)
    n2_ref[...] = normed
    i2_ref[...] = spread_lanes(inverse, PAIR)


def hidden_kernel(
    n2_ref,
    i2_ref,
    og_ref,
    we_ref,
    wc_ref,
    be_ref,
    vec_ref,
    result_ref,
    grad_ref,
    ge_ref,
    gc_ref,
    bias_ref,
    small_ref,
    inner_ref,
    hidden_ref,
    low_ref,
    total_ref,
):
    groups = we_ref.shape[0]
    gain2, shift2, out_bias, gain3, shift3 = (vec_ref[i : i + 1, :] for i in range(5))
    second = n2_ref[...] * gain2 + shift2
    low_ref[...] = second.astype(BF16)
    total_ref[...] = second + out_bias

    def forward(z, carry):
        inner = dot_nn(low_ref[...], we_ref[z]) + be_ref[pl.ds(z, 1), :]
        inner_ref[z] = inner
        hidden = (inner * jax.nn.sigmoid(inner)).astype(BF16)
        hidden_ref[z] = hidden
        total_ref[...] += dot_nt(hidden, wc_ref[z])
        return carry

    lax.fori_loop(0, groups, forward, 0)
    normed, inverse = norm_forward(total_ref[...])
    result_ref[...] = (normed * gain3 + shift3).astype(result_ref.dtype)
    gradient = og_ref[...].astype(F32)
    small_ref[0:1, :] = column_sum(gradient * normed)
    small_ref[1:2, :] = column_sum(gradient)
    third = norm_backward(gradient, normed, inverse, gain3)
    small_ref[2:3, :] = column_sum(third)
    third_low = third.astype(BF16)
    total_ref[...] = third

    def backward(z, carry):
        inner = inner_ref[z]
        hidden_back = dot_nn(third_low, wc_ref[z])
        gc_ref[z] = dot_tn(third_low, hidden_ref[z]).astype(BF16)
        logistic = jax.nn.sigmoid(inner)
        inner_back = (hidden_back * logistic * (1.0 + inner * (1.0 - logistic))).astype(BF16)
        bias_ref[pl.ds(z, 1), :] = column_sum(inner_back.astype(F32))
        ge_ref[z] = dot_tn(low_ref[...], inner_back).astype(BF16)
        total_ref[...] += dot_nt(inner_back, we_ref[z])
        return carry

    lax.fori_loop(0, groups, backward, 0)
    gradient = total_ref[...]
    normed = n2_ref[...]
    small_ref[3:4, :] = column_sum(gradient * normed)
    small_ref[4:5, :] = column_sum(gradient)
    second_grad = norm_backward(gradient, normed, i2_ref[:, 0:1], gain2)
    small_ref[5:6, :] = column_sum(second_grad)
    small_ref[6:8, :] = jnp.zeros((2, small_ref.shape[1]), F32)
    grad_ref[...] = second_grad


def cross_back_kernel(
    info_ref,
    grad_ref,
    cmixed_ref,
    clse_ref,
    cq_ref,
    ckv_ref,
    ockv_ref,
    wco_ref,
    wcq_ref,
    n1_ref,
    i1_ref,
    vec_ref,
    gco_ref,
    gcq_ref,
    own_ref,
    other_ref,
    first_grad_ref,
    small_ref,
    bias_ref,
    full_ref,
    dkv_ref,
    mixed_back_ref,
    dq_ref,
):
    core = info_ref[0]
    limit = info_ref[1]
    heads = cq_ref.shape[0]
    rows = cq_ref.shape[1] // 2
    span = 4 * rows
    gain1, shift1 = (vec_ref[i : i + 1, :] for i in range(2))
    join_keys(core, ckv_ref, ockv_ref, full_ref, rows)
    grad_low = grad_ref[...].astype(BF16)
    for z in range(heads):
        gco_ref[z] = dot_tn(grad_low, cmixed_ref[z]).astype(BF16)
        mixed_back_ref[z] = dot_nn(grad_low, wco_ref[z]).astype(BF16)
    dkv_ref[...] = jnp.zeros_like(dkv_ref)

    def mask(scores, at):
        key = lax.broadcasted_iota(jnp.int32, scores.shape, 0) + at
        return jnp.where(key < limit, scores, NEGATIVE)

    for row0 in (0, rows):
        attend_block_back(
            cq_ref,
            full_ref,
            cmixed_ref,
            clse_ref,
            mixed_back_ref,
            dq_ref,
            dkv_ref,
            row0,
            rows,
            span,
            2 * rows,
            mask,
        )
    part_keys(core, dkv_ref, own_ref, other_ref, rows)
    normed = n1_ref[...]
    first_low = (normed * gain1 + shift1).astype(BF16)
    gradient = grad_ref[...]
    for z in range(heads):
        dq = dq_ref[z]
        gcq_ref[z] = dot_tn(first_low, dq).astype(BF16)
        bias_ref[z : z + 1, :] = column_sum(dq.astype(F32))
        gradient = gradient + dot_nt(dq, wcq_ref[z])
    small_ref[0:1, :] = column_sum(gradient * normed)
    small_ref[1:2, :] = column_sum(gradient)
    first_grad = norm_backward(gradient, normed, i1_ref[:, 0:1], gain1)
    small_ref[2:3, :] = column_sum(first_grad)
    small_ref[3:8, :] = jnp.zeros((5, small_ref.shape[1]), F32)
    first_grad_ref[...] = first_grad


def self_back_kernel(
    info_ref,
    grad_ref,
    mixed_ref,
    lse_ref,
    q_ref,
    kv_ref,
    okv_ref,
    wo_ref,
    go_ref,
    dq_ref,
    own_ref,
    other_ref,
    full_ref,
    dkv_ref,
    mixed_back_ref,
):
    core = info_ref[0]
    heads = q_ref.shape[0]
    rows = q_ref.shape[1] // 2
    join_keys(core, kv_ref, okv_ref, full_ref, rows)
    grad_low = grad_ref[...].astype(BF16)
    for z in range(heads):
        go_ref[z] = dot_tn(grad_low, mixed_ref[z]).astype(BF16)
        mixed_back_ref[z] = dot_nn(grad_low, wo_ref[z]).astype(BF16)
    dkv_ref[...] = jnp.zeros_like(dkv_ref)
    for parity in range(2):

        @pl.when(core == parity)
        def _():
            for row0, span in ((0, (parity + 1) * rows), (rows, (4 - parity) * rows)):
                attend_block_back(
                    q_ref,
                    full_ref,
                    mixed_ref,
                    lse_ref,
                    mixed_back_ref,
                    dq_ref,
                    dkv_ref,
                    row0,
                    rows,
                    span,
                    rows,
                    causal_last_back(rows, span),
                )

    part_keys(core, dkv_ref, own_ref, other_ref, rows)


def encoder_back_kernel(
    e_ref, own_ref, arrived_ref, wk_ref, wv_ref, gkv_ref, out_ref, bias_ref, total_ref
):
    e = e_ref[...]
    for z in range(wk_ref.shape[0]):
        dk = (own_ref[0, z] + arrived_ref[0, z].astype(F32)).astype(BF16)
        dv = (own_ref[1, z] + arrived_ref[1, z].astype(F32)).astype(BF16)
        bias_ref[z : z + 1, :] = column_sum(dv.astype(F32))
        gkv_ref[z] = dot_tn(e, jnp.concatenate([dk, dv], axis=1)).astype(BF16)
        term = dot_nt(dk, wk_ref[z]) + dot_nt(dv, wv_ref[z])
        if z == 0:
            total_ref[...] = term
        else:
            total_ref[...] += term
    out_ref[...] = total_ref[...].astype(out_ref.dtype)


def tokens_back_kernel(
    x_ref, dq_ref, own_ref, arrived_ref, first_grad_ref, ws_ref, gs_ref, out_ref, bias_ref, total_ref
):
    x = x_ref[...]
    heads = ws_ref.shape[0]
    total_ref[...] = first_grad_ref[...]
    for z in range(heads):
        dq = dq_ref[z]
        dk = (own_ref[0, z] + arrived_ref[0, z].astype(F32)).astype(BF16)
        dv = (own_ref[1, z] + arrived_ref[1, z].astype(F32)).astype(BF16)
        bias_ref[z : z + 1, :] = column_sum(dq.astype(F32))
        bias_ref[heads + z : heads + z + 1, :] = column_sum(dv.astype(F32))
        joined = jnp.concatenate([dq, dk, dv], axis=1)
        gs_ref[z] = dot_tn(x, joined).astype(BF16)
        total_ref[...] += dot_nt(joined, ws_ref[z])
    out_ref[...] = total_ref[...].astype(out_ref.dtype)


def flipped(index, bits):
    for bit in bits:
        index = index + bit - 2 * bit * ((index // bit) % 2)
    return index


def bits_of(number):
    return [1 << i for i in range(number.bit_length()) if (number >> i) & 1]


def subsets(bits):
    out = [0]
    for bit in bits:
        out = out + [m + bit for m in out]
    return out


class Links:
    def __init__(self, send, recv):
        self.send, self.recv, self.count = send, recv, 0

    def start(self, src, dst, device):
        at = self.count
        self.count += 1
        copy = pltpu.make_async_remote_copy(
            src_ref=src,
            dst_ref=dst,
            send_sem=self.send.at[at],
            recv_sem=self.recv.at[at],
            device_id=device,
            device_id_type=MESH,
        )
        copy.start()
        return copy


def greet(row, col, row_bits, col_count):
    barrier = pltpu.get_barrier_semaphore()
    for bit in row_bits:
        pl.semaphore_signal(
            barrier, inc=1, device_id=(flipped(row, [bit]), col), device_id_type=MESH
        )
    for k in range(1, col_count):
        pl.semaphore_signal(
            barrier, inc=1, device_id=(row, flipped(col, bits_of(k))), device_id_type=MESH
        )
    pl.semaphore_wait(barrier, len(row_bits) + col_count - 1)


def gather_copies(row_count, col_count):
    plane = row_count // 2
    return (col_count - 1) + 2 * (plane - 1) + plane * 2


def gather_kernel(row_count, col_count, group_count, *refs):
    shards = refs[:group_count]
    wholes = refs[group_count : 2 * group_count]
    send, recv, local = refs[2 * group_count :]
    row, col = lax.axis_index("row"), lax.axis_index("col")
    row_bits = bits_of(row_count - 1)
    plane_bits = row_bits[1:]
    half = col_count // 2
    greet(row, col, row_bits, col_count)
    links = Links(send, recv)
    keep, z_copies = [], []
    for g in range(group_count):
        copy = pltpu.make_async_copy(shards[g], wholes[g].at[col, row], local.at[g])
        copy.start()
        keep.append(copy)
        z_copies.append(
            [
                links.start(
                    shards[g], wholes[g].at[col, row], (row, flipped(col, bits_of(k)))
                )
                for k in range(1, col_count)
            ]
        )
    sides = ((0, plane_bits), (half, plane_bits[::-1]))
    plane_copies = [dict() for _ in range(group_count)]
    core_copies = [[] for _ in range(group_count)]

    def block(g, side, m):
        return wholes[g].at[pl.ds(side, half), flipped(row, bits_of(m))]

    def send_out(g, side, order, m):
        reached = max([order.index(b) for b in bits_of(m)], default=-1)
        for bit in order[reached + 1 :]:
            plane_copies[g][(side, m + bit)] = links.start(
                block(g, side, m), block(g, side, m), (flipped(row, [bit]), col)
            )
        core_copies[g].append(
            links.start(block(g, side, m), block(g, side, m), (flipped(row, [1]), col))
        )

    for g in range(group_count):
        keep[g].wait()
        for copy in z_copies[g]:
            copy.wait_recv()
        for side, order in sides:
            send_out(g, side, order, 0)
    for level in range(1, len(plane_bits) + 1):
        for g in range(group_count):
            for side, order in sides:
                for m in subsets(plane_bits):
                    if len(bits_of(m)) == level:
                        plane_copies[g][(side, m)].wait_recv()
                        send_out(g, side, order, m)
    for g in range(group_count):
        for copy in core_copies[g]:
            copy.wait_recv()
    for g in range(group_count):
        for copy in z_copies[g] + list(plane_copies[g].values()) + core_copies[g]:
            copy.wait_send()


def gather_weights(shards, row_count, col_count):
    groups = len(shards)
    count = groups * gather_copies(row_count, col_count)
    outs = [
        jax.ShapeDtypeStruct((col_count, row_count) + s.shape, s.dtype) for s in shards
    ]
    wholes = pl.pallas_call(
        functools.partial(gather_kernel, row_count, col_count, groups),
        out_shape=outs,
        in_specs=[VMEM_SPEC] * groups,
        out_specs=[ANY_SPEC] * groups,
        scratch_shapes=[
            pltpu.SemaphoreType.DMA((count,)),
            pltpu.SemaphoreType.DMA((count,)),
            pltpu.SemaphoreType.DMA((groups,)),
        ],
        compiler_params=pltpu.CompilerParams(collective_id=0, has_side_effects=True),
        cost_estimate=pl.CostEstimate(flops=0, bytes_accessed=100 << 20, transcendentals=0),
        name="gather_weights",
    )(*shards)
    return [w.reshape(col_count, -1, w.shape[-1]) for w in wholes]


def add_blocks(target, source, pieces):
    for into, other in pieces:
        target[into] = (target[into].astype(F32) + source[other].astype(F32)).astype(BF16)


def reduce_kernel(row_count, col_count, group_count, *refs):
    grads = refs[:group_count]
    small_in = refs[group_count]
    outs = refs[group_count + 1 : 2 * group_count + 1]
    small_out = refs[2 * group_count + 1]
    scratch = refs[2 * group_count + 2 :]
    sums = scratch[:group_count]
    from_core = scratch[group_count : 2 * group_count]
    from_plane = scratch[2 * group_count : 3 * group_count]
    from_col = scratch[3 * group_count : 4 * group_count]
    small_sum, small_from, send, recv = scratch[4 * group_count :]
    row, col = lax.axis_index("row"), lax.axis_index("col")
    row_bits = bits_of(row_count - 1)
    plane_bits = row_bits[1:]
    half = col_count // 2
    greet(row, col, row_bits, col_count)
    links = Links(send, recv)
    everything = []
    members = subsets(plane_bits)
    core_copies = []
    for g in range(group_count):
        batch = []
        for at, m in enumerate(members):
            batch.append(
                links.start(
                    grads[g].at[:, flipped(row, [1] + bits_of(m))],
                    from_core[g].at[at],
                    (flipped(row, [1]), col),
                )
            )
        core_copies.append(batch)
        everything += batch
    small_steps = [(b, 0) for b in row_bits] + [(b, 1) for b in bits_of(col_count - 1)]

    def small_start(at):
        bit, axis = small_steps[at]
        device = (flipped(row, [bit]), col) if axis == 0 else (row, flipped(col, [bit]))
        return links.start(small_sum.at[at % 2], small_from.at[at], device)

    sides = ((0, plane_bits), (half, plane_bits[::-1]))
    width = [1 << i for i in range(len(plane_bits))]
    small_sum[0] = small_in[...]
    small_copy = small_start(0)
    pending = [[None, None] for _ in range(group_count)]

    def small_next(at, copy):
        copy.wait()
        small_sum[(at + 1) % 2] = small_sum[at % 2] + small_from[at]
        return small_start(at + 1) if at + 1 < len(small_steps) else None

    def plane_slots(side_at, level):
        order = sides[side_at][1]
        bit = order[level]
        later = order[level + 1 :]
        return bit, [m for m in subsets(later)]

    def plane_send(g, side_at, level):
        bit, slots = plane_slots(side_at, level)
        side = sides[side_at][0]
        batch = []
        for m in slots:
            batch.append(
                (
                    m,
                    links.start(
                        sums[g].at[members.index(m + bit), pl.ds(side, half)],
                        from_plane[g].at[plane_base[side_at][level] + slots.index(m)],
                        (flipped(row, [bit]), col),
                    ),
                )
            )
        pending[g][side_at] = batch
        everything.extend([c for _, c in batch])

    plane_base = []
    at = 0
    for side_at in range(2):
        bases = []
        for level in range(len(plane_bits)):
            bases.append(at)
            at += len(plane_slots(side_at, level)[1])
        plane_base.append(bases)

    def add_half(g, side_at, m, slot):
        side = sides[side_at][0]
        into = members.index(m)

        def body(i, carry):
            sums[g][into, side + i] = (
                sums[g][into, side + i].astype(F32) + from_plane[g][slot, i].astype(F32)
            ).astype(BF16)
            return carry

        lax.fori_loop(0, half, body, 0)

    small_at = 0
    for g in range(group_count):
        for at, m in enumerate(members):
            core_copies[g][at].wait_recv()
            own_row = flipped(row, bits_of(m))

            def body(i, carry, g=g, at=at, own_row=own_row):
                sums[g][at, i] = (
                    grads[g][i, own_row].astype(F32) + from_core[g][at, i].astype(F32)
                ).astype(BF16)
                return carry

            lax.fori_loop(0, col_count, body, 0)
        for side_at in range(2):
            plane_send(g, side_at, 0)
        if small_copy is not None:
            small_copy = small_next(small_at, small_copy)
            small_at += 1
    for level in range(len(plane_bits)):
        for g in range(group_count):
            for side_at in range(2):
                batch = pending[g][side_at]
                slots = plane_slots(side_at, level)[1]
                for m, copy in batch:
                    copy.wait_recv()
                    add_half(g, side_at, m, plane_base[side_at][level] + slots.index(m))
                if level + 1 < len(plane_bits):
                    plane_send(g, side_at, level + 1)
            if level + 1 == len(plane_bits):
                batch = []
                for k in range(1, col_count):
                    far = flipped(col, bits_of(k))
                    batch.append(
                        links.start(sums[g].at[0, far], from_col[g].at[k - 1], (row, far))
                    )
                pending[g] = batch
                everything.extend(batch)
        if small_copy is not None:
            small_copy = small_next(small_at, small_copy)
            small_at += 1
    while small_copy is not None:
        small_copy = small_next(small_at, small_copy)
        small_at += 1
    small_out[...] = small_sum[small_at % 2]
    for g in range(group_count):
        total = sums[g][0, col].astype(F32)
        for k in range(1, col_count):
            pending[g][k - 1].wait_recv()
            total = total + from_col[g][k - 1].astype(F32)
        outs[g][...] = total
    for copy in everything:
        copy.wait_send()


def reduce_grads(grads, small, row_count, col_count):
    groups = len(grads)
    plane = row_count // 2
    grads = [g.reshape(col_count, row_count, -1, g.shape[-1]) for g in grads]
    blocks = [g.shape[2:] for g in grads]
    half = col_count // 2
    levels = bits_of(row_count - 1)[1:]
    plane_slots = 2 * (plane - 1)
    small_steps = len(levels) + 1 + len(bits_of(col_count - 1))
    count = groups * (plane + plane_slots + col_count - 1) + small_steps
    outs = [jax.ShapeDtypeStruct(b, F32) for b in blocks]
    outs.append(jax.ShapeDtypeStruct(small.shape, F32))
    scratch = [pltpu.VMEM((plane, col_count) + b, BF16) for b in blocks]
    scratch += [pltpu.VMEM((plane, col_count) + b, BF16) for b in blocks]
    scratch += [pltpu.VMEM((plane_slots, half) + b, BF16) for b in blocks]
    scratch += [pltpu.VMEM((col_count - 1,) + b, BF16) for b in blocks]
    scratch += [
        pltpu.VMEM((2,) + small.shape, F32),
        pltpu.VMEM((small_steps,) + small.shape, F32),
        pltpu.SemaphoreType.DMA((count,)),
        pltpu.SemaphoreType.DMA((count,)),
    ]
    return pl.pallas_call(
        functools.partial(reduce_kernel, row_count, col_count, groups),
        out_shape=outs,
        in_specs=[VMEM_SPEC] * (groups + 1),
        out_specs=[VMEM_SPEC] * (groups + 1),
        scratch_shapes=scratch,
        compiler_params=pltpu.CompilerParams(
            collective_id=1, has_side_effects=True, vmem_limit_bytes=VMEM_LIMIT
        ),
        cost_estimate=pl.CostEstimate(flops=0, bytes_accessed=100 << 20, transcendentals=0),
        name="reduce_grads",
    )(*grads, small)


def routes(row_count, col_count):
    even = (0, 1, 1, 0)
    near, far = [], []
    for r in range(row_count):
        for c in range(col_count):
            to_row = (r // 2) * 2 + even[c]
            micro = c // 2
            near.append((r * col_count + c, to_row * col_count + 2 * micro + r % 2))
            far.append((r * col_count + c, to_row * col_count + 2 * (1 - micro) + r % 2))
    swap = [
        (r * col_count + c, (r ^ 1) * col_count + c)
        for r in range(row_count)
        for c in range(col_count)
    ]
    return near, far, swap


def per_device(
    tokens,
    encoded,
    source_len,
    out_grad,
    self_query,
    self_key,
    self_value,
    self_output,
    self_query_bias,
    self_value_bias,
    self_output_bias,
    cross_query,
    cross_key,
    cross_value,
    cross_output,
    cross_query_bias,
    cross_value_bias,
    cross_output_bias,
    expand,
    expand_bias,
    contract,
    contract_bias,
    attn_gain,
    attn_shift,
    cross_gain,
    cross_shift,
    final_gain,
    final_shift,
):
    row_count = lax.axis_size("row")
    cols = lax.axis_size("col")
    row, col = lax.axis_index("row"), lax.axis_index("col")
    micro_count, part, width = tokens.shape
    head_width = self_query.shape[1]
    hid = expand.shape[1]
    assert micro_count == 2 and cols == 4 and source_len.shape[1] == 1
    assert head_width == PAIR and row_count % 2 == 0
    near, far, swap = routes(row_count, cols)
    back = lambda pairs: [(b, a) for a, b in pairs]
    core = row % 2
    low_col = col < 2
    own_rows = 2 * part

    def collect(array):
        array = array.astype(BF16)
        a = lax.ppermute(jnp.where(low_col, array[0], array[1]), AXES, near)
        b = lax.ppermute(jnp.where(low_col, array[1], array[0]), AXES, far)
        return jnp.concatenate([jnp.where(low_col, a, b), jnp.where(low_col, b, a)], axis=0)

    def give_back(array):
        low, high = array[:part], array[part:]
        a = lax.ppermute(jnp.where(low_col, low, high), AXES, back(near))
        b = lax.ppermute(jnp.where(low_col, high, low), AXES, back(far))
        return jnp.stack([jnp.where(low_col, a, b), jnp.where(low_col, b, a)]).astype(F32)

    def trade(array):
        return lax.ppermute(array, AXES, swap)

    x = collect(tokens)
    shards = (
        jnp.concatenate([self_query, self_key, self_value], axis=1),
        jnp.concatenate(
            [self_output.T, cross_query, cross_key, cross_value, cross_output.T], axis=1
        ),
        jnp.concatenate([expand, contract.T], axis=1),
    )
    w_self, w_attn, w_hidden = gather_weights(shards, row_count, cols)
    e = collect(encoded)
    lengths = jnp.where(core == col % 2, source_len, trade(source_len))
    limit = jnp.where(low_col, lengths[0, 0], lengths[1, 0])
    info = jnp.stack([core, limit]).astype(jnp.int32)

    def cut(index):
        return pl.BlockSpec((cols, width, PAIR), lambda i: (0, 0, index))

    def wide(index):
        return pl.BlockSpec((cols, width, hid), lambda i: (0, 0, index))

    def by_head(vector):
        return vector.reshape(cols, PAIR)

    def stacked(*vectors):
        gap = -len(vectors) % 8
        return jnp.concatenate(
            [jnp.stack(vectors), jnp.zeros((gap, width), F32)], axis=0
        )

    heads_low = jax.ShapeDtypeStruct((cols, own_rows, PAIR), BF16)
    heads_f32 = jax.ShapeDtypeStruct((cols, own_rows, PAIR), F32)
    pairs_low = jax.ShapeDtypeStruct((2, cols, own_rows, PAIR), BF16)
    pairs_f32 = jax.ShapeDtypeStruct((2, cols, own_rows, PAIR), F32)
    rows_f32 = jax.ShapeDtypeStruct((own_rows, width), F32)
    rows_low = jax.ShapeDtypeStruct((own_rows, width), BF16)
    stat_f32 = jax.ShapeDtypeStruct((own_rows, PAIR), F32)
    small_f32 = jax.ShapeDtypeStruct((8, width), F32)
    head_bias = jax.ShapeDtypeStruct((cols, PAIR), F32)
    grad_head = jax.ShapeDtypeStruct((cols, width, PAIR), BF16)
    grad_wide = jax.ShapeDtypeStruct((cols, width, hid), BF16)
    full_keys = pltpu.VMEM((2, cols, 4 * part, PAIR), BF16)
    full_grads = pltpu.VMEM((2, cols, 4 * part, PAIR), F32)
    head_scratch = pltpu.VMEM((cols, own_rows, PAIR), BF16)
    square = 2 * own_rows * width * width

    def columns(array, index):
        return lax.slice_in_dim(array, index * PAIR, (index + 1) * PAIR, axis=2)

    w_out, w_cq, w_ck, w_cv, w_co = (columns(w_attn, i) for i in range(5))
    w_exp = w_hidden[:, :, :hid]
    w_con = w_hidden[:, :, hid:]

    q, kv, ckv = call(
        project_kernel,
        [heads_low, pairs_low, pairs_low],
        [VMEM_SPEC] * 8,
        (
            x,
            e,
            w_self,
            w_ck,
            w_cv,
            by_head(self_query_bias),
            by_head(self_value_bias),
            by_head(cross_value_bias),
        ),
        flops=5 * square,
        name="project",
    )
    okv = trade(kv)
    ockv = trade(ckv)
    mixed, lse, n1, i1, cq, cmixed, clse, n2, i2 = call(
        forward_kernel,
        [
            heads_low,
            heads_f32,
            rows_f32,
            stat_f32,
            heads_low,
            heads_low,
            heads_f32,
            rows_f32,
            stat_f32,
        ],
        [SMEM_SPEC] + [VMEM_SPEC] * 11,
        (
            info,
            q,
            kv,
            okv,
            ckv,
            ockv,
            x,
            w_out,
            w_cq,
            w_co,
            by_head(cross_query_bias),
            stacked(self_output_bias, attn_gain, attn_shift, cross_output_bias),
        ),
        scratch=[full_keys],
        flops=30 * square,
        name="forward",
    )
    og = collect(out_grad)
    result, second_grad, g_exp, g_con, exp_bias, small_a = call(
        hidden_kernel,
        [
            rows_low,
            rows_f32,
            grad_wide,
            grad_wide,
            jax.ShapeDtypeStruct((cols, hid), F32),
            small_f32,
        ],
        [VMEM_SPEC] * 7,
        (
            n2,
            i2,
            og,
            w_exp,
            w_con,
            expand_bias.reshape(cols, hid),
            stacked(cross_gain, cross_shift, contract_bias, final_gain, final_shift),
        ),
        scratch=[
            pltpu.VMEM((cols, own_rows, hid), F32),
            pltpu.VMEM((cols, own_rows, hid), BF16),
            pltpu.VMEM((own_rows, width), BF16),
            pltpu.VMEM((own_rows, width), F32),
        ],
        flops=24 * square,
        name="hidden",
    )
    result_home = give_back(result)
    g_co, g_cq, dckv_own, dckv_other, first_grad, small_b, cq_bias = call(
        cross_back_kernel,
        [grad_head, grad_head, pairs_f32, pairs_low, rows_f32, small_f32, head_bias],
        [SMEM_SPEC] + [VMEM_SPEC] * 11,
        (
            info,
            second_grad,
            cmixed,
            clse,
            cq,
            ckv,
            ockv,
            w_co,
            w_cq,
            n1,
            i1,
            stacked(attn_gain, attn_shift),
        ),
        scratch=[full_keys, full_grads, head_scratch, head_scratch],
        flops=30 * square,
        name="cross_back",
    )
    dckv_arrived = trade(dckv_other)
    g_o, dq, dkv_own, dkv_other = call(
        self_back_kernel,
        [grad_head, heads_low, pairs_f32, pairs_low],
        [SMEM_SPEC] + [VMEM_SPEC] * 7,
        (info, first_grad, mixed, lse, q, kv, okv, w_out),
        scratch=[full_keys, full_grads, head_scratch],
        flops=20 * square,
        name="self_back",
    )
    dkv_arrived = trade(dkv_other)
    g_ckv, encoded_back, cv_bias = call(
        encoder_back_kernel,
        [
            jax.ShapeDtypeStruct((cols, width, 2 * PAIR), BF16),
            rows_low,
            head_bias,
        ],
        [VMEM_SPEC] * 5,
        (e, dckv_own, dckv_arrived, w_ck, w_cv),
        scratch=[pltpu.VMEM((own_rows, width), F32)],
        flops=4 * square,
        name="encoder_back",
    )
    encoded_home = give_back(encoded_back)
    g_self, tokens_back, qv_bias = call(
        tokens_back_kernel,
        [
            jax.ShapeDtypeStruct((cols, width, 3 * PAIR), BF16),
            rows_low,
            jax.ShapeDtypeStruct((2 * cols, PAIR), F32),
        ],
        [VMEM_SPEC] * 6,
        (x, dq, dkv_own, dkv_arrived, first_grad, w_self),
        scratch=[pltpu.VMEM((own_rows, width), F32)],
        flops=6 * square,
        name="tokens_back",
    )
    tokens_home = give_back(tokens_back)

    small = jnp.concatenate(
        [
            small_a,
            small_b,
            qv_bias.reshape(2, width),
            cq_bias.reshape(1, width),
            cv_bias.reshape(1, width),
            exp_bias.reshape(-1, width),
        ],
        axis=0,
    )
    small = jnp.concatenate([small, jnp.zeros((-small.shape[0] % 8, width), F32)], axis=0)
    r_self, r_attn, r_exp, r_con, total = reduce_grads(
        (g_self, jnp.concatenate([g_o, g_cq, g_ckv, g_co], axis=2), g_exp, g_con),
        small,
        row_count,
        cols,
    )

    def block(array, index):
        return lax.slice_in_dim(array, index * PAIR, (index + 1) * PAIR, axis=1)

    return (
        result_home,
        tokens_home,
        encoded_home,
        block(r_self, 0),
        block(r_self, 1),
        block(r_self, 2),
        block(r_attn, 0).T,
        total[16],
        total[17],
        total[10],
        block(r_attn, 1),
        block(r_attn, 2),
        block(r_attn, 3),
        block(r_attn, 4).T,
        total[18],
        total[19],
        total[5],
        r_exp,
        total[20 : 20 + cols * hid // width].reshape(-1),
        r_con.T,
        total[2],
        total[8],
        total[9],
        total[3],
        total[4],
        total[0],
        total[1],
    )


def solution(mesh):
    return jax.shard_map(
        per_device,
        mesh=mesh,
        in_specs=(
            P(None, ("row", "col"), None),
            P(None, ("row", "col"), None),
            P(None, "row"),
            P(None, ("row", "col"), None),
            P("row", "col"),
            P("row", "col"),
            P("row", "col"),
            P("col", "row"),
            P(),
            P(),
            P(),
            P("row", "col"),
            P("row", "col"),
            P("row", "col"),
            P("col", "row"),
            P(),
            P(),
            P(),
            P("row", "col"),
            P(),
            P("col", "row"),
            P(),
            P(),
            P(),
            P(),
            P(),
            P(),
            P(),
        ),
        out_specs=(
            P(None, ("row", "col"), None),
            P(None, ("row", "col"), None),
            P(None, ("row", "col"), None),
            P("row", "col"),
            P("row", "col"),
            P("row", "col"),
            P("col", "row"),
            P(),
            P(),
            P(),
            P("row", "col"),
            P("row", "col"),
            P("row", "col"),
            P("col", "row"),
            P(),
            P(),
            P(),
            P("row", "col"),
            P(),
            P("col", "row"),
            P(),
            P(),
            P(),
            P(),
            P(),
            P(),
            P(),
        ),
        check_vma=False,
    )
```

```python
import functools

import jax
import jax.numpy as jnp
from jax import lax
from jax.experimental import pallas as pl
from jax.experimental.pallas import tpu as pltpu
from jax.sharding import PartitionSpec as P

HEAD_DIM = 64
PAIR = 2 * HEAD_DIM
NEGATIVE = -1e30
EPSILON = 1e-05
ROW, COL = "row", "col"
AXES = (ROW, COL)
MESH = pl.DeviceIdType.MESH
F32 = jnp.float32
BF16 = jnp.bfloat16
VMEM_SPEC = pl.BlockSpec(memory_space=pltpu.VMEM)
SMEM_SPEC = pl.BlockSpec(memory_space=pltpu.SMEM)
ANY_SPEC = pl.BlockSpec(memory_space=pl.ANY)
VMEM_LIMIT = 67_043_328


def dot_nn(a, b):
    return lax.dot_general(a, b, (((1,), (0,)), ((), ())), preferred_element_type=F32)


def dot_nt(a, b):
    return lax.dot_general(a, b, (((1,), (1,)), ((), ())), preferred_element_type=F32)


def dot_tn(a, b):
    return lax.dot_general(a, b, (((0,), (0,)), ((), ())), preferred_element_type=F32)


def norm_forward(values):
    average = jnp.mean(values, axis=1, keepdims=True)
    centered = values - average
    inverse = lax.rsqrt(jnp.mean(centered * centered, axis=1, keepdims=True) + EPSILON)
    return centered * inverse, inverse


def norm_backward(gradient, normed, inverse, gain):
    scaled = gradient * gain
    mean_scaled = jnp.mean(scaled, axis=1, keepdims=True)
    mean_product = jnp.mean(scaled * normed, axis=1, keepdims=True)
    return (scaled - mean_scaled - normed * mean_product) * inverse


def column_sum(values):
    return jnp.sum(values, axis=0, keepdims=True)


def spread_lanes(column, width):
    return jnp.broadcast_to(column, (column.shape[0], width))


def lane_masks():
    lane = lax.broadcasted_iota(jnp.int32, (1, PAIR), 1)
    first = (lane < HEAD_DIM).astype(F32)
    return first, (1.0 - first)


def attend_block(q_ref, kv_ref, out_ref, lse_ref, row0, rows, span, mask):
    first, second = lane_masks()
    halves = (first.astype(BF16), second.astype(BF16))

    def one_pair(z, carry):
        q_pair = q_ref[z, pl.ds(row0, rows), :]
        k_pair = kv_ref[0, z, pl.ds(0, span), :]
        v_pair = kv_ref[1, z, pl.ds(0, span), :]
        outs, stats = [], []
        for half in halves:
            scores = mask(dot_nt(q_pair * half, k_pair))
            row_max = jnp.max(scores, axis=1, keepdims=True)
            raised = jnp.exp(scores - row_max)
            summed = jnp.sum(raised, axis=1, keepdims=True)
            probs = (raised * (1.0 / summed)).astype(BF16)
            outs.append(dot_nn(probs, v_pair))
            stats.append(row_max + jnp.log(summed))
        out_ref[z, pl.ds(row0, rows), :] = (outs[0] * first + outs[1] * second).astype(BF16)
        lse_ref[z, pl.ds(row0, rows), :] = (
            spread_lanes(stats[0], PAIR) * first + spread_lanes(stats[1], PAIR) * second
        )
        return carry

    lax.fori_loop(0, q_ref.shape[0], one_pair, 0)


def attend_block_back(
    q_ref, kv_ref, mixed_ref, lse_ref, grad_ref, dq_ref, dkv_ref, row0, rows, span, chunk, mask
):
    first, second = lane_masks()
    halves = (first.astype(BF16), second.astype(BF16))

    def one_pair(z, carry):
        q_pair = q_ref[z, pl.ds(row0, rows), :]
        g_pair = grad_ref[z, pl.ds(row0, rows), :]
        stats = jnp.transpose(lse_ref[z, pl.ds(row0, rows), :])
        products = jnp.transpose(
            g_pair.astype(F32) * mixed_ref[z, pl.ds(row0, rows), :].astype(F32)
        )
        lse_rows = (stats[0:1, :], stats[HEAD_DIM : HEAD_DIM + 1, :])
        deltas = (column_sum(products[:HEAD_DIM, :]), column_sum(products[HEAD_DIM:, :]))
        q_half = [q_pair * half for half in halves]
        g_half = [g_pair * half for half in halves]
        dq = [jnp.zeros((rows, PAIR), F32), jnp.zeros((rows, PAIR), F32)]
        for at in range(0, span, chunk):
            k_part = kv_ref[0, z, pl.ds(at, chunk), :]
            v_part = kv_ref[1, z, pl.ds(at, chunk), :]
            dk = jnp.zeros((chunk, PAIR), F32)
            dv = jnp.zeros((chunk, PAIR), F32)
            for h in range(2):
                scores = mask(dot_nt(k_part, q_half[h]), at)
                probs = jnp.exp(scores - lse_rows[h])
                prob_grads = dot_nt(v_part, g_half[h])
                score_low = (probs * (prob_grads - deltas[h])).astype(BF16)
                dv = dv + dot_nn(probs.astype(BF16), g_half[h])
                dk = dk + dot_nn(score_low, q_half[h])
                dq[h] = dq[h] + dot_tn(score_low, k_part)
            dkv_ref[0, z, pl.ds(at, chunk), :] += dk
            dkv_ref[1, z, pl.ds(at, chunk), :] += dv
        dq_ref[z, pl.ds(row0, rows), :] = (dq[0] * first + dq[1] * second).astype(
            BF16
        ) * jnp.asarray(HEAD_DIM**-0.5, BF16)
        return carry

    lax.fori_loop(0, q_ref.shape[0], one_pair, 0)


def causal_last(rows, span):
    def mask(scores):
        query = lax.broadcasted_iota(jnp.int32, scores.shape, 0) + (span - rows)
        key = lax.broadcasted_iota(jnp.int32, scores.shape, 1)
        return jnp.where(key <= query, scores, NEGATIVE)

    return mask


def causal_last_back(rows, span):
    def mask(scores, at):
        if at + scores.shape[0] <= span - rows:
            return scores
        key = lax.broadcasted_iota(jnp.int32, scores.shape, 0) + at
        query = lax.broadcasted_iota(jnp.int32, scores.shape, 1) + (span - rows)
        return jnp.where(key <= query, scores, NEGATIVE)

    return mask


class Refs:
    pass


def named(names, refs):
    out = Refs()
    out.__dict__.update(zip(names, refs))
    return out


def flipped(index, bits):
    for bit in bits:
        index = index + bit - 2 * bit * ((index // bit) % 2)
    return index


def bits_of(number):
    return [1 << i for i in range(number.bit_length()) if (number >> i) & 1]


def subsets(bits):
    out = [0]
    for bit in bits:
        out = out + [m + bit for m in out]
    return out


class Links:
    def __init__(self, send, recv):
        self.send, self.recv, self.count, self.open = send, recv, 0, []

    def take(self, amount=1):
        at = self.count
        self.count += amount
        return at

    def copy(self, src, dst, device, send_at, recv_at):
        return pltpu.make_async_remote_copy(
            src_ref=src,
            dst_ref=dst,
            send_sem=self.send.at[send_at],
            recv_sem=self.recv.at[recv_at],
            device_id=device,
            device_id_type=MESH,
        )

    def start(self, src, dst, device):
        at = self.take()
        copy = self.copy(src, dst, device, at, at)
        copy.start()
        self.open.append(copy)
        return copy

    def drain(self):
        for copy in self.open:
            copy.wait_send()
        self.open = []


class Place:
    def __init__(self, row_count, col_count):
        self.rows, self.cols = row_count, col_count
        self.row, self.col = lax.axis_index(ROW), lax.axis_index(COL)
        self.core = self.row % 2
        self.row_bits = bits_of(row_count - 1)
        self.plane_bits = self.row_bits[1:]
        self.half = col_count // 2
        self.members = subsets(self.plane_bits)
        self.sides = ((0, self.plane_bits), (self.half, self.plane_bits[::-1]))
        self.partner = (flipped(self.row, [1]), self.col)
        self.pair_row = (self.row // 2) * 2

    def greet(self):
        barrier = pltpu.get_barrier_semaphore()
        count = 0
        for side in range(2):
            for k in range(self.cols):
                if side + k:
                    device = (
                        flipped(self.row, [1] if side else []),
                        flipped(self.col, bits_of(k)),
                    )
                    pl.semaphore_signal(barrier, inc=1, device_id=device, device_id_type=MESH)
                    count += 1
        for bit in self.plane_bits:
            device = (flipped(self.row, [bit]), self.col)
            pl.semaphore_signal(barrier, inc=1, device_id=device, device_id_type=MESH)
            count += 1
        pl.semaphore_wait(barrier, count)


class Inbound:
    def __init__(self, place, links, source, target):
        self.place, self.links, self.source, self.target = place, links, source, target
        self.part = source.shape[1]
        self.send_at = links.take(2)
        self.recv_at = self.send_at

    def copies(self):
        p = self.place
        slot = p.col // 2
        to_row = p.pair_row + ((p.col + 1) // 2) % 2
        into = self.target.at[pl.ds(pl.multiple_of(slot * self.part, self.part), self.part)]
        out = []
        for b in range(2):
            device = (to_row, 2 * b + p.core)
            out.append(
                self.links.copy(
                    self.source.at[b], into, device, self.send_at + b, self.recv_at + slot
                )
            )
        local = pltpu.make_async_copy(self.source.at[0], into, self.links.recv.at[self.recv_at])
        return out, local

    def stays(self):
        return self.place.col == self.place.core

    def start(self):
        out, local = self.copies()
        out[1].start()

        @pl.when(self.stays())
        def _():
            local.start()

        @pl.when(jnp.logical_not(self.stays()))
        def _():
            out[0].start()

    def arrive(self):
        p = self.place
        for slot in range(2):
            into = self.target.at[pl.ds(slot * self.part, self.part)]
            remote = self.links.copy(
                self.source.at[0], into, p.partner, self.send_at, self.recv_at + slot
            )
            if slot:
                remote.wait_recv()
            else:
                local = pltpu.make_async_copy(
                    self.source.at[0], into, self.links.recv.at[self.recv_at]
                )

                @pl.when(self.stays())
                def _():
                    local.wait()

                @pl.when(jnp.logical_not(self.stays()))
                def _():
                    remote.wait_recv()

    def drain(self):
        out, _ = self.copies()
        out[1].wait_send()

        @pl.when(jnp.logical_not(self.stays()))
        def _():
            out[0].wait_send()


class Outbound:
    def __init__(self, place, links, source, target):
        self.place, self.links, self.source, self.target = place, links, source, target
        self.part = target.shape[1]
        self.send_at = links.take(2)
        self.recv_at = self.send_at

    def copies(self):
        p = self.place
        micro = p.col // 2
        to_row = p.pair_row + p.col % 2
        out = []
        for i, to_col in enumerate((p.core, 3 - p.core)):
            out.append(
                self.links.copy(
                    self.source.at[pl.ds(i * self.part, self.part)],
                    self.target.at[micro],
                    (to_row, to_col),
                    self.send_at + i,
                    self.recv_at + micro,
                )
            )
        local = pltpu.make_async_copy(
            self.source.at[pl.ds(0, self.part)],
            self.target.at[0],
            self.links.recv.at[self.recv_at],
        )
        return out, local

    def stays(self):
        return self.place.col == self.place.core

    def start(self):
        out, local = self.copies()
        out[1].start()

        @pl.when(self.stays())
        def _():
            local.start()

        @pl.when(jnp.logical_not(self.stays()))
        def _():
            out[0].start()

    def arrive(self):
        p = self.place
        for micro in range(2):
            remote = self.links.copy(
                self.source.at[pl.ds(0, self.part)],
                self.target.at[micro],
                p.partner,
                self.send_at,
                self.recv_at + micro,
            )
            if micro:
                remote.wait_recv()
            else:
                _, local = self.copies()

                @pl.when(self.stays())
                def _():
                    local.wait()

                @pl.when(jnp.logical_not(self.stays()))
                def _():
                    remote.wait_recv()

    def drain(self):
        out, _ = self.copies()
        out[1].wait_send()

        @pl.when(jnp.logical_not(self.stays()))
        def _():
            out[0].wait_send()


class Gather:
    def __init__(self, place, links, shard, whole):
        self.place, self.links, self.shard, self.whole = place, links, shard, whole
        self.plane, self.pair = {}, []

    def start(self):
        p = self.place
        self.along = [
            self.links.start(
                self.shard, self.whole.at[p.col, p.row], (p.row, flipped(p.col, bits_of(k)))
            )
            for k in range(1, p.cols)
        ]
        self.whole[p.col, p.row] = self.shard[...]

    def block(self, side, m):
        p = self.place
        return self.whole.at[pl.ds(side, p.half), flipped(p.row, bits_of(m))]

    def send_out(self, side, order, m):
        p = self.place
        reached = max([order.index(b) for b in bits_of(m)], default=-1)
        here = self.block(side, m)
        for bit in order[reached + 1 :]:
            self.plane[(side, m + bit)] = self.links.start(
                here, here, (flipped(p.row, [bit]), p.col)
            )
        self.pair.append(self.links.start(here, here, p.partner))

    def after_col(self):
        for copy in self.along:
            copy.wait_recv()
        for side, order in self.place.sides:
            self.send_out(side, order, 0)

    def after_plane(self, level):
        for side, order in self.place.sides:
            for m in self.place.members:
                if len(bits_of(m)) == level:
                    self.plane[(side, m)].wait_recv()
                    self.send_out(side, order, m)

    def after_planes(self):
        for level in range(1, len(self.place.plane_bits) + 1):
            self.after_plane(level)

    def finish(self):
        for copy in self.pair:
            copy.wait_recv()


class Reduce:
    def __init__(self, place, links, grads, from_pair, from_plane, from_col, out):
        self.place, self.links, self.grads = place, links, grads
        self.sums, self.from_plane, self.from_col, self.out = from_pair, from_plane, from_col, out
        at = 0
        self.bases = []
        for _, order in place.sides:
            bases = []
            for level in range(len(order)):
                bases.append(at)
                at += len(subsets(order[level + 1 :]))
            self.bases.append(bases)

    def start(self):
        p = self.place
        self.pair = [
            self.links.start(
                self.grads.at[:, flipped(p.row, [1] + bits_of(m))], self.sums.at[at], p.partner
            )
            for at, m in enumerate(p.members)
        ]

    def after_pair(self):
        p = self.place
        for at, m in enumerate(p.members):
            self.pair[at].wait_recv()
            own_row = flipped(p.row, bits_of(m))

            def body(i, carry, at=at, own_row=own_row):
                self.sums[at, i] = (
                    self.grads[i, own_row].astype(F32) + self.sums[at, i].astype(F32)
                ).astype(BF16)
                return carry

            lax.fori_loop(0, p.cols, body, 0)
        self.moving = [self.send(side, 0) for side in range(2)]

    def send(self, side_at, level):
        p = self.place
        side, order = p.sides[side_at]
        bit = order[level]
        batch = []
        for slot, m in enumerate(subsets(order[level + 1 :])):
            at = self.bases[side_at][level] + slot
            copy = self.links.start(
                self.sums.at[p.members.index(m + bit), pl.ds(side, p.half)],
                self.from_plane.at[at],
                (flipped(p.row, [bit]), p.col),
            )
            batch.append((m, at, copy))
        return batch

    def after_plane(self, level):
        p = self.place
        last = level + 1 == len(p.plane_bits)
        for side_at in range(2):
            side = p.sides[side_at][0]
            for m, at, copy in self.moving[side_at]:
                copy.wait_recv()
                into = p.members.index(m)

                def body(i, carry, into=into, at=at, side=side):
                    self.sums[into, side + i] = (
                        self.sums[into, side + i].astype(F32)
                        + self.from_plane[at, i].astype(F32)
                    ).astype(BF16)
                    return carry

                lax.fori_loop(0, p.half, body, 0)
            if not last:
                self.moving[side_at] = self.send(side_at, level + 1)
        if last:
            self.along = []
            for k in range(1, p.cols):
                far = flipped(p.col, bits_of(k))
                self.along.append(
                    self.links.start(self.sums.at[0, far], self.from_col.at[k - 1], (p.row, far))
                )

    def finish(self):
        p = self.place
        total = self.sums[0, p.col].astype(F32)
        for k in range(1, p.cols):
            self.along[k - 1].wait_recv()
            total = total + self.from_col[k - 1].astype(F32)
        self.out[...] = total


class Total:
    def __init__(self, place, links, sums, arrived):
        self.place, self.links, self.sums, self.arrived = place, links, sums, arrived
        self.steps = [(b, 0) for b in place.row_bits] + [(b, 1) for b in bits_of(place.cols - 1)]
        self.at = 0

    def start(self):
        p = self.place
        bit, axis = self.steps[self.at]
        device = (flipped(p.row, [bit]), p.col) if axis == 0 else (p.row, flipped(p.col, [bit]))
        self.copy = self.links.start(self.sums.at[self.at % 2], self.arrived.at[self.at], device)

    def step(self):
        if self.at < len(self.steps):
            self.copy.wait_recv()
            if self.at:
                self.before.wait_send()
                self.links.open = [c for c in self.links.open if c is not self.before]
            self.before = self.copy
            at = self.at
            self.sums[(at + 1) % 2] = self.sums[at % 2] + self.arrived[at]
            self.at += 1
            if self.at < len(self.steps):
                self.start()

    def finish(self):
        while self.at < len(self.steps):
            self.step()
        return self.sums[self.at % 2]


def flat_rows(value):
    count, depth, width = value.shape
    if depth % 16 or value.dtype == F32:
        return value.astype(F32).reshape(count * depth, width).astype(value.dtype)
    return value.reshape(count * depth, width)


def row_blocks(value, count):
    return value.reshape(count, value.shape[0] // count, value.shape[1]).astype(BF16)


def layer_kernel(row_count, col_count, names, *refs):
    g = named(names, refs)
    p = Place(row_count, col_count)
    links = Links(g.send, g.recv)
    part = g.tokens.shape[1]
    width = g.tokens.shape[2]
    hid = g.expand.shape[1]
    cols = col_count
    own = 2 * part
    span = 4 * part
    scale = HEAD_DIM**-0.5
    low_at = pl.multiple_of(p.core * part, part)
    high_at = pl.multiple_of((3 - p.core) * part, part)
    other_low = pl.multiple_of((1 - p.core) * part, part)
    other_high = pl.multiple_of((2 + p.core) * part, part)

    def self_w(z, lo=0, hi=3):
        return flat_rows(g.w_self[z, :, :, lo * PAIR : hi * PAIR])

    def attn_w(z, at, count=1):
        return flat_rows(g.w_attn[z, :, :, at * PAIR : (at + count) * PAIR])

    def heads_of(vector, z):
        return vector[:, z * PAIR : (z + 1) * PAIR]

    p.greet()
    x_in = Inbound(p, links, g.tokens, g.x)
    e_in = Inbound(p, links, g.encoded, g.e)
    og_in = Inbound(p, links, g.og_low, g.og)
    x_in.start()
    g.pack_self[:, 0:PAIR] = g.self_query[...]
    g.pack_self[:, PAIR : 2 * PAIR] = g.self_key[...]
    g.pack_self[:, 2 * PAIR :] = g.self_value[...]
    get_self = Gather(p, links, g.pack_self, g.w_self)
    get_self.start()
    for i, shard in enumerate(
        (g.self_output, g.cross_query, g.cross_key, g.cross_value, g.cross_output)
    ):
        value = shard[...]
        if i in (0, 4):
            value = jnp.transpose(value.astype(F32)).astype(BF16)
        g.pack_attn[:, i * PAIR : (i + 1) * PAIR] = value
    get_attn = Gather(p, links, g.pack_attn, g.w_attn)
    g.pack_hidden[:, 0:hid] = g.expand[...]
    g.pack_hidden[:, hid:] = jnp.transpose(g.contract[...].astype(F32)).astype(BF16)
    get_hidden = Gather(p, links, g.pack_hidden, g.w_hidden)
    for m in range(2):
        g.len_own[m] = jnp.full(g.len_own.shape[1:], g.source_len[m, 0], jnp.int32)
    len_copy = links.start(g.len_own, g.len_other, p.partner)
    g.og_low[...] = g.out_grad[...].astype(BF16)
    get_self.after_col()
    get_attn.start()
    e_in.start()
    get_self.after_planes()
    get_attn.after_col()
    get_self.finish()
    x_in.arrive()

    x = g.x[...]
    for z in range(cols):
        rows = dot_nn(x, self_w(z))
        g.q[z] = ((rows[:, 0:PAIR] + heads_of(g.self_query_bias, z)) * scale).astype(BF16)
        k_rows = rows[:, PAIR : 2 * PAIR].astype(BF16)
        v_rows = (rows[:, 2 * PAIR :] + heads_of(g.self_value_bias, z)).astype(BF16)
        for i, value in enumerate((k_rows, v_rows)):
            g.kv[i, z, pl.ds(low_at, part), :] = value[:part]
            g.kv[i, z, pl.ds(high_at, part), :] = value[part:]

    def swap(ref):
        out = []
        for at in (low_at, high_at):
            piece = ref.at[:, :, pl.ds(at, part), :]
            out.append(links.start(piece, piece, p.partner))
        return out

    def swapped(copies):
        for copy in copies:
            copy.wait_recv()

    kv_swap = swap(g.kv)
    get_hidden.start()
    get_attn.after_plane(1)
    swapped(kv_swap)
    for block in range(2):
        for parity in range(2):

            @pl.when(p.core == parity)
            def _():
                keys = (4 - parity if block else parity + 1) * part
                attend_block(
                    g.q, g.kv, g.mixed, g.lse, block * part, part, keys, causal_last(part, keys)
                )

        if block == 0:
            for level in range(2, len(p.plane_bits) + 1):
                get_attn.after_plane(level)
            get_hidden.after_col()
            og_in.start()
    get_attn.finish()
    e_in.arrive()
    len_copy.wait_recv()
    e = g.e[...]
    for z in range(cols):
        rows = dot_nn(e, attn_w(z, 2, 2))
        k_rows = rows[:, :PAIR].astype(BF16)
        v_rows = (rows[:, PAIR:] + heads_of(g.cross_value_bias, z)).astype(BF16)
        for i, value in enumerate((k_rows, v_rows)):
            g.ckv[i, z, pl.ds(low_at, part), :] = value[:part]
            g.ckv[i, z, pl.ds(high_at, part), :] = value[part:]
    ckv_swap = swap(g.ckv)

    branch = g.self_output_bias[...] + g.x[...].astype(F32)
    for z in range(cols):
        branch = branch + dot_nt(g.mixed[z], attn_w(z, 0))
    normed, inverse = norm_forward(branch)
    g.n1[...] = normed
    g.i1[...] = spread_lanes(inverse, PAIR)
    first_low = (normed * g.attn_gain[...] + g.attn_shift[...]).astype(BF16)
    for z in range(cols):
        g.cq[z] = (
            (dot_nn(first_low, attn_w(z, 1)) + heads_of(g.cross_query_bias, z)) * scale
        ).astype(BF16)
    get_hidden.after_plane(1)

    mine = p.col % 2 == p.core
    first_micro = p.col // 2 == 0
    own_len = jnp.where(first_micro, g.len_own[0, 0:1, 0:1], g.len_own[1, 0:1, 0:1])
    other_len = jnp.where(first_micro, g.len_other[0, 0:1, 0:1], g.len_other[1, 0:1, 0:1])
    limit = jnp.where(mine, own_len, other_len)

    def source_mask(scores):
        key = lax.broadcasted_iota(jnp.int32, scores.shape, 1)
        return jnp.where(key < limit, scores, NEGATIVE)

    def source_mask_back(scores, at):
        key = lax.broadcasted_iota(jnp.int32, scores.shape, 0) + at
        return jnp.where(key < limit, scores, NEGATIVE)

    swapped(ckv_swap)
    for block in range(2):
        attend_block(g.cq, g.ckv, g.cmixed, g.clse, block * part, part, span, source_mask)
        if block == 0:
            for level in range(2, len(p.plane_bits) + 1):
                get_hidden.after_plane(level)
    branch = g.n1[...] * g.attn_gain[...] + g.attn_shift[...] + g.cross_output_bias[...]
    for z in range(cols):
        branch = branch + dot_nt(g.cmixed[z], attn_w(z, 4))
    normed, inverse = norm_forward(branch)
    g.n2[...] = normed
    g.i2[...] = spread_lanes(inverse, PAIR)
    get_hidden.finish()
    og_in.arrive()

    result_out = Outbound(p, links, g.result_low, g.result_home)

    def hidden_stage(inner_ref, hidden_ref, low_ref, total_ref):
        second = g.n2[...] * g.cross_gain[...] + g.cross_shift[...]
        low_ref[...] = second.astype(BF16)
        total_ref[...] = second + g.contract_bias[...]

        def forward(z, carry):
            bias = g.expand_bias[:, pl.ds(pl.multiple_of(z * hid, PAIR), hid)]
            inner = dot_nn(low_ref[...], flat_rows(g.w_hidden[z, :, :, :hid])) + bias
            inner_ref[z] = inner
            hidden = (inner * jax.nn.sigmoid(inner)).astype(BF16)
            hidden_ref[z] = hidden
            total_ref[...] += dot_nt(hidden, flat_rows(g.w_hidden[z, :, :, hid:]))
            return carry

        lax.fori_loop(0, cols, forward, 0)
        normed, inverse = norm_forward(total_ref[...])
        g.result_low[...] = (normed * g.final_gain[...] + g.final_shift[...]).astype(BF16)
        result_out.start()
        gradient = g.og[...].astype(F32)
        g.small[0, 0:1, :] = column_sum(gradient * normed)
        g.small[0, 1:2, :] = column_sum(gradient)
        third = norm_backward(gradient, normed, inverse, g.final_gain[...])
        g.small[0, 2:3, :] = column_sum(third)
        third_low = third.astype(BF16)
        total_ref[...] = third

        def backward(z, carry):
            inner = inner_ref[z]
            hidden_back = dot_nn(third_low, flat_rows(g.w_hidden[z, :, :, hid:]))
            g.g_hidden[z, :, :, hid:] = row_blocks(dot_tn(third_low, hidden_ref[z]), row_count)
            logistic = jax.nn.sigmoid(inner)
            inner_back = (hidden_back * logistic * (1.0 + inner * (1.0 - logistic))).astype(BF16)
            g.small[0, pl.ds(13 + z, 1), :] = column_sum(inner_back.astype(F32))
            g.g_hidden[z, :, :, :hid] = row_blocks(dot_tn(low_ref[...], inner_back), row_count)
            total_ref[...] += dot_nt(inner_back, flat_rows(g.w_hidden[z, :, :, :hid]))
            return carry

        lax.fori_loop(0, cols, backward, 0)
        gradient = total_ref[...]
        normed = g.n2[...]
        g.small[0, 3:4, :] = column_sum(gradient * normed)
        g.small[0, 4:5, :] = column_sum(gradient)
        second_grad = norm_backward(gradient, normed, g.i2[:, 0:1], g.cross_gain[...])
        g.small[0, 5:6, :] = column_sum(second_grad)
        g.grad[...] = second_grad

    pl.run_scoped(
        hidden_stage,
        pltpu.VMEM((cols, own, hid), F32),
        pltpu.VMEM((cols, own, hid), BF16),
        pltpu.VMEM((own, width), BF16),
        pltpu.VMEM((own, width), F32),
    )
    put_hidden = Reduce(p, links, g.g_hidden, g.p_hidden, g.q_hidden, g.c_hidden, g.r_hidden)
    put_hidden.start()
    put_back = Reduce(p, links, g.g_back, g.p_back, g.q_back, g.c_back, g.r_back)
    put_enc = Reduce(p, links, g.g_enc, g.p_enc, g.q_enc, g.c_enc, g.r_enc)
    put_self = Reduce(p, links, g.g_self, g.p_self, g.q_self, g.c_self, g.r_self)
    enc_out = Outbound(p, links, g.enc_low, g.enc_home)
    tok_out = Outbound(p, links, g.tok_low, g.tok_home)

    def trade(acc_ref, stage_ref, arrive_ref):
        for i in range(2):
            stage_ref[i, :, 0:part, :] = acc_ref[i, :, pl.ds(other_low, part), :].astype(BF16)
            stage_ref[i, :, part:own, :] = acc_ref[i, :, pl.ds(other_high, part), :].astype(BF16)
        return links.start(stage_ref, arrive_ref, p.partner)

    def joined(acc_ref, arrive_ref, i, z):
        mine_rows = jnp.concatenate(
            [acc_ref[i, z, pl.ds(low_at, part), :], acc_ref[i, z, pl.ds(high_at, part), :]],
            axis=0,
        )
        return (mine_rows + arrive_ref[i, z].astype(F32)).astype(BF16)

    def back_stage(cross_acc, self_acc):
        grad_low = g.grad[...].astype(BF16)
        for z in range(cols):
            g.g_back[z, :, :, 2 * PAIR :] = row_blocks(dot_tn(grad_low, g.cmixed[z]), row_count)
            g.mixed_back[z] = dot_nn(grad_low, attn_w(z, 4)).astype(BF16)
        cross_acc[...] = jnp.zeros_like(cross_acc)
        for block in range(2):
            attend_block_back(
                g.cq,
                g.ckv,
                g.cmixed,
                g.clse,
                g.mixed_back,
                g.dq,
                cross_acc,
                block * part,
                part,
                span,
                own,
                source_mask_back,
            )
            if block == 0:
                put_hidden.after_pair()
        ckv_trade = trade(cross_acc, g.stage_cross, g.arrive_cross)
        put_hidden.after_plane(0)
        normed = g.n1[...]
        first_low = (normed * g.attn_gain[...] + g.attn_shift[...]).astype(BF16)
        gradient = g.grad[...]
        for z in range(cols):
            dq = g.dq[z]
            g.g_back[z, :, :, PAIR : 2 * PAIR] = row_blocks(dot_tn(first_low, dq), row_count)
            g.small[0, 11:12, z * PAIR : (z + 1) * PAIR] = column_sum(dq.astype(F32))
            gradient = gradient + dot_nt(dq, attn_w(z, 1))
        g.small[0, 6:7, :] = column_sum(gradient * normed)
        g.small[0, 7:8, :] = column_sum(gradient)
        first_grad = norm_backward(gradient, normed, g.i1[:, 0:1], g.attn_gain[...])
        g.small[0, 8:9, :] = column_sum(first_grad)
        g.grad[...] = first_grad
        grad_low = first_grad.astype(BF16)
        for z in range(cols):
            g.g_back[z, :, :, 0:PAIR] = row_blocks(dot_tn(grad_low, g.mixed[z]), row_count)
            g.mixed_back[z] = dot_nn(grad_low, attn_w(z, 0)).astype(BF16)
        put_back.start()

        ckv_trade.wait_recv()
        e = g.e[...]
        for z in range(cols):
            dk = joined(cross_acc, g.arrive_cross, 0, z)
            dv = joined(cross_acc, g.arrive_cross, 1, z)
            g.small[0, 12:13, z * PAIR : (z + 1) * PAIR] = column_sum(dv.astype(F32))
            both = jnp.concatenate([dk, dv], axis=1)
            g.g_enc[z] = row_blocks(dot_tn(e, both), row_count)
            term = dot_nt(both, attn_w(z, 2, 2))
            total = term if z == 0 else total + term
        g.enc_low[...] = total.astype(BF16)
        enc_out.start()
        put_enc.start()
        for level in range(1, len(p.plane_bits)):
            put_hidden.after_plane(level)

        self_acc[...] = jnp.zeros_like(self_acc)
        for block in range(2):
            for parity in range(2):

                @pl.when(p.core == parity)
                def _():
                    keys = (4 - parity if block else parity + 1) * part
                    attend_block_back(
                        g.q,
                        g.kv,
                        g.mixed,
                        g.lse,
                        g.mixed_back,
                        g.dq,
                        self_acc,
                        block * part,
                        part,
                        keys,
                        part,
                        causal_last_back(part, keys),
                    )

            if block == 0:
                put_back.after_pair()
                put_enc.after_pair()
        kv_trade = trade(self_acc, g.stage_self, g.arrive_self)
        for level in range(len(p.plane_bits)):
            put_back.after_plane(level)
            put_enc.after_plane(level)
        kv_trade.wait_recv()
        x = g.x[...]
        total = g.grad[...]
        for z in range(cols):
            dq = g.dq[z]
            dk = joined(self_acc, g.arrive_self, 0, z)
            dv = joined(self_acc, g.arrive_self, 1, z)
            g.small[0, 9:10, z * PAIR : (z + 1) * PAIR] = column_sum(dq.astype(F32))
            g.small[0, 10:11, z * PAIR : (z + 1) * PAIR] = column_sum(dv.astype(F32))
            both = jnp.concatenate([dq, dk, dv], axis=1)
            g.g_self[z] = row_blocks(dot_tn(x, both), row_count)
            total = total + dot_nt(both, self_w(z))
        g.tok_low[...] = total.astype(BF16)

        tok_out.start()
        put_self.start()
        total = Total(p, links, g.small, g.small_arrived)
        total.start()
        put_hidden.finish()
        put_back.finish()
        put_enc.finish()
        put_self.after_pair()
        total.step()
        for level in range(len(p.plane_bits)):
            put_self.after_plane(level)
            total.step()
        g.r_small[...] = total.finish()
        put_self.finish()
        for moved in (result_out, enc_out, tok_out):
            moved.arrive()
            moved.drain()
        for moved in (x_in, e_in, og_in):
            moved.drain()
        links.drain()

    count = g.small.shape[1]
    g.small[0, 13 + cols : count, :] = jnp.zeros((count - 13 - cols, width), F32)
    pl.run_scoped(
        back_stage,
        pltpu.VMEM((2, cols, span, PAIR), F32),
        pltpu.VMEM((2, cols, span, PAIR), F32),
    )


def finish_kernel(width, names, out_names, *refs):
    g = named(names, refs[: len(names)])
    homes, o = refs[len(names) : len(names) + 3], named(out_names, refs[len(names) + 3 :])
    for home, source in zip(homes, (g.result_home, g.tok_home, g.enc_home)):
        home[...] = source[...].astype(F32)
    hid = o.expand.shape[1]

    def block(ref, at):
        return ref[:, at * PAIR : (at + 1) * PAIR]

    o.self_query[...] = block(g.r_self, 0)
    o.self_key[...] = block(g.r_self, 1)
    o.self_value[...] = block(g.r_self, 2)
    o.self_output[...] = jnp.transpose(block(g.r_back, 0))
    o.cross_query[...] = block(g.r_back, 1)
    o.cross_output[...] = jnp.transpose(block(g.r_back, 2))
    o.cross_key[...] = block(g.r_enc, 0)
    o.cross_value[...] = block(g.r_enc, 1)
    o.expand[...] = g.r_hidden[:, :hid]
    o.contract[...] = jnp.transpose(g.r_hidden[:, hid:])
    vectors = (
        o.final_gain,
        o.final_shift,
        o.contract_bias,
        o.cross_gain,
        o.cross_shift,
        o.cross_output_bias,
        o.attn_gain,
        o.attn_shift,
        o.self_output_bias,
        o.self_query_bias,
        o.self_value_bias,
        o.cross_query_bias,
        o.cross_value_bias,
    )
    for i, vector in enumerate(vectors):
        vector[...] = g.r_small[i : i + 1, :]
    at = len(vectors)
    for z in range(o.expand_bias.shape[1] // width):
        o.expand_bias[:, z * width : (z + 1) * width] = g.r_small[at + z : at + z + 1, :]


def per_device(
    tokens,
    encoded,
    source_len,
    out_grad,
    self_query,
    self_key,
    self_value,
    self_output,
    self_query_bias,
    self_value_bias,
    self_output_bias,
    cross_query,
    cross_key,
    cross_value,
    cross_output,
    cross_query_bias,
    cross_value_bias,
    cross_output_bias,
    expand,
    expand_bias,
    contract,
    contract_bias,
    attn_gain,
    attn_shift,
    cross_gain,
    cross_shift,
    final_gain,
    final_shift,
):
    inputs = dict(locals())
    row_count = lax.axis_size(ROW)
    cols = lax.axis_size(COL)
    micro_count, part, width = tokens.shape
    depth, head_width = self_query.shape
    hid = expand.shape[1]
    assert micro_count == 2 and cols == 4 and source_len.shape[1] == 1
    assert head_width == PAIR and row_count % 4 == 0 and hid == width
    own = 2 * part
    plane = row_count // 2
    small_rows = -(-(13 + cols) // 8) * 8
    small_steps = len(bits_of(row_count - 1)) + len(bits_of(cols - 1))
    links = 3 * (cols - 1 + 2 * (plane - 1) + 2 * plane)
    links += 4 * (plane + 2 * (plane - 1) + cols - 1) + small_steps
    links += 6 * 2 + 1 + 4 + 2

    def whole(columns):
        return pltpu.VMEM((cols, row_count, depth, columns), BF16)

    def from_pair(columns):
        return pltpu.VMEM((plane, cols, depth, columns), BF16)

    def from_plane(columns):
        return pltpu.VMEM((2 * (plane - 1), cols // 2, depth, columns), BF16)

    def from_col(columns):
        return pltpu.VMEM((cols - 1, depth, columns), BF16)

    rows_low = pltpu.VMEM((own, width), BF16)
    rows_f32 = pltpu.VMEM((own, width), F32)
    stat_f32 = pltpu.VMEM((own, PAIR), F32)
    heads_low = pltpu.VMEM((cols, own, PAIR), BF16)
    heads_f32 = pltpu.VMEM((cols, own, PAIR), F32)
    keys_low = pltpu.VMEM((2, cols, 2 * own, PAIR), BF16)
    half_keys = pltpu.VMEM((2, cols, own, PAIR), BF16)
    lengths = pltpu.VMEM((2, 8, PAIR), jnp.int32)
    scratch = dict(
        x=rows_low,
        e=rows_low,
        og=rows_low,
        og_low=pltpu.VMEM((2, part, width), BF16),
        pack_self=pltpu.VMEM((depth, 3 * PAIR), BF16),
        pack_attn=pltpu.VMEM((depth, 5 * PAIR), BF16),
        pack_hidden=pltpu.VMEM((depth, 2 * hid), BF16),
        w_self=whole(3 * PAIR),
        w_attn=whole(5 * PAIR),
        w_hidden=whole(2 * hid),
        len_own=lengths,
        len_other=lengths,
        q=heads_low,
        kv=keys_low,
        ckv=keys_low,
        mixed=heads_low,
        lse=heads_f32,
        n1=rows_f32,
        i1=stat_f32,
        cq=heads_low,
        cmixed=heads_low,
        clse=heads_f32,
        n2=rows_f32,
        i2=stat_f32,
        grad=rows_f32,
        mixed_back=heads_low,
        dq=heads_low,
        result_low=rows_low,
        enc_low=rows_low,
        tok_low=rows_low,
        stage_cross=half_keys,
        arrive_cross=half_keys,
        stage_self=half_keys,
        arrive_self=half_keys,
        small=pltpu.VMEM((2, small_rows, width), F32),
        small_arrived=pltpu.VMEM((small_steps, small_rows, width), F32),
        g_hidden=whole(2 * hid),
        p_hidden=from_pair(2 * hid),
        q_hidden=from_plane(2 * hid),
        c_hidden=from_col(2 * hid),
        g_back=whole(3 * PAIR),
        p_back=from_pair(3 * PAIR),
        q_back=from_plane(3 * PAIR),
        c_back=from_col(3 * PAIR),
        g_enc=whole(2 * PAIR),
        p_enc=from_pair(2 * PAIR),
        q_enc=from_plane(2 * PAIR),
        c_enc=from_col(2 * PAIR),
        g_self=whole(3 * PAIR),
        p_self=from_pair(3 * PAIR),
        q_self=from_plane(3 * PAIR),
        c_self=from_col(3 * PAIR),
        send=pltpu.SemaphoreType.DMA((links,)),
        recv=pltpu.SemaphoreType.DMA((links,)),
    )
    home = jax.ShapeDtypeStruct((2, part, width), BF16)
    outs = dict(
        result_home=(home, ANY_SPEC),
        tok_home=(home, ANY_SPEC),
        enc_home=(home, ANY_SPEC),
        r_self=(jax.ShapeDtypeStruct((depth, 3 * PAIR), F32), VMEM_SPEC),
        r_back=(jax.ShapeDtypeStruct((depth, 3 * PAIR), F32), VMEM_SPEC),
        r_enc=(jax.ShapeDtypeStruct((depth, 2 * PAIR), F32), VMEM_SPEC),
        r_hidden=(jax.ShapeDtypeStruct((depth, 2 * hid), F32), VMEM_SPEC),
        r_small=(jax.ShapeDtypeStruct((small_rows, width), F32), VMEM_SPEC),
    )
    names = tuple(inputs)
    specs = [ANY_SPEC, ANY_SPEC, SMEM_SPEC] + [VMEM_SPEC] * (len(names) - 3)
    moved = pl.pallas_call(
        functools.partial(layer_kernel, row_count, cols, names + tuple(outs) + tuple(scratch)),
        out_shape=[shape for shape, _ in outs.values()],
        in_specs=specs,
        out_specs=[spec for _, spec in outs.values()],
        scratch_shapes=list(scratch.values()),
        compiler_params=pltpu.CompilerParams(
            collective_id=0, has_side_effects=True, vmem_limit_bytes=VMEM_LIMIT
        ),
        name="layer",
    )(*(v.reshape(1, -1) if v.ndim == 1 else v for v in inputs.values()))
    shapes = [(2, part, width)] * 3 + [inputs[n].shape for n in names[4:]]
    final = pl.pallas_call(
        functools.partial(finish_kernel, width, tuple(outs), names[4:]),
        out_shape=[
            jax.ShapeDtypeStruct((1,) + shape if len(shape) == 1 else shape, F32)
            for shape in shapes
        ],
        in_specs=[VMEM_SPEC] * len(outs),
        out_specs=[VMEM_SPEC] * len(shapes),
        compiler_params=pltpu.CompilerParams(vmem_limit_bytes=VMEM_LIMIT),
        name="finish",
    )(*moved)
    return tuple(v.reshape(-1) if v.shape[0] == 1 else v for v in final)


def solution(mesh):
    tokens, down, across, same = P(None, AXES, None), P(ROW, COL), P(COL, ROW), P()
    attention = (down, down, down, across, same, same, same)
    weights = attention * 2 + (down, same, across) + (same,) * 7
    return jax.shard_map(
        per_device,
        mesh=mesh,
        in_specs=(tokens, tokens, P(None, ROW), tokens) + weights,
        out_specs=(tokens, tokens, tokens) + weights,
        check_vma=False,
    )
```

```python
import functools

import jax
import jax.numpy as jnp
from jax import lax
from jax.experimental import pallas as pl
from jax.experimental.pallas import tpu as pltpu
from jax.sharding import PartitionSpec as P

HEAD_DIM = 64
PAIR = 2 * HEAD_DIM
NEGATIVE = -1e30
EPSILON = 1e-05
ROW, COL = "row", "col"
AXES = (ROW, COL)
MESH = pl.DeviceIdType.MESH
F32 = jnp.float32
BF16 = jnp.bfloat16
VMEM_SPEC = pl.BlockSpec(memory_space=pltpu.VMEM)
SMEM_SPEC = pl.BlockSpec(memory_space=pltpu.SMEM)
ANY_SPEC = pl.BlockSpec(memory_space=pl.ANY)
VMEM_LIMIT = 67_043_328


def dot_nn(a, b):
    return lax.dot_general(a, b, (((1,), (0,)), ((), ())), preferred_element_type=F32)


def dot_nt(a, b):
    return lax.dot_general(a, b, (((1,), (1,)), ((), ())), preferred_element_type=F32)


def dot_tn(a, b):
    return lax.dot_general(a, b, (((0,), (0,)), ((), ())), preferred_element_type=F32)


def norm_forward(values):
    average = jnp.mean(values, axis=1, keepdims=True)
    centered = values - average
    inverse = lax.rsqrt(jnp.mean(centered * centered, axis=1, keepdims=True) + EPSILON)
    return centered * inverse, inverse


def norm_backward(gradient, normed, inverse, gain):
    scaled = gradient * gain
    mean_scaled = jnp.mean(scaled, axis=1, keepdims=True)
    mean_product = jnp.mean(scaled * normed, axis=1, keepdims=True)
    return (scaled - mean_scaled - normed * mean_product) * inverse


def column_sum(values):
    return jnp.sum(values, axis=0, keepdims=True)


def spread_lanes(column, width):
    return jnp.broadcast_to(column, (column.shape[0], width))


def lane_masks():
    lane = lax.broadcasted_iota(jnp.int32, (1, PAIR), 1)
    first = (lane < HEAD_DIM).astype(F32)
    return first, (1.0 - first)


def attend_block(q_ref, kv_ref, out_ref, lse_ref, row0, rows, span, mask, pairs):
    first, second = lane_masks()
    halves = (first.astype(BF16), second.astype(BF16))

    def one_pair(z, carry):
        q_pair = q_ref[z, pl.ds(row0, rows), :]
        k_pair = kv_ref[0, z, pl.ds(0, span), :]
        v_pair = kv_ref[1, z, pl.ds(0, span), :]
        outs, stats = [], []
        for half in halves:
            scores = mask(dot_nt(q_pair * half, k_pair))
            row_max = jnp.max(scores, axis=1, keepdims=True)
            raised = jnp.exp(scores - row_max)
            summed = jnp.sum(raised, axis=1, keepdims=True)
            probs = (raised * (1.0 / summed)).astype(BF16)
            outs.append(dot_nn(probs, v_pair))
            stats.append(row_max + jnp.log(summed))
        out_ref[z, pl.ds(row0, rows), :] = (outs[0] * first + outs[1] * second).astype(BF16)
        lse_ref[z, pl.ds(row0, rows), :] = (
            spread_lanes(stats[0], PAIR) * first + spread_lanes(stats[1], PAIR) * second
        )
        return carry

    lax.fori_loop(pairs[0], pairs[1], one_pair, 0)


def attend_block_back(
    q_ref,
    kv_ref,
    mixed_ref,
    lse_ref,
    grad_ref,
    dq_ref,
    dkv_ref,
    row0,
    rows,
    span,
    chunk,
    mask,
    pairs,
):
    first, second = lane_masks()
    halves = (first.astype(BF16), second.astype(BF16))

    def one_pair(z, carry):
        q_pair = q_ref[z, pl.ds(row0, rows), :]
        g_pair = grad_ref[z, pl.ds(row0, rows), :]
        stats = jnp.transpose(lse_ref[z, pl.ds(row0, rows), :])
        products = jnp.transpose(
            g_pair.astype(F32) * mixed_ref[z, pl.ds(row0, rows), :].astype(F32)
        )
        lse_rows = (stats[0:1, :], stats[HEAD_DIM : HEAD_DIM + 1, :])
        deltas = (column_sum(products[:HEAD_DIM, :]), column_sum(products[HEAD_DIM:, :]))
        q_half = [q_pair * half for half in halves]
        g_half = [g_pair * half for half in halves]
        dq = [jnp.zeros((rows, PAIR), F32), jnp.zeros((rows, PAIR), F32)]
        for at in range(0, span, chunk):
            k_part = kv_ref[0, z, pl.ds(at, chunk), :]
            v_part = kv_ref[1, z, pl.ds(at, chunk), :]
            dk = jnp.zeros((chunk, PAIR), F32)
            dv = jnp.zeros((chunk, PAIR), F32)
            for h in range(2):
                scores = mask(dot_nt(k_part, q_half[h]), at)
                probs = jnp.exp(scores - lse_rows[h])
                prob_grads = dot_nt(v_part, g_half[h])
                score_low = (probs * (prob_grads - deltas[h])).astype(BF16)
                dv = dv + dot_nn(probs.astype(BF16), g_half[h])
                dk = dk + dot_nn(score_low, q_half[h])
                dq[h] = dq[h] + dot_tn(score_low, k_part)
            dkv_ref[0, z, pl.ds(at, chunk), :] += dk
            dkv_ref[1, z, pl.ds(at, chunk), :] += dv
        dq_ref[z, pl.ds(row0, rows), :] = (dq[0] * first + dq[1] * second).astype(
            BF16
        ) * jnp.asarray(HEAD_DIM**-0.5, BF16)
        return carry

    lax.fori_loop(pairs[0], pairs[1], one_pair, 0)


def causal_last(rows, span):
    def mask(scores):
        query = lax.broadcasted_iota(jnp.int32, scores.shape, 0) + (span - rows)
        key = lax.broadcasted_iota(jnp.int32, scores.shape, 1)
        return jnp.where(key <= query, scores, NEGATIVE)

    return mask


def causal_last_back(rows, span):
    def mask(scores, at):
        if at + scores.shape[0] <= span - rows:
            return scores
        key = lax.broadcasted_iota(jnp.int32, scores.shape, 0) + at
        query = lax.broadcasted_iota(jnp.int32, scores.shape, 1) + (span - rows)
        return jnp.where(key <= query, scores, NEGATIVE)

    return mask


class Refs:
    pass


def named(names, refs):
    out = Refs()
    out.__dict__.update(zip(names, refs))
    return out


def flipped(index, bits):
    for bit in bits:
        index = index + bit - 2 * bit * ((index // bit) % 2)
    return index


def bits_of(number):
    return [1 << i for i in range(number.bit_length()) if (number >> i) & 1]


def subsets(bits):
    out = [0]
    for bit in bits:
        out = out + [m + bit for m in out]
    return out


class Links:
    def __init__(self, send, recv):
        self.send, self.recv, self.count = send, recv, 0

    def take(self, amount=1):
        at = self.count
        self.count += amount
        return at

    def copy(self, src, dst, device, send_at, recv_at):
        return pltpu.make_async_remote_copy(
            src_ref=src,
            dst_ref=dst,
            send_sem=self.send.at[send_at],
            recv_sem=self.recv.at[recv_at],
            device_id=device,
            device_id_type=MESH,
        )


class Place:
    def __init__(self, row_count, col_count):
        self.rows, self.cols = row_count, col_count
        self.row, self.col = lax.axis_index(ROW), lax.axis_index(COL)
        self.core = self.row % 2
        self.row_bits = bits_of(row_count - 1)
        self.plane_bits = self.row_bits[1:]
        self.half = col_count // 2
        self.members = subsets(self.plane_bits)
        self.sides = ((0, self.plane_bits), (self.half, self.plane_bits[::-1]))
        self.partner = (flipped(self.row, [1]), self.col)
        self.pair_row = (self.row // 2) * 2

    def greet(self):
        barrier = pltpu.get_barrier_semaphore()
        count = 0
        for side in range(2):
            for k in range(self.cols):
                if side + k:
                    device = (
                        flipped(self.row, [1] if side else []),
                        flipped(self.col, bits_of(k)),
                    )
                    pl.semaphore_signal(barrier, inc=1, device_id=device, device_id_type=MESH)
                    count += 1
        for bit in self.plane_bits:
            device = (flipped(self.row, [bit]), self.col)
            pl.semaphore_signal(barrier, inc=1, device_id=device, device_id_type=MESH)
            count += 1
        pl.semaphore_wait(barrier, count)


class Inbound:
    def __init__(self, place, links, source, target):
        self.place, self.links, self.source, self.target = place, links, source, target
        self.part = source.shape[1]
        self.send_at = links.take(2)
        self.recv_at = self.send_at

    def copies(self):
        p = self.place
        slot = p.col // 2
        to_row = p.pair_row + ((p.col + 1) // 2) % 2
        into = self.target.at[pl.ds(pl.multiple_of(slot * self.part, self.part), self.part)]
        out = []
        for b in range(2):
            device = (to_row, 2 * b + p.core)
            out.append(
                self.links.copy(
                    self.source.at[b], into, device, self.send_at + b, self.recv_at + slot
                )
            )
        local = pltpu.make_async_copy(self.source.at[0], into, self.links.recv.at[self.recv_at])
        return out, local

    def stays(self):
        return self.place.col == self.place.core

    def start(self):
        out, local = self.copies()
        out[1].start()

        @pl.when(self.stays())
        def _():
            local.start()

        @pl.when(jnp.logical_not(self.stays()))
        def _():
            out[0].start()

    def arrive(self):
        p = self.place
        for slot in range(2):
            into = self.target.at[pl.ds(slot * self.part, self.part)]
            remote = self.links.copy(
                self.source.at[0], into, p.partner, self.send_at, self.recv_at + slot
            )
            if slot:
                remote.wait_recv()
            else:
                local = pltpu.make_async_copy(
                    self.source.at[0], into, self.links.recv.at[self.recv_at]
                )

                @pl.when(self.stays())
                def _():
                    local.wait()

                @pl.when(jnp.logical_not(self.stays()))
                def _():
                    remote.wait_recv()

    def drain(self):
        out, _ = self.copies()
        out[1].wait_send()

        @pl.when(jnp.logical_not(self.stays()))
        def _():
            out[0].wait_send()


class Outbound:
    def __init__(self, place, links, source, target):
        self.place, self.links, self.source, self.target = place, links, source, target
        self.part = target.shape[1]
        self.send_at = links.take(2)
        self.recv_at = self.send_at

    def copies(self):
        p = self.place
        micro = p.col // 2
        to_row = p.pair_row + p.col % 2
        out = []
        for i, to_col in enumerate((p.core, 3 - p.core)):
            out.append(
                self.links.copy(
                    self.source.at[pl.ds(i * self.part, self.part)],
                    self.target.at[micro],
                    (to_row, to_col),
                    self.send_at + i,
                    self.recv_at + micro,
                )
            )
        local = pltpu.make_async_copy(
            self.source.at[pl.ds(0, self.part)],
            self.target.at[0],
            self.links.recv.at[self.recv_at],
        )
        return out, local

    def stays(self):
        return self.place.col == self.place.core

    def start(self):
        out, local = self.copies()
        out[1].start()

        @pl.when(self.stays())
        def _():
            local.start()

        @pl.when(jnp.logical_not(self.stays()))
        def _():
            out[0].start()

    def arrive(self):
        p = self.place
        for micro in range(2):
            remote = self.links.copy(
                self.source.at[pl.ds(0, self.part)],
                self.target.at[micro],
                p.partner,
                self.send_at,
                self.recv_at + micro,
            )
            if micro:
                remote.wait_recv()
            else:
                _, local = self.copies()

                @pl.when(self.stays())
                def _():
                    local.wait()

                @pl.when(jnp.logical_not(self.stays()))
                def _():
                    remote.wait_recv()

    def drain(self):
        out, _ = self.copies()
        out[1].wait_send()

        @pl.when(jnp.logical_not(self.stays()))
        def _():
            out[0].wait_send()


class Gather:
    def __init__(self, place, links, shard, whole, relayed):
        self.place, self.links, self.shard, self.whole = place, links, shard, whole
        self.relayed = relayed
        self.along_at = links.take(2 * (place.cols - 1))
        self.base = {}
        for m in place.members:
            if m:
                self.base[(False, m)] = links.take(place.cols)
            self.base[(True, m)] = links.take()
        self.orders = (place.plane_bits, place.plane_bits[::-1])
        whole[place.col, place.row] = shard[...]

    def sources(self, step):
        p = self.place
        if step == 0:
            return [(p.col, None, 0)]
        if not self.relayed:
            return [(flipped(p.col, bits_of(step)), None, 0)]
        return [
            (p.col - step, p.col >= step, 1),
            (p.col + step, p.col + step < p.cols, -1),
        ]

    def guarded(self, valid, action):
        if valid is None:
            action()
        else:
            pl.when(valid)(action)

    def hop(self, step, column, direction):
        p = self.place
        block = self.whole.at[column, p.row]
        if not self.relayed:
            at = self.along_at + step - 1
            return self.links.copy(block, block, (p.row, flipped(p.col, bits_of(step))), at, at)
        at = self.along_at + 2 * (step - 1) + (0 if direction > 0 else 1)
        return self.links.copy(block, block, (p.row, p.col + direction), at, at)

    def forward(self, step, column, direction, act):
        p = self.place
        if not self.relayed:
            for far in range(1, p.cols if step == 0 else 0):
                act(self.hop(far, column, 0))
            return
        if step + 1 >= p.cols:
            return
        for way in (1, -1) if step == 0 else (direction,):
            room = p.col + 1 < p.cols if way > 0 else p.col > 0

            @pl.when(room)
            def _(way=way):
                act(self.hop(step + 1, column, way))

    def plane_copy(self, column, m, bit):
        p = self.place
        block = self.whole.at[column, flipped(p.row, bits_of(m))]
        at = self.base[(False, m + bit)] + column
        return self.links.copy(block, block, (flipped(p.row, [bit]), p.col), at, at)

    def pair_copy(self, m):
        p = self.place
        block = self.whole.at[:, flipped(p.row, bits_of(m))]
        at = self.base[(True, m)]
        return self.links.copy(block, block, p.partner, at, at)

    def to_pair(self, level):
        for m in self.place.members:
            if len(bits_of(m)) == level:
                self.pair_copy(m).start()

    def outgoing(self, step, column, m):
        order = self.orders[step % 2]
        reached = max([order.index(b) for b in bits_of(m)], default=-1)
        return [self.plane_copy(column, m, bit) for bit in order[reached + 1 :]]

    def start(self):
        p = self.place
        self.forward(0, p.col, 0, lambda c: c.start())

    def start_plane(self):
        for copy in self.outgoing(0, self.place.col, 0):
            copy.start()

    def step(self, step):
        for column, valid, direction in self.sources(step):

            def action(column=column, direction=direction):
                self.hop(step, column, direction).wait_recv()
                self.forward(step, column, direction, lambda c: c.start())
                for copy in self.outgoing(step, column, 0):
                    copy.start()

            self.guarded(valid, action)

    def arrived(self, column, m, order):
        bit = max(bits_of(m), key=order.index)
        return self.plane_copy(column, m - bit, bit)

    def plane(self, step, level):
        order = self.orders[step % 2]
        for column, valid, _ in self.sources(step):

            def action(column=column):
                for m in self.place.members:
                    if len(bits_of(m)) == level:
                        self.arrived(column, m, order).wait_recv()
                        for copy in self.outgoing(step, column, m):
                            copy.start()

            self.guarded(valid, action)

    def planes_from(self, step, first):
        for level in range(first, len(self.place.plane_bits) + 1):
            self.plane(step, level)

    def each(self, visit):
        p = self.place
        for step in range(p.cols):
            for column, valid, direction in self.sources(step):
                self.guarded(
                    valid, functools.partial(visit, step=step, column=column, direction=direction)
                )

    def finish(self):
        for m in self.place.members:
            self.pair_copy(m).wait_recv()

    def drain(self):
        for m in self.place.members:
            self.pair_copy(m).wait_send()

        def visit(step, column, direction):
            self.forward(step, column, direction, lambda c: c.wait_send())
            for m in self.place.members:
                for copy in self.outgoing(step, column, m):
                    copy.wait_send()

        self.each(visit)


class Reduce:
    def __init__(self, place, links, grads, from_pair, from_plane, from_col, total, out, relayed):
        self.place, self.links, self.grads = place, links, grads
        self.relayed = relayed
        self.sums, self.from_plane, self.from_col = from_pair, from_plane, from_col
        self.total, self.out = total, out
        self.moves = []
        for side_at, (_, order) in enumerate(place.sides):
            for level in range(len(order)):
                for m in subsets(order[level + 1 :]):
                    self.moves.append((side_at, level, m))
        self.pair_at = links.take(len(place.members) * (place.cols if relayed else 1))
        self.plane_at = links.take(len(self.moves))
        self.along_at = links.take(2 * (place.cols - 1))
        self.out_at = links.take()

    def pair_copy(self, at, m, column=None):
        p = self.place
        if column is not None:
            sem = self.pair_at + at * p.cols + column
            return self.links.copy(
                self.grads.at[column, flipped(p.row, [1] + bits_of(m))],
                self.sums.at[at, column],
                p.partner,
                sem,
                sem,
            )
        return self.links.copy(
            self.grads.at[:, flipped(p.row, [1] + bits_of(m))],
            self.sums.at[at],
            p.partner,
            self.pair_at + at,
            self.pair_at + at,
        )

    def pair_copies(self, at, m):
        if self.relayed:
            return [self.pair_copy(at, m, column) for column in range(self.place.cols)]
        return [self.pair_copy(at, m)]

    def start(self):
        for at, m in enumerate(self.place.members):
            self.pair_copy(at, m).start()

    def start_column(self, column):
        for at, m in enumerate(self.place.members):
            self.pair_copy(at, m, column).start()

    def after_pair(self):
        p = self.place
        for at, m in enumerate(p.members):
            for copy in self.pair_copies(at, m):
                copy.wait_recv()
            own_row = flipped(p.row, bits_of(m))

            def body(i, carry, at=at, own_row=own_row):
                self.sums[at, i] = (
                    self.grads[i, own_row].astype(F32) + self.sums[at, i].astype(F32)
                ).astype(BF16)
                return carry

            lax.fori_loop(0, p.cols, body, 0)
        self.send(0)

    def plane_copy(self, at):
        p = self.place
        side_at, level, m = self.moves[at]
        side, order = p.sides[side_at]
        bit = order[level]
        return self.links.copy(
            self.sums.at[p.members.index(m + bit), pl.ds(side, p.half)],
            self.from_plane.at[at],
            (flipped(p.row, [bit]), p.col),
            self.plane_at + at,
            self.plane_at + at,
        )

    def at_level(self, level):
        return [at for at, move in enumerate(self.moves) if move[1] == level]

    def send(self, level):
        for at in self.at_level(level):
            self.plane_copy(at).start()

    def after_plane(self, level):
        p = self.place
        for at in self.at_level(level):
            side_at, _, m = self.moves[at]
            self.plane_copy(at).wait_recv()
            into, side = p.members.index(m), p.sides[side_at][0]

            def body(i, carry, into=into, at=at, side=side):
                self.sums[into, side + i] = (
                    self.sums[into, side + i].astype(F32) + self.from_plane[at, i].astype(F32)
                ).astype(BF16)
                return carry

            lax.fori_loop(0, p.half, body, 0)
        if level + 1 < len(p.plane_bits):
            self.send(level + 1)
        else:
            for step in range(1, 2 if self.relayed else p.cols):
                self.hops(step, lambda c: c.start())

    def hop(self, step, way, column):
        p = self.place
        if not self.relayed:
            at = self.along_at + step - 1
            return self.links.copy(
                self.sums.at[0, column], self.from_col.at[step - 1], (p.row, column), at, at
            )
        slot = 2 * (step - 1) + (0 if way > 0 else 1)
        at = self.along_at + slot
        return self.links.copy(
            self.sums.at[0, column], self.from_col.at[slot], (p.row, p.col + way), at, at
        )

    def hops(self, step, act):
        p = self.place
        if not self.relayed:
            act(self.hop(step, 0, flipped(p.col, bits_of(step))))
            return
        for way in (1, -1):
            here = p.col if way > 0 else p.cols - 1 - p.col
            column = p.cols + p.col - step if way > 0 else p.col - p.cols + step
            inner = p.col + 1 < p.cols if way > 0 else p.col > 0

            @pl.when(jnp.logical_and(here < step, inner))
            def _(way=way, column=column, step=step):
                act(self.hop(step, way, column))

    def step(self, step):
        p = self.place
        for way in (1, -1):
            here = p.col if way > 0 else p.cols - 1 - p.col
            column = p.cols + p.col - 1 - step if way > 0 else p.col - p.cols + 1 + step
            slot = 2 * (step - 1) + (0 if way > 0 else 1)

            @pl.when(jnp.logical_and(here >= 1, here <= step))
            def _(way=way, column=column, slot=slot):
                self.hop(step, way, column).wait_recv()
                self.sums[0, column] = (
                    self.sums[0, column].astype(F32) + self.from_col[slot].astype(F32)
                ).astype(BF16)

        if step + 1 < p.cols:
            self.hops(step + 1, lambda c: c.start())

    def out_copy(self):
        return pltpu.make_async_copy(self.total, self.out, self.links.recv.at[self.out_at])

    def finish(self, done=0):
        p = self.place
        last = p.cols - 1
        if not self.relayed:
            total = self.sums[0, p.col].astype(F32)
            for step in range(1, p.cols):
                self.hop(step, 0, flipped(p.col, bits_of(step))).wait_recv()
                total = total + self.from_col[step - 1].astype(F32)
            self.total[...] = total
        else:
            for step in range(done + 1, last):
                self.step(step)
            self.total[...] = self.sums[0, p.col].astype(F32)
            for way in (1, -1):
                here = p.col if way > 0 else p.cols - 1 - p.col
                slot = 2 * (last - 1) + (0 if way > 0 else 1)

                @pl.when(here >= 1)
                def _(way=way, slot=slot):
                    self.hop(last, way, p.col).wait_recv()
                    self.total[...] += self.from_col[slot].astype(F32)

        self.out_copy().start()

    def drain(self):
        for at, m in enumerate(self.place.members):
            for copy in self.pair_copies(at, m):
                copy.wait_send()
        for at in range(len(self.moves)):
            self.plane_copy(at).wait_send()
        for step in range(1, self.place.cols):
            self.hops(step, lambda c: c.wait_send())
        self.out_copy().wait()


class Swap:
    def __init__(self, place, links, pieces):
        self.place, self.links, self.pieces = place, links, pieces
        self.at = links.take(len(pieces))

    def each(self, act):
        for i, (source, target) in enumerate(self.pieces):
            at = self.at + i
            act(self.links.copy(source, target, self.place.partner, at, at))

    def start(self):
        self.each(lambda c: c.start())

    def arrive(self):
        self.each(lambda c: c.wait_recv())

    def drain(self):
        self.each(lambda c: c.wait_send())


class Total:
    def __init__(self, place, links, sums, arrived, col_first):
        self.place, self.links, self.sums, self.arrived = place, links, sums, arrived
        self.col_at = links.take(place.cols - 1)
        self.row_at = links.take(len(place.row_bits))
        self.steps = len(place.row_bits) + 1
        self.col_step = 0 if col_first else self.steps - 1

    def copies(self, i):
        p = self.place
        if i == self.col_step:
            out = []
            for k in range(1, p.cols):
                at = self.col_at + k - 1
                device = (p.row, flipped(p.col, bits_of(k)))
                into = self.arrived.at[self.steps - 2 + k]
                out.append(self.links.copy(self.sums.at[i], into, device, at, at))
            return out
        bit = i - 1 if self.col_step == 0 else i
        at = self.row_at + bit
        device = (flipped(p.row, [p.row_bits[bit]]), p.col)
        return [self.links.copy(self.sums.at[i], self.arrived.at[bit], device, at, at)]

    def start(self, i=0):
        for copy in self.copies(i):
            copy.start()

    def step(self, i):
        p = self.place
        for copy in self.copies(i):
            copy.wait_recv()
        if i == self.col_step:
            total = None
            for c in range(p.cols):
                term = jnp.where(p.col == c, self.sums[i], 0.0)
                for k in range(1, p.cols):
                    here = flipped(p.col, bits_of(k)) == c
                    term = jnp.where(here, self.arrived[self.steps - 2 + k], term)
                total = term if total is None else total + term
        else:
            total = self.sums[i] + self.arrived[i - 1 if self.col_step == 0 else i]
        self.sums[i + 1] = total
        if i + 1 < self.steps:
            self.start(i + 1)

    def result(self):
        return self.sums[self.steps]

    def drain(self):
        for i in range(self.steps):
            for copy in self.copies(i):
                copy.wait_send()


def flat_rows(value):
    count, depth, width = value.shape
    if depth % 16 or value.dtype == F32:
        return value.astype(F32).reshape(count * depth, width).astype(value.dtype)
    return value.reshape(count * depth, width)


def row_blocks(value, count):
    return value.reshape(count, value.shape[0] // count, value.shape[1]).astype(BF16)


def layer_kernel(row_count, col_count, names, *refs):
    g = named(names, refs)
    p = Place(row_count, col_count)
    links = Links(g.send, g.recv)
    part = g.tokens.shape[1]
    width = g.tokens.shape[2]
    hid = g.expand.shape[1]
    cols = col_count
    own = 2 * part
    span = 4 * part
    scale = HEAD_DIM**-0.5
    low_at = pl.multiple_of(p.core * part, part)
    high_at = pl.multiple_of((3 - p.core) * part, part)
    other_low = pl.multiple_of((1 - p.core) * part, part)
    other_high = pl.multiple_of((2 + p.core) * part, part)

    def self_w(z, lo=0, hi=3):
        return flat_rows(g.w_self[z, :, :, lo * PAIR : hi * PAIR])

    def attn_w(z, at, count=1):
        return flat_rows(g.w_attn[z, :, :, at * PAIR : (at + count) * PAIR])

    def heads_of(vector, z):
        return vector[:, z * PAIR : (z + 1) * PAIR]

    p.greet()
    x_in = Inbound(p, links, g.tokens, g.x)
    e_in = Inbound(p, links, g.encoded, g.e)
    og_in = Inbound(p, links, g.og_low, g.og)
    g.pack_self[:, 0:PAIR] = g.self_query[...]
    g.pack_self[:, PAIR : 2 * PAIR] = g.self_key[...]
    g.pack_self[:, 2 * PAIR :] = g.self_value[...]
    get_self = Gather(p, links, g.pack_self, g.w_self, False)
    get_self.start()
    get_self.start_plane()
    x_in.start()
    for i, shard in enumerate(
        (g.self_output, g.cross_query, g.cross_key, g.cross_value, g.cross_output)
    ):
        g.pack_attn[:, i * PAIR : (i + 1) * PAIR] = shard[...]
    get_attn = Gather(p, links, g.pack_attn, g.w_attn, False)
    g.pack_hidden[:, 0:hid] = g.expand[...]
    g.pack_hidden[:, hid:] = g.contract[...]
    get_hidden = Gather(p, links, g.pack_hidden, g.w_hidden, True)
    for m in range(2):
        g.len_own[m] = jnp.full(g.len_own.shape[1:], g.source_len[0, m], jnp.int32)
    len_swap = Swap(p, links, [(g.len_own, g.len_other)])
    len_swap.start()
    levels = range(2, len(p.plane_bits) + 1)
    get_self.step(1)
    get_self.plane(0, 1)
    get_self.step(2)
    get_self.plane(1, 1)
    get_self.step(3)
    get_self.to_pair(0)
    get_self.plane(2, 1)
    get_self.plane(3, 1)
    get_self.to_pair(1)
    get_attn.start_plane()
    g.og_low[...] = g.out_grad[...].astype(BF16)
    for level in levels:
        for step in range(cols):
            get_self.plane(step, level)
        get_self.to_pair(level)
    get_attn.start()
    get_hidden.start()
    get_self.finish()
    x_in.arrive()
    e_in.start()

    def key_swap(ref, pairs):
        pieces = []
        for at in (low_at, high_at):
            piece = ref.at[:, pl.ds(pairs[0], pairs[1] - pairs[0]), pl.ds(at, part), :]
            pieces.append((piece, piece))
        return Swap(p, links, pieces)

    def keep_keys(ref, z, k_rows, v_rows):
        for i, value in enumerate((k_rows, v_rows)):
            ref[i, z, pl.ds(low_at, part), :] = value[:part].astype(BF16)
            ref[i, z, pl.ds(high_at, part), :] = value[part:].astype(BF16)

    ranges = ((0, cols // 2), (cols // 2, cols))
    half = cols // 2
    kv_swaps = [key_swap(g.kv, pairs) for pairs in ranges]
    ckv_swaps = [key_swap(g.ckv, pairs) for pairs in ranges]
    x = g.x[...]
    for pairs, swap in zip(ranges, kv_swaps):
        for z in range(*pairs):
            rows = dot_nn(x, self_w(z))
            g.q[z] = ((rows[:, 0:PAIR] + heads_of(g.self_query_bias, z)) * scale).astype(BF16)
            keep_keys(
                g.kv,
                z,
                rows[:, PAIR : 2 * PAIR],
                rows[:, 2 * PAIR :] + heads_of(g.self_value_bias, z),
            )
        swap.start()

    def in_segments(work, breaks):
        def segment(at, carry):
            block, first = at % 2, (at // 2) * half
            for i, (before, _) in enumerate(breaks):
                if before is not None:
                    pl.when(at == i)(before)
            work(block, (first, first + half))
            for i, (_, after) in enumerate(breaks):
                if after is not None:
                    pl.when(at == i)(after)
            return carry

        lax.fori_loop(0, 4, segment, 0)

    def causal_blocks(block, run):
        for later in range(2):
            for parity in range(2):
                keys = (4 - parity if later else parity + 1) * part

                @pl.when(jnp.logical_and(block == later, p.core == parity))
                def _(later=later, keys=keys):
                    run(later * part, keys)

    def self_block(block, pairs):
        causal_blocks(
            block,
            lambda row0, keys: attend_block(
                g.q, g.kv, g.mixed, g.lse, row0, part, keys, causal_last(part, keys), pairs
            ),
        )

    def after_self_0():
        get_attn.step(1)
        get_attn.plane(0, 1)

    def after_self_1():
        get_attn.step(2)
        get_attn.step(3)
        get_attn.to_pair(0)
        get_attn.plane(1, 1)
        for level in levels:
            get_attn.plane(0, level)
        get_hidden.step(1)
        kv_swaps[1].arrive()

    def after_self_2():
        get_attn.plane(2, 1)
        get_attn.plane(3, 1)
        get_attn.to_pair(1)
        for level in levels:
            get_attn.plane(1, level)
        get_hidden.start_plane()

    in_segments(
        self_block,
        (
            (kv_swaps[0].arrive, after_self_0),
            (None, after_self_1),
            (None, after_self_2),
            (None, None),
        ),
    )
    for level in levels:
        for step in range(2, cols):
            get_attn.plane(step, level)
        get_attn.to_pair(level)
    get_hidden.step(2)
    get_attn.finish()
    branch = g.self_output_bias[...] + g.x[...].astype(F32)
    for z in range(cols):
        branch = branch + dot_nt(g.mixed[z], attn_w(z, 0))
    normed, inverse = norm_forward(branch)
    g.n1[...] = normed
    g.i1[...] = spread_lanes(inverse, PAIR)
    first_low = (normed * g.attn_gain[...] + g.attn_shift[...]).astype(BF16)
    for z in range(cols):
        g.cq[z] = (
            (dot_nn(first_low, attn_w(z, 1)) + heads_of(g.cross_query_bias, z)) * scale
        ).astype(BF16)
    e_in.arrive()
    len_swap.arrive()
    e = g.e[...]
    for pairs, swap in zip(ranges, ckv_swaps):
        for z in range(*pairs):
            rows = dot_nn(e, attn_w(z, 2, 2))
            keep_keys(
                g.ckv, z, rows[:, :PAIR], rows[:, PAIR:] + heads_of(g.cross_value_bias, z)
            )
        swap.start()
    get_hidden.plane(0, 1)
    get_hidden.plane(1, 1)

    mine = p.col % 2 == p.core
    first_micro = p.col // 2 == 0
    own_len = jnp.where(first_micro, g.len_own[0, 0:1, 0:1], g.len_own[1, 0:1, 0:1])
    other_len = jnp.where(first_micro, g.len_other[0, 0:1, 0:1], g.len_other[1, 0:1, 0:1])
    limit = jnp.where(mine, own_len, other_len)

    def source_mask(scores):
        key = lax.broadcasted_iota(jnp.int32, scores.shape, 1)
        return jnp.where(key < limit, scores, NEGATIVE)

    def source_mask_back(scores, at):
        key = lax.broadcasted_iota(jnp.int32, scores.shape, 0) + at
        return jnp.where(key < limit, scores, NEGATIVE)

    def cross_block(block, pairs):
        row0 = pl.multiple_of(block * part, part)
        attend_block(g.cq, g.ckv, g.cmixed, g.clse, row0, part, span, source_mask, pairs)

    def after_cross_0():
        get_hidden.step(3)
        get_hidden.to_pair(0)
        get_hidden.planes_from(0, 2)
        og_in.start()

    def after_cross_1():
        get_hidden.plane(2, 1)
        get_hidden.planes_from(1, 2)
        ckv_swaps[1].arrive()

    def after_cross_2():
        get_hidden.plane(3, 1)
        get_hidden.to_pair(1)
        get_hidden.planes_from(2, 2)

    in_segments(
        cross_block,
        (
            (ckv_swaps[0].arrive, after_cross_0),
            (None, after_cross_1),
            (None, after_cross_2),
            (None, None),
        ),
    )
    get_hidden.planes_from(3, 2)
    for level in levels:
        get_hidden.to_pair(level)
    branch = g.n1[...] * g.attn_gain[...] + g.attn_shift[...] + g.cross_output_bias[...]
    for z in range(cols):
        branch = branch + dot_nt(g.cmixed[z], attn_w(z, 4))
    normed, inverse = norm_forward(branch)
    g.n2[...] = normed
    g.i2[...] = spread_lanes(inverse, PAIR)
    get_hidden.finish()
    og_in.arrive()

    result_out = Outbound(p, links, g.result_low, g.result_home)
    put_hidden = Reduce(
        p, links, g.g_hidden, g.p_hidden, g.q_hidden, g.c_hidden, g.t_hidden, g.r_hidden, True
    )

    def hidden_stage(inner_ref, hidden_ref, low_ref, total_ref):
        second = g.n2[...] * g.cross_gain[...] + g.cross_shift[...]
        low_ref[...] = second.astype(BF16)
        total_ref[...] = second + g.contract_bias[...]

        def forward(z, carry):
            bias = g.expand_bias[:, pl.ds(pl.multiple_of(z * hid, PAIR), hid)]
            inner = dot_nn(low_ref[...], flat_rows(g.w_hidden[z, :, :, :hid])) + bias
            inner_ref[z] = inner
            hidden = (inner * jax.nn.sigmoid(inner)).astype(BF16)
            hidden_ref[z] = hidden
            total_ref[...] += dot_nt(hidden, flat_rows(g.w_hidden[z, :, :, hid:]))
            return carry

        lax.fori_loop(0, cols, forward, 0)
        normed, inverse = norm_forward(total_ref[...])
        g.result_low[...] = (normed * g.final_gain[...] + g.final_shift[...]).astype(BF16)
        result_out.start()
        gradient = g.og[...].astype(F32)
        g.small[0, 0:1, :] = column_sum(gradient * normed)
        g.small[0, 1:2, :] = column_sum(gradient)
        third = norm_backward(gradient, normed, inverse, g.final_gain[...])
        g.small[0, 2:3, :] = column_sum(third)
        third_low = third.astype(BF16)
        total_ref[...] = third

        def backward(z, carry):
            inner = inner_ref[z]
            hidden_back = dot_nn(third_low, flat_rows(g.w_hidden[z, :, :, hid:]))
            g.g_hidden[z, :, :, hid:] = row_blocks(dot_tn(third_low, hidden_ref[z]), row_count)
            logistic = jax.nn.sigmoid(inner)
            inner_back = (hidden_back * logistic * (1.0 + inner * (1.0 - logistic))).astype(BF16)
            g.small[0, pl.ds(13 + z, 1), :] = column_sum(inner_back.astype(F32))
            g.g_hidden[z, :, :, :hid] = row_blocks(dot_tn(low_ref[...], inner_back), row_count)
            put_hidden.start_column(z)
            total_ref[...] += dot_nt(inner_back, flat_rows(g.w_hidden[z, :, :, :hid]))
            return carry

        lax.fori_loop(0, cols, backward, 0)
        gradient = total_ref[...]
        normed = g.n2[...]
        g.small[0, 3:4, :] = column_sum(gradient * normed)
        g.small[0, 4:5, :] = column_sum(gradient)
        second_grad = norm_backward(gradient, normed, g.i2[:, 0:1], g.cross_gain[...])
        g.small[0, 5:6, :] = column_sum(second_grad)
        g.grad[...] = second_grad

    pl.run_scoped(
        hidden_stage,
        pltpu.VMEM((cols, own, hid), F32),
        pltpu.VMEM((cols, own, hid), BF16),
        pltpu.VMEM((own, width), BF16),
        pltpu.VMEM((own, width), F32),
    )
    put_attn = Reduce(
        p, links, g.g_attn, g.p_attn, g.q_attn, g.c_attn, g.t_attn, g.r_attn, True
    )
    put_self = Reduce(
        p, links, g.g_self, g.p_self, g.q_self, g.c_self, g.t_self, g.r_self, False
    )
    enc_out = Outbound(p, links, g.enc_low, g.enc_home)
    tok_out = Outbound(p, links, g.tok_low, g.tok_home)
    early = Total(p, links, g.small, g.small_arrived, True)
    late = Total(p, links, g.late, g.late_arrived, False)

    def trade(stage_ref, arrive_ref, pairs):
        here = pl.ds(pairs[0], pairs[1] - pairs[0])
        return Swap(p, links, [(stage_ref.at[:, here], arrive_ref.at[:, here])])

    ckv_trades = [trade(g.stage_cross, g.arrive_cross, pairs) for pairs in ranges]
    kv_trades = [trade(g.stage_self, g.arrive_self, pairs) for pairs in ranges]

    def hand_over(acc_ref, stage_ref, trades, at):
        first = ranges[at][0]
        here = pl.ds(first, half)
        for i in range(2):
            stage_ref[i, here, 0:part, :] = acc_ref[i, here, pl.ds(other_low, part), :].astype(
                BF16
            )
            stage_ref[i, here, part:own, :] = acc_ref[i, here, pl.ds(other_high, part), :].astype(
                BF16
            )
        trades[at].start()

    def joined(acc_ref, arrive_ref, i, z):
        mine_rows = jnp.concatenate(
            [acc_ref[i, z, pl.ds(low_at, part), :], acc_ref[i, z, pl.ds(high_at, part), :]],
            axis=0,
        )
        return (mine_rows + arrive_ref[i, z].astype(F32)).astype(BF16)

    def back_stage(cross_acc, self_acc):
        grad_low = g.grad[...].astype(BF16)
        for z in range(cols):
            g.g_attn[z, :, :, 2 * PAIR : 3 * PAIR] = row_blocks(dot_tn(grad_low, g.cmixed[z]), row_count)
            g.mixed_back[z] = dot_nn(grad_low, attn_w(z, 4)).astype(BF16)
        cross_acc[...] = jnp.zeros_like(cross_acc)

        def cross_block_back(block, pairs):
            attend_block_back(
                g.cq,
                g.ckv,
                g.cmixed,
                g.clse,
                g.mixed_back,
                g.dq,
                cross_acc,
                pl.multiple_of(block * part, part),
                part,
                span,
                own,
                source_mask_back,
                pairs,
            )

        def after_back_1():
            hand_over(cross_acc, g.stage_cross, ckv_trades, 0)

        in_segments(
            cross_block_back,
            ((put_hidden.after_pair, None), (None, after_back_1), (None, None), (None, None)),
        )
        hand_over(cross_acc, g.stage_cross, ckv_trades, 1)
        put_hidden.after_plane(0)
        normed = g.n1[...]
        first_low = (normed * g.attn_gain[...] + g.attn_shift[...]).astype(BF16)
        gradient = g.grad[...]
        for z in range(cols):
            dq = g.dq[z]
            g.g_attn[z, :, :, PAIR : 2 * PAIR] = row_blocks(dot_tn(first_low, dq), row_count)
            g.small[0, 11:12, z * PAIR : (z + 1) * PAIR] = column_sum(dq.astype(F32))
            gradient = gradient + dot_nt(dq, attn_w(z, 1))
        g.small[0, 6:7, :] = column_sum(gradient * normed)
        g.small[0, 7:8, :] = column_sum(gradient)
        first_grad = norm_backward(gradient, normed, g.i1[:, 0:1], g.attn_gain[...])
        g.small[0, 8:9, :] = column_sum(first_grad)
        g.grad[...] = first_grad
        grad_low = first_grad.astype(BF16)
        for z in range(cols):
            g.g_attn[z, :, :, 0:PAIR] = row_blocks(dot_tn(grad_low, g.mixed[z]), row_count)
            g.mixed_back[z] = dot_nn(grad_low, attn_w(z, 0)).astype(BF16)

        early.start()

        for swap in ckv_trades:
            swap.arrive()
        e = g.e[...]
        for z in range(cols):
            dk = joined(cross_acc, g.arrive_cross, 0, z)
            dv = joined(cross_acc, g.arrive_cross, 1, z)
            g.late[0, 2:3, z * PAIR : (z + 1) * PAIR] = column_sum(dv.astype(F32))
            both = jnp.concatenate([dk, dv], axis=1)
            g.g_attn[z, :, :, 3 * PAIR :] = row_blocks(dot_tn(e, both), row_count)
            put_attn.start_column(z)
            term = dot_nt(both, attn_w(z, 2, 2))
            total = term if z == 0 else total + term
        g.enc_low[...] = total.astype(BF16)
        enc_out.start()

        self_acc[...] = jnp.zeros_like(self_acc)

        def self_block_back(block, pairs):
            causal_blocks(
                block,
                lambda row0, keys: attend_block_back(
                    g.q,
                    g.kv,
                    g.mixed,
                    g.lse,
                    g.mixed_back,
                    g.dq,
                    self_acc,
                    row0,
                    part,
                    keys,
                    part,
                    causal_last_back(part, keys),
                    pairs,
                ),
            )


        for level in range(1, len(p.plane_bits)):
            put_hidden.after_plane(level)

        def after_back_0():
            put_attn.after_pair()
            early.step(0)

        def after_back_1():
            hand_over(self_acc, g.stage_self, kv_trades, 0)
            put_hidden.step(1)
            early.step(1)

        def after_back_2():
            put_attn.after_plane(0)
            early.step(2)

        in_segments(
            self_block_back,
            ((None, after_back_0), (None, after_back_1), (None, after_back_2), (None, None)),
        )
        hand_over(self_acc, g.stage_self, kv_trades, 1)
        for level in range(1, len(p.plane_bits)):
            put_attn.after_plane(level)
        put_hidden.step(2)
        for i in range(3, early.steps):
            early.step(i)
        for swap in kv_trades:
            swap.arrive()
        x = g.x[...]
        total = g.grad[...]
        for z in range(cols):
            dq = g.dq[z]
            dk = joined(self_acc, g.arrive_self, 0, z)
            dv = joined(self_acc, g.arrive_self, 1, z)
            g.late[0, 0:1, z * PAIR : (z + 1) * PAIR] = column_sum(dq.astype(F32))
            g.late[0, 1:2, z * PAIR : (z + 1) * PAIR] = column_sum(dv.astype(F32))
            both = jnp.concatenate([dq, dk, dv], axis=1)
            g.g_self[z] = row_blocks(dot_tn(x, both), row_count)
            total = total + dot_nt(both, self_w(z))
        g.tok_low[...] = total.astype(BF16)

        put_attn.step(1)
        late.start()
        put_self.start()
        tok_out.start()
        put_self.after_pair()
        put_attn.step(2)
        late.step(0)
        put_self.after_plane(0)
        late.step(1)
        for level in range(1, len(p.plane_bits)):
            put_self.after_plane(level)
        for i in range(2, late.steps - 1):
            late.step(i)
        put_hidden.finish(2)
        put_attn.finish(2)
        late.step(late.steps - 1)
        g.t_small[...] = early.result()
        g.t_small[9:11, :] = late.result()[0:2, :]
        g.t_small[12:13, :] = late.result()[2:3, :]
        small_out = pltpu.make_async_copy(g.t_small, g.r_small, g.recv.at[small_at])
        small_out.start()
        put_self.finish()
        for moved in (result_out, enc_out, tok_out):
            moved.arrive()
            moved.drain()
        small_out.wait()
        for moved in (x_in, e_in, og_in, get_self, get_attn, get_hidden, len_swap, early, late):
            moved.drain()
        for moved in kv_swaps + ckv_swaps + ckv_trades + kv_trades:
            moved.drain()
        for moved in (put_hidden, put_attn, put_self):
            moved.drain()
        assert links.count <= g.send.shape[0]

    small_at = links.take()
    g.small[0, 9:11, :] = jnp.zeros((2, width), F32)
    g.small[0, 12:13, :] = jnp.zeros((1, width), F32)
    g.late[0] = jnp.zeros(g.late.shape[1:], F32)
    count = g.small.shape[1]
    g.small[0, 13 + cols : count, :] = jnp.zeros((count - 13 - cols, width), F32)
    pl.run_scoped(
        back_stage,
        pltpu.VMEM((2, cols, span, PAIR), F32),
        pltpu.VMEM((2, cols, span, PAIR), F32),
    )


def finish_kernel(width, names, out_names, *refs):
    g = named(names, refs[: len(names)])
    homes, o = refs[len(names) : len(names) + 3], named(out_names, refs[len(names) + 3 :])
    for home, source in zip(homes, (g.result_home, g.tok_home, g.enc_home)):
        home[...] = source[...].astype(F32)
    hid = o.expand.shape[1]

    def block(ref, at):
        return ref[:, at * PAIR : (at + 1) * PAIR]

    o.self_query[...] = block(g.r_self, 0)
    o.self_key[...] = block(g.r_self, 1)
    o.self_value[...] = block(g.r_self, 2)
    o.self_output[...] = block(g.r_attn, 0)
    o.cross_query[...] = block(g.r_attn, 1)
    o.cross_output[...] = block(g.r_attn, 2)
    o.cross_key[...] = block(g.r_attn, 3)
    o.cross_value[...] = block(g.r_attn, 4)
    o.expand[...] = g.r_hidden[:, :hid]
    o.contract[...] = g.r_hidden[:, hid:]
    vectors = (
        o.final_gain,
        o.final_shift,
        o.contract_bias,
        o.cross_gain,
        o.cross_shift,
        o.cross_output_bias,
        o.attn_gain,
        o.attn_shift,
        o.self_output_bias,
        o.self_query_bias,
        o.self_value_bias,
        o.cross_query_bias,
        o.cross_value_bias,
    )
    for i, vector in enumerate(vectors):
        vector[...] = g.r_small[i : i + 1, :]
    at = len(vectors)
    for z in range(o.expand_bias.shape[1] // width):
        o.expand_bias[:, z * width : (z + 1) * width] = g.r_small[at + z : at + z + 1, :]


def per_device(
    tokens,
    encoded,
    source_len,
    out_grad,
    self_query,
    self_key,
    self_value,
    self_output,
    self_query_bias,
    self_value_bias,
    self_output_bias,
    cross_query,
    cross_key,
    cross_value,
    cross_output,
    cross_query_bias,
    cross_value_bias,
    cross_output_bias,
    expand,
    expand_bias,
    contract,
    contract_bias,
    attn_gain,
    attn_shift,
    cross_gain,
    cross_shift,
    final_gain,
    final_shift,
):
    inputs = dict(locals())
    names = tuple(inputs)
    turned = [v is source_len or v is self_output or v is cross_output or v is contract
              for v in inputs.values()]
    flat = [v.ndim == 1 for v in inputs.values()]
    row_count = lax.axis_size(ROW)
    cols = lax.axis_size(COL)
    micro_count, part, width = tokens.shape
    depth, head_width = self_query.shape
    hid = expand.shape[1]
    assert micro_count == 2 and cols == 4 and source_len.shape[1] == 1
    assert head_width == PAIR and row_count % 4 == 0 and hid == width
    own = 2 * part
    plane = row_count // 2
    small_rows = -(-(13 + cols) // 8) * 8
    row_steps = len(bits_of(row_count - 1))
    small_steps = row_steps + cols - 1
    links = 3 * (2 * (cols - 1) + (plane - 1) * cols + plane)
    links += 3 * (plane + 2 * (plane - 1) + 2 * (cols - 1) + 1) + 2 * plane * (cols - 1)
    links += 6 * 2 + 1 + 8 + 4 + 2 * small_steps + 1

    def whole(columns):
        return pltpu.VMEM((cols, row_count, depth, columns), BF16)

    def from_pair(columns):
        return pltpu.VMEM((plane, cols, depth, columns), BF16)

    def from_plane(columns):
        return pltpu.VMEM((2 * (plane - 1), cols // 2, depth, columns), BF16)

    def from_col(columns):
        return pltpu.VMEM((2 * (cols - 1), depth, columns), BF16)

    rows_low = pltpu.VMEM((own, width), BF16)
    rows_f32 = pltpu.VMEM((own, width), F32)
    stat_f32 = pltpu.VMEM((own, PAIR), F32)
    heads_low = pltpu.VMEM((cols, own, PAIR), BF16)
    heads_f32 = pltpu.VMEM((cols, own, PAIR), F32)
    keys_low = pltpu.VMEM((2, cols, 2 * own, PAIR), BF16)
    half_keys = pltpu.VMEM((2, cols, own, PAIR), BF16)
    lengths = pltpu.VMEM((2, 8, PAIR), jnp.int32)
    scratch = dict(
        x=rows_low,
        e=rows_low,
        og=rows_low,
        og_low=pltpu.VMEM((2, part, width), BF16),
        pack_self=pltpu.VMEM((depth, 3 * PAIR), BF16),
        pack_attn=pltpu.VMEM((depth, 5 * PAIR), BF16),
        pack_hidden=pltpu.VMEM((depth, 2 * hid), BF16),
        w_self=whole(3 * PAIR),
        w_attn=whole(5 * PAIR),
        w_hidden=whole(2 * hid),
        len_own=lengths,
        len_other=lengths,
        q=heads_low,
        kv=keys_low,
        ckv=keys_low,
        mixed=heads_low,
        lse=heads_f32,
        n1=rows_f32,
        i1=stat_f32,
        cq=heads_low,
        cmixed=heads_low,
        clse=heads_f32,
        n2=rows_f32,
        i2=stat_f32,
        grad=rows_f32,
        mixed_back=heads_low,
        dq=heads_low,
        result_low=rows_low,
        enc_low=rows_low,
        tok_low=rows_low,
        stage_cross=half_keys,
        arrive_cross=half_keys,
        stage_self=half_keys,
        arrive_self=half_keys,
        small=pltpu.VMEM((row_steps + 2, small_rows, width), F32),
        small_arrived=pltpu.VMEM((small_steps, small_rows, width), F32),
        late=pltpu.VMEM((row_steps + 2, 8, width), F32),
        late_arrived=pltpu.VMEM((small_steps, 8, width), F32),
        t_hidden=pltpu.VMEM((depth, 2 * hid), F32),
        t_attn=pltpu.VMEM((depth, 5 * PAIR), F32),
        t_self=pltpu.VMEM((depth, 3 * PAIR), F32),
        t_small=pltpu.VMEM((small_rows, width), F32),
        g_hidden=whole(2 * hid),
        p_hidden=from_pair(2 * hid),
        q_hidden=from_plane(2 * hid),
        c_hidden=from_col(2 * hid),
        g_attn=whole(5 * PAIR),
        p_attn=from_pair(5 * PAIR),
        q_attn=from_plane(5 * PAIR),
        c_attn=from_col(5 * PAIR),
        g_self=whole(3 * PAIR),
        p_self=from_pair(3 * PAIR),
        q_self=from_plane(3 * PAIR),
        c_self=from_col(3 * PAIR),
        send=pltpu.SemaphoreType.DMA((links,)),
        recv=pltpu.SemaphoreType.DMA((links,)),
    )
    home = jax.ShapeDtypeStruct((2, part, width), BF16)
    outs = dict(
        result_home=(home, ANY_SPEC),
        tok_home=(home, ANY_SPEC),
        enc_home=(home, ANY_SPEC),
        r_self=(jax.ShapeDtypeStruct((depth, 3 * PAIR), F32), ANY_SPEC),
        r_attn=(jax.ShapeDtypeStruct((depth, 5 * PAIR), F32), ANY_SPEC),
        r_hidden=(jax.ShapeDtypeStruct((depth, 2 * hid), F32), ANY_SPEC),
        r_small=(jax.ShapeDtypeStruct((small_rows, width), F32), ANY_SPEC),
    )
    specs = [ANY_SPEC, ANY_SPEC, SMEM_SPEC] + [VMEM_SPEC] * (len(names) - 3)
    values = [
        v.reshape(1, -1) if f else (v.T if t else v)
        for v, f, t in zip(inputs.values(), flat, turned)
    ]
    moved = pl.pallas_call(
        functools.partial(layer_kernel, row_count, cols, names + tuple(outs) + tuple(scratch)),
        out_shape=[shape for shape, _ in outs.values()],
        in_specs=specs,
        out_specs=[spec for _, spec in outs.values()],
        scratch_shapes=list(scratch.values()),
        compiler_params=pltpu.CompilerParams(
            collective_id=0, has_side_effects=True, vmem_limit_bytes=VMEM_LIMIT
        ),
        name="layer",
    )(*values)
    shapes = [(2, part, width)] * 3 + [v.shape for v in values[4:]]
    final = pl.pallas_call(
        functools.partial(finish_kernel, width, tuple(outs), names[4:]),
        out_shape=[jax.ShapeDtypeStruct(shape, F32) for shape in shapes],
        in_specs=[VMEM_SPEC] * len(outs),
        out_specs=[VMEM_SPEC] * len(shapes),
        compiler_params=pltpu.CompilerParams(vmem_limit_bytes=VMEM_LIMIT),
        name="finish",
    )(*moved)
    return tuple(final[:3]) + tuple(
        v.reshape(-1) if f else (v.T if t else v)
        for v, f, t in zip(final[3:], flat[4:], turned[4:])
    )


def solution(mesh):
    tokens, down, across, same = P(None, AXES, None), P(ROW, COL), P(COL, ROW), P()
    attention = (down, down, down, across, same, same, same)
    weights = attention * 2 + (down, same, across) + (same,) * 7
    return jax.shard_map(
        per_device,
        mesh=mesh,
        in_specs=(tokens, tokens, P(None, ROW), tokens) + weights,
        out_specs=(tokens, tokens, tokens) + weights,
        check_vma=False,
    )
```

```python
import functools

import jax
import jax.numpy as jnp
from jax import lax
from jax.experimental import pallas as pl
from jax.experimental.pallas import tpu as pltpu
from jax.sharding import PartitionSpec as P

HEAD_DIM = 64
PAIR = 2 * HEAD_DIM
NEGATIVE = -1e30
EPSILON = 1e-05
ROW, COL = "row", "col"
AXES = (ROW, COL)
MESH = pl.DeviceIdType.MESH
F32 = jnp.float32
BF16 = jnp.bfloat16
VMEM_SPEC = pl.BlockSpec(memory_space=pltpu.VMEM)
SMEM_SPEC = pl.BlockSpec(memory_space=pltpu.SMEM)
ANY_SPEC = pl.BlockSpec(memory_space=pl.ANY)
VMEM_LIMIT = 67_043_328


def dot_nn(a, b):
    return lax.dot_general(a, b, (((1,), (0,)), ((), ())), preferred_element_type=F32)


def dot_nt(a, b):
    return lax.dot_general(a, b, (((1,), (1,)), ((), ())), preferred_element_type=F32)


def dot_tn(a, b):
    return lax.dot_general(a, b, (((0,), (0,)), ((), ())), preferred_element_type=F32)


def norm_forward(values):
    average = jnp.mean(values, axis=1, keepdims=True)
    centered = values - average
    inverse = lax.rsqrt(jnp.mean(centered * centered, axis=1, keepdims=True) + EPSILON)
    return centered * inverse, inverse


def norm_backward(gradient, normed, inverse, gain):
    scaled = gradient * gain
    mean_scaled = jnp.mean(scaled, axis=1, keepdims=True)
    mean_product = jnp.mean(scaled * normed, axis=1, keepdims=True)
    return (scaled - mean_scaled - normed * mean_product) * inverse


def column_sum(values):
    return jnp.sum(values, axis=0, keepdims=True)


def spread_lanes(column, width):
    return jnp.broadcast_to(column, (column.shape[0], width))


def lane_masks():
    lane = lax.broadcasted_iota(jnp.int32, (1, PAIR), 1)
    first = (lane < HEAD_DIM).astype(F32)
    return first, (1.0 - first)


def attend_block(q_ref, kv_ref, out_ref, lse_ref, row0, rows, span, mask, pairs):
    first, second = lane_masks()
    halves = (first.astype(BF16), second.astype(BF16))

    def one_pair(z, carry):
        q_pair = q_ref[z, pl.ds(row0, rows), :]
        k_pair = kv_ref[0, z, pl.ds(0, span), :]
        v_pair = kv_ref[1, z, pl.ds(0, span), :]
        outs, stats = [], []
        for half in halves:
            scores = mask(dot_nt(q_pair * half, k_pair))
            row_max = jnp.max(scores, axis=1, keepdims=True)
            raised = jnp.exp(scores - row_max)
            summed = jnp.sum(raised, axis=1, keepdims=True)
            probs = (raised * (1.0 / summed)).astype(BF16)
            outs.append(dot_nn(probs, v_pair))
            stats.append(row_max + jnp.log(summed))
        out_ref[z, pl.ds(row0, rows), :] = (outs[0] * first + outs[1] * second).astype(BF16)
        lse_ref[z, pl.ds(row0, rows), :] = (
            spread_lanes(stats[0], PAIR) * first + spread_lanes(stats[1], PAIR) * second
        )
        return carry

    lax.fori_loop(pairs[0], pairs[1], one_pair, 0)


def attend_block_back(
    q_ref,
    kv_ref,
    mixed_ref,
    lse_ref,
    grad_ref,
    dq_ref,
    dkv_ref,
    row0,
    rows,
    span,
    chunk,
    mask,
    pairs,
):
    first, second = lane_masks()
    halves = (first.astype(BF16), second.astype(BF16))

    def one_pair(z, carry):
        q_pair = q_ref[z, pl.ds(row0, rows), :]
        g_pair = grad_ref[z, pl.ds(row0, rows), :]
        stats = jnp.transpose(lse_ref[z, pl.ds(row0, rows), :])
        products = jnp.transpose(
            g_pair.astype(F32) * mixed_ref[z, pl.ds(row0, rows), :].astype(F32)
        )
        lse_rows = (stats[0:1, :], stats[HEAD_DIM : HEAD_DIM + 1, :])
        deltas = (column_sum(products[:HEAD_DIM, :]), column_sum(products[HEAD_DIM:, :]))
        q_half = [q_pair * half for half in halves]
        g_half = [g_pair * half for half in halves]
        dq = [jnp.zeros((rows, PAIR), F32), jnp.zeros((rows, PAIR), F32)]
        for at in range(0, span, chunk):
            k_part = kv_ref[0, z, pl.ds(at, chunk), :]
            v_part = kv_ref[1, z, pl.ds(at, chunk), :]
            dk = jnp.zeros((chunk, PAIR), F32)
            dv = jnp.zeros((chunk, PAIR), F32)
            for h in range(2):
                scores = mask(dot_nt(k_part, q_half[h]), at)
                probs = jnp.exp(scores - lse_rows[h])
                prob_grads = dot_nt(v_part, g_half[h])
                score_low = (probs * (prob_grads - deltas[h])).astype(BF16)
                dv = dv + dot_nn(probs.astype(BF16), g_half[h])
                dk = dk + dot_nn(score_low, q_half[h])
                dq[h] = dq[h] + dot_tn(score_low, k_part)
            dkv_ref[0, z, pl.ds(at, chunk), :] += dk
            dkv_ref[1, z, pl.ds(at, chunk), :] += dv
        dq_ref[z, pl.ds(row0, rows), :] = (dq[0] * first + dq[1] * second).astype(
            BF16
        ) * jnp.asarray(HEAD_DIM**-0.5, BF16)
        return carry

    lax.fori_loop(pairs[0], pairs[1], one_pair, 0)


def causal_last(rows, span):
    def mask(scores):
        query = lax.broadcasted_iota(jnp.int32, scores.shape, 0) + (span - rows)
        key = lax.broadcasted_iota(jnp.int32, scores.shape, 1)
        return jnp.where(key <= query, scores, NEGATIVE)

    return mask


def causal_last_back(rows, span):
    def mask(scores, at):
        if at + scores.shape[0] <= span - rows:
            return scores
        key = lax.broadcasted_iota(jnp.int32, scores.shape, 0) + at
        query = lax.broadcasted_iota(jnp.int32, scores.shape, 1) + (span - rows)
        return jnp.where(key <= query, scores, NEGATIVE)

    return mask


class Refs:
    pass


def named(names, refs):
    out = Refs()
    out.__dict__.update(zip(names, refs))
    return out


def flipped(index, bits):
    for bit in bits:
        index = index + bit - 2 * bit * ((index // bit) % 2)
    return index


def bits_of(number):
    return [1 << i for i in range(number.bit_length()) if (number >> i) & 1]


def subsets(bits):
    out = [0]
    for bit in bits:
        out = out + [m + bit for m in out]
    return out


class Links:
    def __init__(self, send, recv):
        self.send, self.recv, self.count = send, recv, 0

    def take(self, amount=1):
        at = self.count
        self.count += amount
        return at

    def copy(self, src, dst, device, send_at, recv_at):
        return pltpu.make_async_remote_copy(
            src_ref=src,
            dst_ref=dst,
            send_sem=self.send.at[send_at],
            recv_sem=self.recv.at[recv_at],
            device_id=device,
            device_id_type=MESH,
        )


class Place:
    def __init__(self, row_count, col_count):
        self.rows, self.cols = row_count, col_count
        self.row, self.col = lax.axis_index(ROW), lax.axis_index(COL)
        self.core = self.row % 2
        self.row_bits = bits_of(row_count - 1)
        self.plane_bits = self.row_bits[1:]
        self.half = col_count // 2
        self.members = subsets(self.plane_bits)
        self.sides = ((0, self.plane_bits), (self.half, self.plane_bits[::-1]))
        self.partner = (flipped(self.row, [1]), self.col)
        self.pair_row = (self.row // 2) * 2

    def greet(self):
        barrier = pltpu.get_barrier_semaphore()
        count = 0
        for side in range(2):
            for k in range(self.cols):
                if side + k:
                    device = (
                        flipped(self.row, [1] if side else []),
                        flipped(self.col, bits_of(k)),
                    )
                    pl.semaphore_signal(barrier, inc=1, device_id=device, device_id_type=MESH)
                    count += 1
        for bit in self.plane_bits:
            device = (flipped(self.row, [bit]), self.col)
            pl.semaphore_signal(barrier, inc=1, device_id=device, device_id_type=MESH)
            count += 1
        pl.semaphore_wait(barrier, count)


class Inbound:
    def __init__(self, place, links, source, target):
        self.place, self.links, self.source, self.target = place, links, source, target
        self.part = source.shape[1]
        self.send_at = links.take(2)
        self.recv_at = self.send_at

    def copies(self):
        p = self.place
        slot = p.col // 2
        to_row = p.pair_row + ((p.col + 1) // 2) % 2
        into = self.target.at[pl.ds(pl.multiple_of(slot * self.part, self.part), self.part)]
        out = []
        for b in range(2):
            device = (to_row, 2 * b + p.core)
            out.append(
                self.links.copy(
                    self.source.at[b], into, device, self.send_at + b, self.recv_at + slot
                )
            )
        local = pltpu.make_async_copy(self.source.at[0], into, self.links.recv.at[self.recv_at])
        return out, local

    def stays(self):
        return self.place.col == self.place.core

    def start(self):
        out, local = self.copies()
        out[1].start()

        @pl.when(self.stays())
        def _():
            local.start()

        @pl.when(jnp.logical_not(self.stays()))
        def _():
            out[0].start()

    def arrive(self):
        p = self.place
        for slot in range(2):
            into = self.target.at[pl.ds(slot * self.part, self.part)]
            remote = self.links.copy(
                self.source.at[0], into, p.partner, self.send_at, self.recv_at + slot
            )
            if slot:
                remote.wait_recv()
            else:
                local = pltpu.make_async_copy(
                    self.source.at[0], into, self.links.recv.at[self.recv_at]
                )

                @pl.when(self.stays())
                def _():
                    local.wait()

                @pl.when(jnp.logical_not(self.stays()))
                def _():
                    remote.wait_recv()

    def drain(self):
        out, _ = self.copies()
        out[1].wait_send()

        @pl.when(jnp.logical_not(self.stays()))
        def _():
            out[0].wait_send()


class Outbound:
    def __init__(self, place, links, source, target):
        self.place, self.links, self.source, self.target = place, links, source, target
        self.part = target.shape[1]
        self.send_at = links.take(2)
        self.recv_at = self.send_at

    def copies(self):
        p = self.place
        micro = p.col // 2
        to_row = p.pair_row + p.col % 2
        out = []
        for i, to_col in enumerate((p.core, 3 - p.core)):
            out.append(
                self.links.copy(
                    self.source.at[pl.ds(i * self.part, self.part)],
                    self.target.at[micro],
                    (to_row, to_col),
                    self.send_at + i,
                    self.recv_at + micro,
                )
            )
        local = pltpu.make_async_copy(
            self.source.at[pl.ds(0, self.part)],
            self.target.at[0],
            self.links.recv.at[self.recv_at],
        )
        return out, local

    def stays(self):
        return self.place.col == self.place.core

    def start(self):
        out, local = self.copies()
        out[1].start()

        @pl.when(self.stays())
        def _():
            local.start()

        @pl.when(jnp.logical_not(self.stays()))
        def _():
            out[0].start()

    def arrive(self):
        p = self.place
        for micro in range(2):
            remote = self.links.copy(
                self.source.at[pl.ds(0, self.part)],
                self.target.at[micro],
                p.partner,
                self.send_at,
                self.recv_at + micro,
            )
            if micro:
                remote.wait_recv()
            else:
                _, local = self.copies()

                @pl.when(self.stays())
                def _():
                    local.wait()

                @pl.when(jnp.logical_not(self.stays()))
                def _():
                    remote.wait_recv()

    def drain(self):
        out, _ = self.copies()
        out[1].wait_send()

        @pl.when(jnp.logical_not(self.stays()))
        def _():
            out[0].wait_send()


class Gather:
    def __init__(self, place, links, shard, whole, relayed):
        self.place, self.links, self.shard, self.whole = place, links, shard, whole
        self.relayed = relayed
        self.along_at = links.take(2 * (place.cols - 1))
        self.base = {}
        for m in place.members:
            if m:
                self.base[(False, m)] = links.take(place.cols)
            self.base[(True, m)] = links.take()
        self.orders = (place.plane_bits, place.plane_bits[::-1])
        whole[place.col, place.row] = shard[...]

    def sources(self, step):
        p = self.place
        if step == 0:
            return [(p.col, None, 0)]
        if not self.relayed:
            return [(flipped(p.col, bits_of(step)), None, 0)]
        return [
            (p.col - step, p.col >= step, 1),
            (p.col + step, p.col + step < p.cols, -1),
        ]

    def guarded(self, valid, action):
        if valid is None:
            action()
        else:
            pl.when(valid)(action)

    def hop(self, step, column, direction):
        p = self.place
        block = self.whole.at[column, p.row]
        if not self.relayed:
            at = self.along_at + step - 1
            return self.links.copy(block, block, (p.row, flipped(p.col, bits_of(step))), at, at)
        at = self.along_at + 2 * (step - 1) + (0 if direction > 0 else 1)
        return self.links.copy(block, block, (p.row, p.col + direction), at, at)

    def forward(self, step, column, direction, act):
        p = self.place
        if not self.relayed:
            for far in range(1, p.cols if step == 0 else 0):
                act(self.hop(far, column, 0))
            return
        if step + 1 >= p.cols:
            return
        for way in (1, -1) if step == 0 else (direction,):
            room = p.col + 1 < p.cols if way > 0 else p.col > 0

            @pl.when(room)
            def _(way=way):
                act(self.hop(step + 1, column, way))

    def plane_copy(self, column, m, bit):
        p = self.place
        block = self.whole.at[column, flipped(p.row, bits_of(m))]
        at = self.base[(False, m + bit)] + column
        return self.links.copy(block, block, (flipped(p.row, [bit]), p.col), at, at)

    def pair_copy(self, m):
        p = self.place
        block = self.whole.at[:, flipped(p.row, bits_of(m))]
        at = self.base[(True, m)]
        return self.links.copy(block, block, p.partner, at, at)

    def to_pair(self, level):
        for m in self.place.members:
            if len(bits_of(m)) == level:
                self.pair_copy(m).start()

    def outgoing(self, step, column, m):
        order = self.orders[step % 2]
        reached = max([order.index(b) for b in bits_of(m)], default=-1)
        return [self.plane_copy(column, m, bit) for bit in order[reached + 1 :]]

    def start(self):
        p = self.place
        self.forward(0, p.col, 0, lambda c: c.start())

    def start_plane(self):
        for copy in self.outgoing(0, self.place.col, 0):
            copy.start()

    def step(self, step):
        for column, valid, direction in self.sources(step):

            def action(column=column, direction=direction):
                self.hop(step, column, direction).wait_recv()
                self.forward(step, column, direction, lambda c: c.start())
                for copy in self.outgoing(step, column, 0):
                    copy.start()

            self.guarded(valid, action)

    def arrived(self, column, m, order):
        bit = max(bits_of(m), key=order.index)
        return self.plane_copy(column, m - bit, bit)

    def plane(self, step, level):
        order = self.orders[step % 2]
        for column, valid, _ in self.sources(step):

            def action(column=column):
                for m in self.place.members:
                    if len(bits_of(m)) == level:
                        self.arrived(column, m, order).wait_recv()
                        for copy in self.outgoing(step, column, m):
                            copy.start()

            self.guarded(valid, action)

    def planes_from(self, step, first):
        for level in range(first, len(self.place.plane_bits) + 1):
            self.plane(step, level)

    def each(self, visit):
        p = self.place
        for step in range(p.cols):
            for column, valid, direction in self.sources(step):
                self.guarded(
                    valid, functools.partial(visit, step=step, column=column, direction=direction)
                )

    def finish(self):
        for m in self.place.members:
            self.pair_copy(m).wait_recv()

    def drain(self):
        for m in self.place.members:
            self.pair_copy(m).wait_send()

        def visit(step, column, direction):
            self.forward(step, column, direction, lambda c: c.wait_send())
            for m in self.place.members:
                for copy in self.outgoing(step, column, m):
                    copy.wait_send()

        self.each(visit)


class Reduce:
    def __init__(self, place, links, grads, from_pair, from_plane, from_col, total, out, relayed):
        self.place, self.links, self.grads = place, links, grads
        self.relayed = relayed
        self.sums, self.from_plane, self.from_col = from_pair, from_plane, from_col
        self.total, self.out = total, out
        self.moves = []
        for side_at, (_, order) in enumerate(place.sides):
            for level in range(len(order)):
                for m in subsets(order[level + 1 :]):
                    self.moves.append((side_at, level, m))
        self.pair_at = links.take(len(place.members) * (place.cols if relayed else 1))
        self.plane_at = links.take(len(self.moves))
        self.along_at = links.take(2 * (place.cols - 1))
        self.out_at = links.take()

    def pair_copy(self, at, m, column=None):
        p = self.place
        if column is not None:
            sem = self.pair_at + at * p.cols + column
            return self.links.copy(
                self.grads.at[column, flipped(p.row, [1] + bits_of(m))],
                self.sums.at[at, column],
                p.partner,
                sem,
                sem,
            )
        return self.links.copy(
            self.grads.at[:, flipped(p.row, [1] + bits_of(m))],
            self.sums.at[at],
            p.partner,
            self.pair_at + at,
            self.pair_at + at,
        )

    def pair_copies(self, at, m):
        if self.relayed:
            return [self.pair_copy(at, m, column) for column in range(self.place.cols)]
        return [self.pair_copy(at, m)]

    def start(self):
        for at, m in enumerate(self.place.members):
            self.pair_copy(at, m).start()

    def start_column(self, column):
        for at, m in enumerate(self.place.members):
            self.pair_copy(at, m, column).start()

    def after_pair(self):
        p = self.place
        for at, m in enumerate(p.members):
            for copy in self.pair_copies(at, m):
                copy.wait_recv()
            own_row = flipped(p.row, bits_of(m))

            def body(i, carry, at=at, own_row=own_row):
                self.sums[at, i] = (
                    self.grads[i, own_row].astype(F32) + self.sums[at, i].astype(F32)
                ).astype(BF16)
                return carry

            lax.fori_loop(0, p.cols, body, 0)
        self.send(0)

    def plane_copy(self, at):
        p = self.place
        side_at, level, m = self.moves[at]
        side, order = p.sides[side_at]
        bit = order[level]
        return self.links.copy(
            self.sums.at[p.members.index(m + bit), pl.ds(side, p.half)],
            self.from_plane.at[at],
            (flipped(p.row, [bit]), p.col),
            self.plane_at + at,
            self.plane_at + at,
        )

    def at_level(self, level):
        return [at for at, move in enumerate(self.moves) if move[1] == level]

    def send(self, level):
        for at in self.at_level(level):
            self.plane_copy(at).start()

    def after_plane(self, level):
        p = self.place
        for at in self.at_level(level):
            side_at, _, m = self.moves[at]
            self.plane_copy(at).wait_recv()
            into, side = p.members.index(m), p.sides[side_at][0]

            def body(i, carry, into=into, at=at, side=side):
                self.sums[into, side + i] = (
                    self.sums[into, side + i].astype(F32) + self.from_plane[at, i].astype(F32)
                ).astype(BF16)
                return carry

            lax.fori_loop(0, p.half, body, 0)
        if level + 1 < len(p.plane_bits):
            self.send(level + 1)
        else:
            for step in range(1, 2 if self.relayed else p.cols):
                self.hops(step, lambda c: c.start())

    def hop(self, step, way, column):
        p = self.place
        if not self.relayed:
            at = self.along_at + step - 1
            return self.links.copy(
                self.sums.at[0, column], self.from_col.at[step - 1], (p.row, column), at, at
            )
        slot = 2 * (step - 1) + (0 if way > 0 else 1)
        at = self.along_at + slot
        return self.links.copy(
            self.sums.at[0, column], self.from_col.at[slot], (p.row, p.col + way), at, at
        )

    def hops(self, step, act):
        p = self.place
        if not self.relayed:
            act(self.hop(step, 0, flipped(p.col, bits_of(step))))
            return
        for way in (1, -1):
            here = p.col if way > 0 else p.cols - 1 - p.col
            column = p.cols + p.col - step if way > 0 else p.col - p.cols + step
            inner = p.col + 1 < p.cols if way > 0 else p.col > 0

            @pl.when(jnp.logical_and(here < step, inner))
            def _(way=way, column=column, step=step):
                act(self.hop(step, way, column))

    def step(self, step):
        p = self.place
        for way in (1, -1):
            here = p.col if way > 0 else p.cols - 1 - p.col
            column = p.cols + p.col - 1 - step if way > 0 else p.col - p.cols + 1 + step
            slot = 2 * (step - 1) + (0 if way > 0 else 1)

            @pl.when(jnp.logical_and(here >= 1, here <= step))
            def _(way=way, column=column, slot=slot):
                self.hop(step, way, column).wait_recv()
                self.sums[0, column] = (
                    self.sums[0, column].astype(F32) + self.from_col[slot].astype(F32)
                ).astype(BF16)

        if step + 1 < p.cols:
            self.hops(step + 1, lambda c: c.start())

    def out_copy(self):
        return pltpu.make_async_copy(self.total, self.out, self.links.recv.at[self.out_at])

    def finish(self, done=0):
        p = self.place
        last = p.cols - 1
        if not self.relayed:
            total = self.sums[0, p.col].astype(F32)
            for step in range(1, p.cols):
                self.hop(step, 0, flipped(p.col, bits_of(step))).wait_recv()
                total = total + self.from_col[step - 1].astype(F32)
            self.total[...] = total
        else:
            for step in range(done + 1, last):
                self.step(step)
            self.total[...] = self.sums[0, p.col].astype(F32)
            for way in (1, -1):
                here = p.col if way > 0 else p.cols - 1 - p.col
                slot = 2 * (last - 1) + (0 if way > 0 else 1)

                @pl.when(here >= 1)
                def _(way=way, slot=slot):
                    self.hop(last, way, p.col).wait_recv()
                    self.total[...] += self.from_col[slot].astype(F32)

        self.out_copy().start()

    def drain(self):
        for at, m in enumerate(self.place.members):
            for copy in self.pair_copies(at, m):
                copy.wait_send()
        for at in range(len(self.moves)):
            self.plane_copy(at).wait_send()
        for step in range(1, self.place.cols):
            self.hops(step, lambda c: c.wait_send())
        self.out_copy().wait()


class Swap:
    def __init__(self, place, links, pieces):
        self.place, self.links, self.pieces = place, links, pieces
        self.at = links.take(len(pieces))

    def each(self, act):
        for i, (source, target) in enumerate(self.pieces):
            at = self.at + i
            act(self.links.copy(source, target, self.place.partner, at, at))

    def start(self):
        self.each(lambda c: c.start())

    def arrive(self):
        self.each(lambda c: c.wait_recv())

    def drain(self):
        self.each(lambda c: c.wait_send())


class Total:
    def __init__(self, place, links, sums, arrived, col_first):
        self.place, self.links, self.sums, self.arrived = place, links, sums, arrived
        self.col_at = links.take(place.cols - 1)
        self.row_at = links.take(len(place.row_bits))
        self.steps = len(place.row_bits) + 1
        self.col_step = 0 if col_first else self.steps - 1

    def copies(self, i):
        p = self.place
        if i == self.col_step:
            out = []
            for k in range(1, p.cols):
                at = self.col_at + k - 1
                device = (p.row, flipped(p.col, bits_of(k)))
                into = self.arrived.at[self.steps - 2 + k]
                out.append(self.links.copy(self.sums.at[i], into, device, at, at))
            return out
        bit = i - 1 if self.col_step == 0 else i
        at = self.row_at + bit
        device = (flipped(p.row, [p.row_bits[bit]]), p.col)
        return [self.links.copy(self.sums.at[i], self.arrived.at[bit], device, at, at)]

    def start(self, i=0):
        for copy in self.copies(i):
            copy.start()

    def step(self, i):
        p = self.place
        for copy in self.copies(i):
            copy.wait_recv()
        if i == self.col_step:
            total = None
            for c in range(p.cols):
                term = jnp.where(p.col == c, self.sums[i], 0.0)
                for k in range(1, p.cols):
                    here = flipped(p.col, bits_of(k)) == c
                    term = jnp.where(here, self.arrived[self.steps - 2 + k], term)
                total = term if total is None else total + term
        else:
            total = self.sums[i] + self.arrived[i - 1 if self.col_step == 0 else i]
        self.sums[i + 1] = total
        if i + 1 < self.steps:
            self.start(i + 1)

    def result(self):
        return self.sums[self.steps]

    def drain(self):
        for i in range(self.steps):
            for copy in self.copies(i):
                copy.wait_send()


def flat_rows(value):
    count, depth, width = value.shape
    if depth % 16 or value.dtype == F32:
        return value.astype(F32).reshape(count * depth, width).astype(value.dtype)
    return value.reshape(count * depth, width)


def row_blocks(value, count):
    return value.reshape(count, value.shape[0] // count, value.shape[1]).astype(BF16)


def layer_kernel(row_count, col_count, names, *refs):
    g = named(names, refs)
    p = Place(row_count, col_count)
    links = Links(g.send, g.recv)
    part = g.tokens.shape[1]
    width = g.tokens.shape[2]
    hid = g.expand.shape[1]
    cols = col_count
    own = 2 * part
    span = 4 * part
    scale = HEAD_DIM**-0.5
    low_at = pl.multiple_of(p.core * part, part)
    high_at = pl.multiple_of((3 - p.core) * part, part)
    other_low = pl.multiple_of((1 - p.core) * part, part)
    other_high = pl.multiple_of((2 + p.core) * part, part)

    def self_w(z, lo=0, hi=3):
        return flat_rows(g.w_self[z, :, :, lo * PAIR : hi * PAIR])

    def attn_w(z, at, count=1):
        return flat_rows(g.w_attn[z, :, :, at * PAIR : (at + count) * PAIR])

    def heads_of(vector, z):
        return vector[:, z * PAIR : (z + 1) * PAIR]

    p.greet()
    x_in = Inbound(p, links, g.tokens, g.x)
    e_in = Inbound(p, links, g.encoded, g.e)
    og_in = Inbound(p, links, g.og_low, g.og)
    g.pack_self[:, 0:PAIR] = g.self_query[...]
    g.pack_self[:, PAIR : 2 * PAIR] = g.self_key[...]
    g.pack_self[:, 2 * PAIR :] = g.self_value[...]
    get_self = Gather(p, links, g.pack_self, g.w_self, False)
    get_self.start()
    get_self.start_plane()
    for i, shard in enumerate(
        (g.self_output, g.cross_query, g.cross_key, g.cross_value, g.cross_output)
    ):
        g.pack_attn[:, i * PAIR : (i + 1) * PAIR] = shard[...]
    get_attn = Gather(p, links, g.pack_attn, g.w_attn, False)
    g.pack_hidden[:, 0:hid] = g.expand[...]
    g.pack_hidden[:, hid:] = g.contract[...]
    get_hidden = Gather(p, links, g.pack_hidden, g.w_hidden, True)
    for m in range(2):
        g.len_own[m] = jnp.full(g.len_own.shape[1:], g.source_len[0, m], jnp.int32)
    len_swap = Swap(p, links, [(g.len_own, g.len_other)])
    len_swap.start()
    levels = range(2, len(p.plane_bits) + 1)
    get_self.step(1)
    x_in.start()
    get_self.plane(0, 1)
    get_self.step(2)
    get_self.plane(1, 1)
    get_self.step(3)
    get_self.to_pair(0)
    get_self.plane(2, 1)
    get_self.plane(3, 1)
    get_self.to_pair(1)
    get_attn.start_plane()
    g.og_low[...] = g.out_grad[...].astype(BF16)
    for level in levels:
        for step in range(cols):
            get_self.plane(step, level)
        get_self.to_pair(level)
    get_attn.start()
    get_hidden.start()
    get_self.finish()
    x_in.arrive()
    e_in.start()

    def key_swap(ref, pairs):
        pieces = []
        for at in (low_at, high_at):
            piece = ref.at[:, pl.ds(pairs[0], pairs[1] - pairs[0]), pl.ds(at, part), :]
            pieces.append((piece, piece))
        return Swap(p, links, pieces)

    def keep_keys(ref, z, k_rows, v_rows):
        for i, value in enumerate((k_rows, v_rows)):
            ref[i, z, pl.ds(low_at, part), :] = value[:part].astype(BF16)
            ref[i, z, pl.ds(high_at, part), :] = value[part:].astype(BF16)

    ranges = ((0, cols // 2), (cols // 2, cols))
    half = cols // 2
    kv_swaps = [key_swap(g.kv, pairs) for pairs in ranges]
    ckv_swaps = [key_swap(g.ckv, pairs) for pairs in ranges]
    x = g.x[...]
    for pairs, swap in zip(ranges, kv_swaps):
        for z in range(*pairs):
            rows = dot_nn(x, self_w(z))
            g.q[z] = ((rows[:, 0:PAIR] + heads_of(g.self_query_bias, z)) * scale).astype(BF16)
            keep_keys(
                g.kv,
                z,
                rows[:, PAIR : 2 * PAIR],
                rows[:, 2 * PAIR :] + heads_of(g.self_value_bias, z),
            )
        swap.start()

    def in_segments(work, breaks):
        def segment(at, carry):
            block, first = at % 2, (at // 2) * half
            for i, (before, _) in enumerate(breaks):
                if before is not None:
                    pl.when(at == i)(before)
            work(block, (first, first + half))
            for i, (_, after) in enumerate(breaks):
                if after is not None:
                    pl.when(at == i)(after)
            return carry

        lax.fori_loop(0, 4, segment, 0)

    def causal_blocks(block, run):
        for later in range(2):
            for parity in range(2):
                keys = (4 - parity if later else parity + 1) * part

                @pl.when(jnp.logical_and(block == later, p.core == parity))
                def _(later=later, keys=keys):
                    run(later * part, keys)

    def self_block(block, pairs):
        causal_blocks(
            block,
            lambda row0, keys: attend_block(
                g.q, g.kv, g.mixed, g.lse, row0, part, keys, causal_last(part, keys), pairs
            ),
        )

    def after_self_0():
        get_attn.step(1)
        get_attn.plane(0, 1)

    def after_self_1():
        get_attn.step(2)
        get_attn.step(3)
        get_attn.to_pair(0)
        get_attn.plane(1, 1)
        for level in levels:
            get_attn.plane(0, level)
        kv_swaps[1].arrive()

    def after_self_2():
        get_attn.plane(2, 1)
        get_attn.plane(3, 1)
        get_attn.to_pair(1)
        for level in levels:
            get_attn.plane(1, level)
        get_hidden.step(1)
        get_hidden.start_plane()

    in_segments(
        self_block,
        (
            (kv_swaps[0].arrive, after_self_0),
            (None, after_self_1),
            (None, after_self_2),
            (None, None),
        ),
    )
    for level in levels:
        for step in range(2, cols):
            get_attn.plane(step, level)
        get_attn.to_pair(level)
    get_hidden.step(2)
    get_attn.finish()
    branch = g.self_output_bias[...] + g.x[...].astype(F32)
    for z in range(cols):
        branch = branch + dot_nt(g.mixed[z], attn_w(z, 0))
    normed, inverse = norm_forward(branch)
    g.n1[...] = normed
    g.i1[...] = spread_lanes(inverse, PAIR)
    first_low = (normed * g.attn_gain[...] + g.attn_shift[...]).astype(BF16)
    for z in range(cols):
        g.cq[z] = (
            (dot_nn(first_low, attn_w(z, 1)) + heads_of(g.cross_query_bias, z)) * scale
        ).astype(BF16)
    e_in.arrive()
    len_swap.arrive()
    e = g.e[...]
    for pairs, swap in zip(ranges, ckv_swaps):
        for z in range(*pairs):
            rows = dot_nn(e, attn_w(z, 2, 2))
            keep_keys(
                g.ckv, z, rows[:, :PAIR], rows[:, PAIR:] + heads_of(g.cross_value_bias, z)
            )
        swap.start()
    get_hidden.plane(0, 1)
    get_hidden.plane(1, 1)

    mine = p.col % 2 == p.core
    first_micro = p.col // 2 == 0
    own_len = jnp.where(first_micro, g.len_own[0, 0:1, 0:1], g.len_own[1, 0:1, 0:1])
    other_len = jnp.where(first_micro, g.len_other[0, 0:1, 0:1], g.len_other[1, 0:1, 0:1])
    limit = jnp.where(mine, own_len, other_len)

    def source_mask(scores):
        key = lax.broadcasted_iota(jnp.int32, scores.shape, 1)
        return jnp.where(key < limit, scores, NEGATIVE)

    def source_mask_back(scores, at):
        key = lax.broadcasted_iota(jnp.int32, scores.shape, 0) + at
        return jnp.where(key < limit, scores, NEGATIVE)

    def cross_block(block, pairs):
        row0 = pl.multiple_of(block * part, part)
        attend_block(g.cq, g.ckv, g.cmixed, g.clse, row0, part, span, source_mask, pairs)

    def after_cross_0():
        get_hidden.step(3)
        get_hidden.to_pair(0)
        get_hidden.planes_from(0, 2)
        og_in.start()

    def after_cross_1():
        get_hidden.plane(2, 1)
        get_hidden.planes_from(1, 2)
        ckv_swaps[1].arrive()

    def after_cross_2():
        get_hidden.plane(3, 1)
        get_hidden.to_pair(1)
        get_hidden.planes_from(2, 2)

    in_segments(
        cross_block,
        (
            (ckv_swaps[0].arrive, after_cross_0),
            (None, after_cross_1),
            (None, after_cross_2),
            (None, None),
        ),
    )
    get_hidden.planes_from(3, 2)
    for level in levels:
        get_hidden.to_pair(level)
    branch = g.n1[...] * g.attn_gain[...] + g.attn_shift[...] + g.cross_output_bias[...]
    for z in range(cols):
        branch = branch + dot_nt(g.cmixed[z], attn_w(z, 4))
    normed, inverse = norm_forward(branch)
    g.n2[...] = normed
    g.i2[...] = spread_lanes(inverse, PAIR)
    get_hidden.finish()
    og_in.arrive()

    result_out = Outbound(p, links, g.result_low, g.result_home)
    put_hidden = Reduce(
        p, links, g.g_hidden, g.p_hidden, g.q_hidden, g.c_hidden, g.t_hidden, g.r_hidden, True
    )

    def hidden_stage(inner_ref, hidden_ref, low_ref, total_ref):
        second = g.n2[...] * g.cross_gain[...] + g.cross_shift[...]
        low_ref[...] = second.astype(BF16)
        total_ref[...] = second + g.contract_bias[...]

        def forward(z, carry):
            bias = g.expand_bias[:, pl.ds(pl.multiple_of(z * hid, PAIR), hid)]
            inner = dot_nn(low_ref[...], flat_rows(g.w_hidden[z, :, :, :hid])) + bias
            inner_ref[z] = inner
            hidden = (inner * jax.nn.sigmoid(inner)).astype(BF16)
            hidden_ref[z] = hidden
            total_ref[...] += dot_nt(hidden, flat_rows(g.w_hidden[z, :, :, hid:]))
            return carry

        lax.fori_loop(0, cols, forward, 0)
        normed, inverse = norm_forward(total_ref[...])
        g.result_low[...] = (normed * g.final_gain[...] + g.final_shift[...]).astype(BF16)
        result_out.start()
        gradient = g.og[...].astype(F32)
        g.small[0, 0:1, :] = column_sum(gradient * normed)
        g.small[0, 1:2, :] = column_sum(gradient)
        third = norm_backward(gradient, normed, inverse, g.final_gain[...])
        g.small[0, 2:3, :] = column_sum(third)
        third_low = third.astype(BF16)
        total_ref[...] = third

        def backward(z, carry):
            inner = inner_ref[z]
            hidden_back = dot_nn(third_low, flat_rows(g.w_hidden[z, :, :, hid:]))
            g.g_hidden[z, :, :, hid:] = row_blocks(dot_tn(third_low, hidden_ref[z]), row_count)
            logistic = jax.nn.sigmoid(inner)
            inner_back = (hidden_back * logistic * (1.0 + inner * (1.0 - logistic))).astype(BF16)
            g.small[0, pl.ds(13 + z, 1), :] = column_sum(inner_back.astype(F32))
            g.g_hidden[z, :, :, :hid] = row_blocks(dot_tn(low_ref[...], inner_back), row_count)
            put_hidden.start_column(z)
            total_ref[...] += dot_nt(inner_back, flat_rows(g.w_hidden[z, :, :, :hid]))
            return carry

        lax.fori_loop(0, cols, backward, 0)
        gradient = total_ref[...]
        normed = g.n2[...]
        g.small[0, 3:4, :] = column_sum(gradient * normed)
        g.small[0, 4:5, :] = column_sum(gradient)
        second_grad = norm_backward(gradient, normed, g.i2[:, 0:1], g.cross_gain[...])
        g.small[0, 5:6, :] = column_sum(second_grad)
        g.grad[...] = second_grad

    pl.run_scoped(
        hidden_stage,
        pltpu.VMEM((cols, own, hid), F32),
        pltpu.VMEM((cols, own, hid), BF16),
        pltpu.VMEM((own, width), BF16),
        pltpu.VMEM((own, width), F32),
    )
    put_attn = Reduce(
        p, links, g.g_attn, g.p_attn, g.q_attn, g.c_attn, g.t_attn, g.r_attn, True
    )
    put_self = Reduce(
        p, links, g.g_self, g.p_self, g.q_self, g.c_self, g.t_self, g.r_self, False
    )
    enc_out = Outbound(p, links, g.enc_low, g.enc_home)
    tok_out = Outbound(p, links, g.tok_low, g.tok_home)
    early = Total(p, links, g.small, g.small_arrived, True)
    late = Total(p, links, g.late, g.late_arrived, False)

    def trade(stage_ref, arrive_ref, pairs):
        here = pl.ds(pairs[0], pairs[1] - pairs[0])
        return Swap(p, links, [(stage_ref.at[:, here], arrive_ref.at[:, here])])

    ckv_trades = [trade(g.stage_cross, g.arrive_cross, pairs) for pairs in ranges]
    kv_trades = [trade(g.stage_self, g.arrive_self, pairs) for pairs in ranges]

    def hand_over(acc_ref, stage_ref, trades, at):
        first = ranges[at][0]
        here = pl.ds(first, half)
        for i in range(2):
            stage_ref[i, here, 0:part, :] = acc_ref[i, here, pl.ds(other_low, part), :].astype(
                BF16
            )
            stage_ref[i, here, part:own, :] = acc_ref[i, here, pl.ds(other_high, part), :].astype(
                BF16
            )
        trades[at].start()

    def joined(acc_ref, arrive_ref, i, z):
        mine_rows = jnp.concatenate(
            [acc_ref[i, z, pl.ds(low_at, part), :], acc_ref[i, z, pl.ds(high_at, part), :]],
            axis=0,
        )
        return (mine_rows + arrive_ref[i, z].astype(F32)).astype(BF16)

    def back_stage(cross_acc, self_acc):
        grad_low = g.grad[...].astype(BF16)
        for z in range(cols):
            g.g_attn[z, :, :, 2 * PAIR : 3 * PAIR] = row_blocks(dot_tn(grad_low, g.cmixed[z]), row_count)
            g.mixed_back[z] = dot_nn(grad_low, attn_w(z, 4)).astype(BF16)
        cross_acc[...] = jnp.zeros_like(cross_acc)

        def cross_block_back(block, pairs):
            attend_block_back(
                g.cq,
                g.ckv,
                g.cmixed,
                g.clse,
                g.mixed_back,
                g.dq,
                cross_acc,
                pl.multiple_of(block * part, part),
                part,
                span,
                own,
                source_mask_back,
                pairs,
            )

        def after_back_1():
            hand_over(cross_acc, g.stage_cross, ckv_trades, 0)

        in_segments(
            cross_block_back,
            ((put_hidden.after_pair, None), (None, after_back_1), (None, None), (None, None)),
        )
        hand_over(cross_acc, g.stage_cross, ckv_trades, 1)
        put_hidden.after_plane(0)
        normed = g.n1[...]
        first_low = (normed * g.attn_gain[...] + g.attn_shift[...]).astype(BF16)
        gradient = g.grad[...]
        for z in range(cols):
            dq = g.dq[z]
            g.g_attn[z, :, :, PAIR : 2 * PAIR] = row_blocks(dot_tn(first_low, dq), row_count)
            g.small[0, 11:12, z * PAIR : (z + 1) * PAIR] = column_sum(dq.astype(F32))
            gradient = gradient + dot_nt(dq, attn_w(z, 1))
        g.small[0, 6:7, :] = column_sum(gradient * normed)
        g.small[0, 7:8, :] = column_sum(gradient)
        first_grad = norm_backward(gradient, normed, g.i1[:, 0:1], g.attn_gain[...])
        g.small[0, 8:9, :] = column_sum(first_grad)
        g.grad[...] = first_grad
        grad_low = first_grad.astype(BF16)
        for z in range(cols):
            g.g_attn[z, :, :, 0:PAIR] = row_blocks(dot_tn(grad_low, g.mixed[z]), row_count)
            g.mixed_back[z] = dot_nn(grad_low, attn_w(z, 0)).astype(BF16)

        early.start()

        for swap in ckv_trades:
            swap.arrive()
        e = g.e[...]
        for z in range(cols):
            dk = joined(cross_acc, g.arrive_cross, 0, z)
            dv = joined(cross_acc, g.arrive_cross, 1, z)
            g.late[0, 2:3, z * PAIR : (z + 1) * PAIR] = column_sum(dv.astype(F32))
            both = jnp.concatenate([dk, dv], axis=1)
            g.g_attn[z, :, :, 3 * PAIR :] = row_blocks(dot_tn(e, both), row_count)
            put_attn.start_column(z)
            term = dot_nt(both, attn_w(z, 2, 2))
            total = term if z == 0 else total + term
        g.enc_low[...] = total.astype(BF16)
        enc_out.start()

        self_acc[...] = jnp.zeros_like(self_acc)

        def self_block_back(block, pairs):
            causal_blocks(
                block,
                lambda row0, keys: attend_block_back(
                    g.q,
                    g.kv,
                    g.mixed,
                    g.lse,
                    g.mixed_back,
                    g.dq,
                    self_acc,
                    row0,
                    part,
                    keys,
                    part,
                    causal_last_back(part, keys),
                    pairs,
                ),
            )


        for level in range(1, len(p.plane_bits)):
            put_hidden.after_plane(level)

        def after_back_0():
            put_attn.after_pair()
            early.step(0)

        def after_back_1():
            hand_over(self_acc, g.stage_self, kv_trades, 0)
            put_hidden.step(1)
            early.step(1)

        def after_back_2():
            put_attn.after_plane(0)
            early.step(2)

        in_segments(
            self_block_back,
            ((None, after_back_0), (None, after_back_1), (None, after_back_2), (None, None)),
        )
        hand_over(self_acc, g.stage_self, kv_trades, 1)
        for level in range(1, len(p.plane_bits)):
            put_attn.after_plane(level)
        put_hidden.step(2)
        for i in range(3, early.steps):
            early.step(i)
        for swap in kv_trades:
            swap.arrive()
        x = g.x[...]
        total = g.grad[...]
        for z in range(cols):
            dq = g.dq[z]
            dk = joined(self_acc, g.arrive_self, 0, z)
            dv = joined(self_acc, g.arrive_self, 1, z)
            g.late[0, 0:1, z * PAIR : (z + 1) * PAIR] = column_sum(dq.astype(F32))
            g.late[0, 1:2, z * PAIR : (z + 1) * PAIR] = column_sum(dv.astype(F32))
            both = jnp.concatenate([dq, dk, dv], axis=1)
            g.g_self[z] = row_blocks(dot_tn(x, both), row_count)
            total = total + dot_nt(both, self_w(z))
        g.tok_low[...] = total.astype(BF16)

        put_attn.step(1)
        late.start()
        put_self.start()
        tok_out.start()
        put_self.after_pair()
        late.step(0)
        late.step(1)
        put_self.after_plane(0)
        for i in range(2, late.steps - 1):
            late.step(i)
        for level in range(1, len(p.plane_bits)):
            put_self.after_plane(level)
        put_attn.step(2)
        put_hidden.finish(2)
        put_attn.finish(2)
        late.step(late.steps - 1)
        g.t_small[...] = early.result()
        g.t_small[9:11, :] = late.result()[0:2, :]
        g.t_small[12:13, :] = late.result()[2:3, :]
        small_out = pltpu.make_async_copy(g.t_small, g.r_small, g.recv.at[small_at])
        small_out.start()
        put_self.finish()
        for moved in (result_out, enc_out, tok_out):
            moved.arrive()
            moved.drain()
        small_out.wait()
        for moved in (x_in, e_in, og_in, get_self, get_attn, get_hidden, len_swap, early, late):
            moved.drain()
        for moved in kv_swaps + ckv_swaps + ckv_trades + kv_trades:
            moved.drain()
        for moved in (put_hidden, put_attn, put_self):
            moved.drain()
        assert links.count <= g.send.shape[0]

    small_at = links.take()
    g.small[0, 9:11, :] = jnp.zeros((2, width), F32)
    g.small[0, 12:13, :] = jnp.zeros((1, width), F32)
    g.late[0] = jnp.zeros(g.late.shape[1:], F32)
    count = g.small.shape[1]
    g.small[0, 13 + cols : count, :] = jnp.zeros((count - 13 - cols, width), F32)
    pl.run_scoped(
        back_stage,
        pltpu.VMEM((2, cols, span, PAIR), F32),
        pltpu.VMEM((2, cols, span, PAIR), F32),
    )


def finish_kernel(width, names, out_names, *refs):
    g = named(names, refs[: len(names)])
    homes, o = refs[len(names) : len(names) + 3], named(out_names, refs[len(names) + 3 :])
    for home, source in zip(homes, (g.result_home, g.tok_home, g.enc_home)):
        home[...] = source[...].astype(F32)
    hid = o.expand.shape[1]

    def block(ref, at):
        return ref[:, at * PAIR : (at + 1) * PAIR]

    o.self_query[...] = block(g.r_self, 0)
    o.self_key[...] = block(g.r_self, 1)
    o.self_value[...] = block(g.r_self, 2)
    o.self_output[...] = block(g.r_attn, 0)
    o.cross_query[...] = block(g.r_attn, 1)
    o.cross_output[...] = block(g.r_attn, 2)
    o.cross_key[...] = block(g.r_attn, 3)
    o.cross_value[...] = block(g.r_attn, 4)
    o.expand[...] = g.r_hidden[:, :hid]
    o.contract[...] = g.r_hidden[:, hid:]
    vectors = (
        o.final_gain,
        o.final_shift,
        o.contract_bias,
        o.cross_gain,
        o.cross_shift,
        o.cross_output_bias,
        o.attn_gain,
        o.attn_shift,
        o.self_output_bias,
        o.self_query_bias,
        o.self_value_bias,
        o.cross_query_bias,
        o.cross_value_bias,
    )
    for i, vector in enumerate(vectors):
        vector[...] = g.r_small[i : i + 1, :]
    at = len(vectors)
    for z in range(o.expand_bias.shape[1] // width):
        o.expand_bias[:, z * width : (z + 1) * width] = g.r_small[at + z : at + z + 1, :]


def per_device(
    tokens,
    encoded,
    source_len,
    out_grad,
    self_query,
    self_key,
    self_value,
    self_output,
    self_query_bias,
    self_value_bias,
    self_output_bias,
    cross_query,
    cross_key,
    cross_value,
    cross_output,
    cross_query_bias,
    cross_value_bias,
    cross_output_bias,
    expand,
    expand_bias,
    contract,
    contract_bias,
    attn_gain,
    attn_shift,
    cross_gain,
    cross_shift,
    final_gain,
    final_shift,
):
    inputs = dict(locals())
    names = tuple(inputs)
    turned = [v is source_len or v is self_output or v is cross_output or v is contract
              for v in inputs.values()]
    flat = [v.ndim == 1 for v in inputs.values()]
    row_count = lax.axis_size(ROW)
    cols = lax.axis_size(COL)
    micro_count, part, width = tokens.shape
    depth, head_width = self_query.shape
    hid = expand.shape[1]
    assert micro_count == 2 and cols == 4 and source_len.shape[1] == 1
    assert head_width == PAIR and row_count % 4 == 0 and hid == width
    own = 2 * part
    plane = row_count // 2
    small_rows = -(-(13 + cols) // 8) * 8
    row_steps = len(bits_of(row_count - 1))
    small_steps = row_steps + cols - 1
    links = 3 * (2 * (cols - 1) + (plane - 1) * cols + plane)
    links += 3 * (plane + 2 * (plane - 1) + 2 * (cols - 1) + 1) + 2 * plane * (cols - 1)
    links += 6 * 2 + 1 + 8 + 4 + 2 * small_steps + 1

    def whole(columns):
        return pltpu.VMEM((cols, row_count, depth, columns), BF16)

    def from_pair(columns):
        return pltpu.VMEM((plane, cols, depth, columns), BF16)

    def from_plane(columns):
        return pltpu.VMEM((2 * (plane - 1), cols // 2, depth, columns), BF16)

    def from_col(columns):
        return pltpu.VMEM((2 * (cols - 1), depth, columns), BF16)

    rows_low = pltpu.VMEM((own, width), BF16)
    rows_f32 = pltpu.VMEM((own, width), F32)
    stat_f32 = pltpu.VMEM((own, PAIR), F32)
    heads_low = pltpu.VMEM((cols, own, PAIR), BF16)
    heads_f32 = pltpu.VMEM((cols, own, PAIR), F32)
    keys_low = pltpu.VMEM((2, cols, 2 * own, PAIR), BF16)
    half_keys = pltpu.VMEM((2, cols, own, PAIR), BF16)
    lengths = pltpu.VMEM((2, 8, PAIR), jnp.int32)
    scratch = dict(
        x=rows_low,
        e=rows_low,
        og=rows_low,
        og_low=pltpu.VMEM((2, part, width), BF16),
        pack_self=pltpu.VMEM((depth, 3 * PAIR), BF16),
        pack_attn=pltpu.VMEM((depth, 5 * PAIR), BF16),
        pack_hidden=pltpu.VMEM((depth, 2 * hid), BF16),
        w_self=whole(3 * PAIR),
        w_attn=whole(5 * PAIR),
        w_hidden=whole(2 * hid),
        len_own=lengths,
        len_other=lengths,
        q=heads_low,
        kv=keys_low,
        ckv=keys_low,
        mixed=heads_low,
        lse=heads_f32,
        n1=rows_f32,
        i1=stat_f32,
        cq=heads_low,
        cmixed=heads_low,
        clse=heads_f32,
        n2=rows_f32,
        i2=stat_f32,
        grad=rows_f32,
        mixed_back=heads_low,
        dq=heads_low,
        result_low=rows_low,
        enc_low=rows_low,
        tok_low=rows_low,
        stage_cross=half_keys,
        arrive_cross=half_keys,
        stage_self=half_keys,
        arrive_self=half_keys,
        small=pltpu.VMEM((row_steps + 2, small_rows, width), F32),
        small_arrived=pltpu.VMEM((small_steps, small_rows, width), F32),
        late=pltpu.VMEM((row_steps + 2, 8, width), F32),
        late_arrived=pltpu.VMEM((small_steps, 8, width), F32),
        t_hidden=pltpu.VMEM((depth, 2 * hid), F32),
        t_attn=pltpu.VMEM((depth, 5 * PAIR), F32),
        t_self=pltpu.VMEM((depth, 3 * PAIR), F32),
        t_small=pltpu.VMEM((small_rows, width), F32),
        g_hidden=whole(2 * hid),
        p_hidden=from_pair(2 * hid),
        q_hidden=from_plane(2 * hid),
        c_hidden=from_col(2 * hid),
        g_attn=whole(5 * PAIR),
        p_attn=from_pair(5 * PAIR),
        q_attn=from_plane(5 * PAIR),
        c_attn=from_col(5 * PAIR),
        g_self=whole(3 * PAIR),
        p_self=from_pair(3 * PAIR),
        q_self=from_plane(3 * PAIR),
        c_self=from_col(3 * PAIR),
        send=pltpu.SemaphoreType.DMA((links,)),
        recv=pltpu.SemaphoreType.DMA((links,)),
    )
    home = jax.ShapeDtypeStruct((2, part, width), BF16)
    outs = dict(
        result_home=(home, ANY_SPEC),
        tok_home=(home, ANY_SPEC),
        enc_home=(home, ANY_SPEC),
        r_self=(jax.ShapeDtypeStruct((depth, 3 * PAIR), F32), ANY_SPEC),
        r_attn=(jax.ShapeDtypeStruct((depth, 5 * PAIR), F32), ANY_SPEC),
        r_hidden=(jax.ShapeDtypeStruct((depth, 2 * hid), F32), ANY_SPEC),
        r_small=(jax.ShapeDtypeStruct((small_rows, width), F32), ANY_SPEC),
    )
    specs = [ANY_SPEC, ANY_SPEC, SMEM_SPEC] + [VMEM_SPEC] * (len(names) - 3)
    values = [
        v.reshape(1, -1) if f else (v.T if t else v)
        for v, f, t in zip(inputs.values(), flat, turned)
    ]
    moved = pl.pallas_call(
        functools.partial(layer_kernel, row_count, cols, names + tuple(outs) + tuple(scratch)),
        out_shape=[shape for shape, _ in outs.values()],
        in_specs=specs,
        out_specs=[spec for _, spec in outs.values()],
        scratch_shapes=list(scratch.values()),
        compiler_params=pltpu.CompilerParams(
            collective_id=0, has_side_effects=True, vmem_limit_bytes=VMEM_LIMIT
        ),
        name="layer",
    )(*values)
    shapes = [(2, part, width)] * 3 + [v.shape for v in values[4:]]
    final = pl.pallas_call(
        functools.partial(finish_kernel, width, tuple(outs), names[4:]),
        out_shape=[jax.ShapeDtypeStruct(shape, F32) for shape in shapes],
        in_specs=[VMEM_SPEC] * len(outs),
        out_specs=[VMEM_SPEC] * len(shapes),
        compiler_params=pltpu.CompilerParams(vmem_limit_bytes=VMEM_LIMIT),
        name="finish",
    )(*moved)
    return tuple(final[:3]) + tuple(
        v.reshape(-1) if f else (v.T if t else v)
        for v, f, t in zip(final[3:], flat[4:], turned[4:])
    )


def solution(mesh):
    tokens, down, across, same = P(None, AXES, None), P(ROW, COL), P(COL, ROW), P()
    attention = (down, down, down, across, same, same, same)
    weights = attention * 2 + (down, same, across) + (same,) * 7
    return jax.shard_map(
        per_device,
        mesh=mesh,
        in_specs=(tokens, tokens, P(None, ROW), tokens) + weights,
        out_specs=(tokens, tokens, tokens) + weights,
        check_vma=False,
    )
```
